32 devices in a mesh: enc: 2 (over x), batch: 16 (over z, y, core).
Axes of the slice: x: 2, y: 2, z: 4, core: 2. Of those that a mesh axis runs over, the one named last changes fastest.
Arguments:
- tokens: bfloat16 [2, 16384, 768], P('enc', 'batch'), may hold values from -6 to 6
- cotangent: bfloat16 [2, 16384, 768], P('enc', 'batch'), may hold values from -6 to 6
- projection: bfloat16 [2, 768, 2304], P('enc'), may hold values from -0.21875 to 0.21875
- offsets: bfloat16 [2, 1536], P('enc'), may hold values from -1.1953125 to 1.1953125
- merger: bfloat16 [2, 768, 768], P('enc'), may hold values from -1.75 to 1.75
- adjust: bfloat16 [2, 768], P('enc'), may hold values from -1.1953125 to 1.1953125
- scaling: bfloat16 [2, 768], P('enc'), may hold values from 0.5 to 1.5
- centering: bfloat16 [2, 768], P('enc'), may hold values from -1.1953125 to 1.1953125
- expansion: bfloat16 [2, 768, 3072], P('enc'), may hold values from -0.21875 to 0.21875
- lifting: bfloat16 [2, 3072], P('enc'), may hold values from -1.1953125 to 1.1953125
- contraction: bfloat16 [2, 3072, 768], P('enc'), may hold values from -0.15625 to 0.15625
- settling: bfloat16 [2, 768], P('enc'), may hold values from -1.1953125 to 1.1953125
- rescale: bfloat16 [2, 768], P('enc'), may hold values from 0.5 to 1.5
- recenter: bfloat16 [2, 768], P('enc'), may hold values from -1.1953125 to 1.1953125
- segments: int32 [16384], P('batch'), may hold values from 0 to 15, as said below
- passage_starts: int32 [256], P('batch'), may hold values from 0 to 1023, as said below
- passage_counts: int32 [16], replicated, may hold values from 4 to 16, as said below
- positives: int32 [256], P('batch'), may hold values from 0 to 255, as said below
Outputs:
- encoded: bfloat16 [2, 16384, 768], P('enc', 'batch')
- tokens_gradient: float32 [2, 16384, 768], P('enc', 'batch')
- gradient_projection: float32 [2, 768, 2304], P('enc')
- gradient_offsets: float32 [2, 1536], P('enc')
- gradient_merger: float32 [2, 768, 768], P('enc')
- gradient_adjust: float32 [2, 768], P('enc')
- gradient_scaling: float32 [2, 768], P('enc')
- gradient_centering: float32 [2, 768], P('enc')
- gradient_expansion: float32 [2, 768, 3072], P('enc')
- gradient_lifting: float32 [2, 3072], P('enc')
- gradient_contraction: float32 [2, 3072, 768], P('enc')
- gradient_settling: float32 [2, 768], P('enc')
- gradient_rescale: float32 [2, 768], P('enc')
- gradient_recenter: float32 [2, 768], P('enc')
The draws below stay inside these ranges and needn't reach their ends.
Inputs may be any that keep to these rules, and one draw needn't show every extreme that they name: `segments`: within one index of batch, passages are runs of consecutive tokens numbered from 0 upward in order; every row of 256 tokens starts a passage and holds 1 to 4 of them; passages start at multiples of 8. `passage_starts`: on each index of batch, slot s below that index's passage count holds the position of passage s's first token; other slots hold arbitrary positions. `passage_counts`: the number of passages on each index of batch; some index holds 16 in every draw. `positives`: A slot i * 16 + s with s below the passage count of index i.
All inputs are finite; a program needn't handle non-finite values.
Results may differ from the reference program's by a relative error of at most 0.014.
Values may be sent and summed in bfloat16 or wider, within the bound.
No kernel may reach another device: no remote copies, remote signals or barrier semaphores. Data moves between devices by JAX's collectives and lax.ppermute only.
A program may use at most 192 MiB of HBM per device.

```python
import math
import jax
import jax.numpy as jnp
from jax import lax

HIDDEN_SPAN = 768
HEADS = 12
HD = 64
FF = 3072
TOK_DEV = 1024
PLEN = 256
QLEN = 64
SEGS_ROW = 4
BLOCK = 512
CAP = 16
SLOTS = 256
NQ = 256
TOKENS = 16384
N_ENC = 2


def layout_draw(key):
    devices = SLOTS // CAP
    row_dev = TOK_DEV // PLEN
    row_total = devices * row_dev
    grain = PLEN // 32
    per_row = jax.random.randint(jax.random.fold_in(key, 11), (devices, row_dev), 1, SEGS_ROW + 1)
    full_device = jax.random.randint(jax.random.fold_in(key, 12), (), 0, devices)
    per_row = jnp.where(jnp.arange(devices, dtype=jnp.int32)[:, None] == full_device, SEGS_ROW, per_row).reshape(row_total)
    priority = jax.random.randint(jax.random.fold_in(key, 13), (row_total, 31), 0, 1 << 20) * 32 + jnp.arange(31, dtype=jnp.int32)[None, :]
    ordered = jnp.sort(priority, axis=1)
    padded_order = jnp.concatenate([ordered, jnp.full((row_total, 1), 1 << 30, jnp.int32)], axis=1)
    limit = jnp.take_along_axis(padded_order, (per_row - 1)[:, None], axis=1)
    chosen = (priority < limit).astype(jnp.int32)
    begins = jnp.zeros((row_total, PLEN), jnp.int32)
    begins = begins.at[:, 0].set(1)
    begins = begins.at[:, grain * jnp.arange(1, 32, dtype=jnp.int32)].set(chosen)
    begins = begins.reshape(devices, TOK_DEV)
    segment_marks = jnp.cumsum(begins, axis=1) - 1
    counts = jnp.sum(begins, axis=1).astype(jnp.int32)
    token_index = jnp.arange(TOK_DEV, dtype=jnp.int32)
    slot_index = jnp.arange(CAP, dtype=jnp.int32)
    matched = (segment_marks[:, None, :] == slot_index[None, :, None]) & (begins[:, None, :] == 1)
    starts = jnp.sum(jnp.where(matched, token_index[None, None, :], 0), axis=2).astype(jnp.int32)
    filler = jax.random.randint(jax.random.fold_in(key, 14), (devices, CAP), 0, TOK_DEV)
    starts = jnp.where(slot_index[None, :] < counts[:, None], starts, filler)
    return (segment_marks.reshape(-1).astype(jnp.int32), starts.reshape(-1).astype(jnp.int32), counts)


def draw_segments(key, part):
    return layout_draw(key)[0]


def draw_passage_starts(key, part):
    return layout_draw(key)[1]


def draw_passage_counts(key, part):
    return layout_draw(key)[2]


def draw_positives(key, part):
    counts = layout_draw(key)[2]
    devices = SLOTS // CAP
    owner = jax.random.randint(jax.random.fold_in(key, 21), (NQ,), 0, devices)
    raw_pick = jax.random.randint(jax.random.fold_in(key, 22), (NQ,), 0, 1 << 20)
    return (owner * CAP + raw_pick % counts[owner]).astype(jnp.int32)


def level_of(key, extent, cuts, smallest, high):
    gain, own = 1.0, jax.random.fold_in(key, 6)
    for position, parts in cuts:
        heights = jnp.exp(jax.random.uniform(jax.random.fold_in(own, position), (parts,), jnp.float32, smallest / len(cuts), high / len(cuts)))
        gain = gain * jnp.repeat(heights, extent[position] // parts).reshape([-1 if axis == position else 1 for axis in range(len(extent))])
    return gain


def gaussian(rng, extent, width, most, split=(), kind=jnp.bfloat16):
    drawn = width * jax.random.normal(rng, extent, jnp.float32)
    if split:
        drawn = drawn * level_of(rng, extent, split, -0.22, 0.18)
    return jnp.clip(drawn, -most, most).astype(kind)


def setup_inputs(seed: int = 0) -> dict:
    seeds = jax.random.split(jax.random.key(seed), 19)
    tokens = gaussian(seeds[0], (N_ENC, TOKENS, HIDDEN_SPAN), 1.0, 6.0, ((0, 2), (1, 16)))
    cotangent = gaussian(seeds[1], (N_ENC, TOKENS, HIDDEN_SPAN), 1.0, 6.0, ((0, 2), (1, 16)))
    projection = gaussian(seeds[2], (N_ENC, HIDDEN_SPAN, 3 * HIDDEN_SPAN), HIDDEN_SPAN ** -0.5, 0.21875, ((0, 2),))
    offsets = gaussian(seeds[3], (N_ENC, 2 * HIDDEN_SPAN), 0.2, 1.1953125, ((0, 2),))
    merger = gaussian(seeds[4], (N_ENC, HIDDEN_SPAN, HIDDEN_SPAN), (HIDDEN_SPAN // 64) ** -0.5, 1.75, ((0, 2),))
    adjust = gaussian(seeds[5], (N_ENC, HIDDEN_SPAN), 0.2, 1.1953125, ((0, 2),))
    scaling = jnp.clip(1.0 + 0.1 * jax.random.normal(seeds[6], (N_ENC, HIDDEN_SPAN), jnp.float32), 0.5, 1.5).astype(jnp.bfloat16)
    centering = gaussian(seeds[7], (N_ENC, HIDDEN_SPAN), 0.2, 1.1953125, ((0, 2),))
    expansion = gaussian(seeds[8], (N_ENC, HIDDEN_SPAN, FF), HIDDEN_SPAN ** -0.5, 0.21875, ((0, 2),))
    lifting = gaussian(seeds[9], (N_ENC, FF), 0.2, 1.1953125, ((0, 2),))
    contraction = gaussian(seeds[10], (N_ENC, FF, HIDDEN_SPAN), (FF // 2) ** -0.5, 0.15625, ((0, 2),))
    settling = gaussian(seeds[11], (N_ENC, HIDDEN_SPAN), 0.2, 1.1953125, ((0, 2),))
    rescale = jnp.clip(1.0 + 0.1 * jax.random.normal(seeds[12], (N_ENC, HIDDEN_SPAN), jnp.float32), 0.5, 1.5).astype(jnp.bfloat16)
    recenter = gaussian(seeds[13], (N_ENC, HIDDEN_SPAN), 0.2, 1.1953125, ((0, 2),))
    segments = draw_segments(jax.random.fold_in(seeds[18], 71), 0)
    passage_starts = draw_passage_starts(jax.random.fold_in(seeds[18], 71), 0)
    passage_counts = draw_passage_counts(jax.random.fold_in(seeds[18], 71), 0)
    positives = draw_positives(jax.random.fold_in(seeds[18], 71), 0)
    return dict(tokens=tokens, cotangent=cotangent, projection=projection, offsets=offsets, merger=merger, adjust=adjust, scaling=scaling, centering=centering, expansion=expansion, lifting=lifting, contraction=contraction, settling=settling, rescale=rescale, recenter=recenter, segments=segments, passage_starts=passage_starts, passage_counts=passage_counts, positives=positives)


EPSILON = 1e-12
SHARPNESS_DIVISOR = 2.0
LOSS_WEIGHT = 2.0

@jax.custom_vjp
def low(v):
    return lax.optimization_barrier(v.astype(jnp.bfloat16)).astype(jnp.float32)

@jax.custom_vjp
def reduced_backward(v):
    return v

def low_keep(v):
    return (low(v), None)

def low_pass(kept, grad):
    return (grad,)

def back_keep(v):
    return (v, None)

def back_low(kept, grad):
    return (low(grad),)
low.defvjp(low_keep, low_pass)
reduced_backward.defvjp(back_keep, back_low)

def highest_precision(left, right):
    return jnp.dot(left, right, precision=lax.Precision.HIGHEST)

def layer_norm(values, scale_row, shift_row):
    centered = values - lax.optimization_barrier(jnp.mean(values, axis=-1, keepdims=True))
    spread = lax.optimization_barrier(jnp.mean(centered * centered, axis=-1, keepdims=True))
    return centered * lax.rsqrt(spread + EPSILON) * scale_row + shift_row

def encode_block(params, block_rows, block_marks):
    projection, offsets, merger, adjust, scaling, centering, expansion, lifting, contraction, settling, rescale, recenter = params
    row_count = block_rows.shape[0]
    full_bias = jnp.concatenate([offsets[:HIDDEN_SPAN], jnp.zeros((HIDDEN_SPAN,), block_rows.dtype), offsets[HIDDEN_SPAN:]])
    packed = low(reduced_backward(highest_precision(block_rows, projection) + full_bias))
    parted = packed.reshape(row_count, 3, HEADS, HD)
    scores = jnp.einsum('qhd,khd->hqk', parted[:, 0], parted[:, 1], precision=lax.Precision.HIGHEST) * (1.0 / math.sqrt(HD))
    scores = reduced_backward(scores)
    same_mark = block_marks[:, None] == block_marks[None, :]
    scores = jnp.where(same_mark[None], scores, -1e+30)
    probability = jax.nn.softmax(scores, axis=-1)
    context = jnp.einsum('hqk,khd->qhd', low(probability), parted[:, 2], precision=lax.Precision.HIGHEST)
    context = low(reduced_backward(context.reshape(row_count, HIDDEN_SPAN)))
    attended = reduced_backward(highest_precision(context, merger) + adjust)
    normed_one = layer_norm(block_rows + attended, scaling, centering)
    hidden = reduced_backward(highest_precision(low(normed_one), expansion) + lifting)
    activated = low(jax.nn.gelu(hidden, approximate=False))
    shrunk = reduced_backward(highest_precision(activated, contraction) + settling)
    return layer_norm(normed_one + shrunk, rescale, recenter)

def encode(params, rows_in, marks):
    block_count = rows_in.shape[0] // BLOCK
    stepper = jax.checkpoint(lambda paired: encode_block(params, paired[0], paired[1]))
    encoded = lax.map(stepper, (rows_in.reshape(block_count, BLOCK, HIDDEN_SPAN), marks.reshape(block_count, BLOCK)))
    return encoded.reshape(block_count * BLOCK, HIDDEN_SPAN)

def stacked(question_part, passage_part):
    return jnp.stack([question_part, passage_part]).astype(jnp.float32)

def reference(tokens, cotangent, projection, offsets, merger, adjust, scaling, centering, expansion, lifting, contraction, settling, rescale, recenter, segments, passage_starts, passage_counts, positives):
    weight_list = (projection, offsets, merger, adjust, scaling, centering, expansion, lifting, contraction, settling, rescale, recenter)
    question_marks = jnp.arange(TOKENS, dtype=jnp.int32) // QLEN
    slot_index = jnp.arange(SLOTS, dtype=jnp.int32)
    valid_entries = slot_index % CAP < passage_counts[slot_index // CAP]
    passage_rows_at = slot_index // CAP * TOK_DEV + passage_starts
    question_rows_at = jnp.arange(NQ, dtype=jnp.int32) * QLEN
    cot_float = cotangent.astype(jnp.float32)
    smoothing_divisor = SHARPNESS_DIVISOR / math.sqrt(HIDDEN_SPAN)

    def objective(question_params, passage_params, question_tokens, passage_tokens):
        question_out = encode(question_params, question_tokens, question_marks)
        passage_out = encode(passage_params, passage_tokens, segments)
        question_embedding = low(jnp.take(question_out, question_rows_at, axis=0))
        passage_embedding = low(jnp.take(passage_out, passage_rows_at, axis=0))
        score_matrix = reduced_backward(highest_precision(question_embedding, passage_embedding.T) * smoothing_divisor)
        score_matrix = jnp.where(valid_entries[None, :], score_matrix, -1e+30)
        picked = jnp.take_along_axis(score_matrix, positives[:, None], axis=1)[:, 0]
        loss_total = jnp.sum(jax.nn.logsumexp(score_matrix, axis=1) - picked)
        total = jnp.sum(cot_float[0] * question_out) + jnp.sum(cot_float[1] * passage_out) + LOSS_WEIGHT * loss_total
        return (total, (question_out, passage_out))
    question_params = tuple((weight[0].astype(jnp.float32) for weight in weight_list))
    passage_params = tuple((weight[1].astype(jnp.float32) for weight in weight_list))
    total, backward, outputs = jax.vjp(objective, question_params, passage_params, tokens[0].astype(jnp.float32), tokens[1].astype(jnp.float32), has_aux=True)
    query_sensitivities, passage_grads, question_tokens_grad, passage_tokens_grad = backward(jnp.ones_like(total))
    layer_out = jnp.stack([outputs[0], outputs[1]]).astype(jnp.bfloat16)
    tokens_gradient = stacked(question_tokens_grad, passage_tokens_grad)
    merged = [stacked(query_sensitivities[index], passage_grads[index]) for index in range(12)]
    return (layer_out, tokens_gradient, merged[0], merged[1], merged[2], merged[3], merged[4], merged[5], merged[6], merged[7], merged[8], merged[9], merged[10], merged[11])
```

```python
import math

import jax
import jax.numpy as jnp
from jax import lax
from jax.sharding import PartitionSpec as P

HEADS = 12
QLEN = 64
BLOCK = 512


EPSILON = 1e-12
SHARPNESS_DIVISOR = 2.0
LOSS_WEIGHT = 2.0
FLOAT_KIND = jnp.float32
BRAIN = jnp.bfloat16


def swapped(value, axis, apart):
    mask = 2**apart
    pairs = [(source, source ^ mask) for source in range(lax.axis_size(axis))]
    return lax.ppermute(value, axis, pairs)


def layer_norm(values, scale_row, shift_row):
    centered = values - jnp.mean(values, axis=-1, keepdims=True)
    spread = jnp.mean(centered * centered, axis=-1, keepdims=True)
    return centered * lax.rsqrt(spread + EPSILON) * scale_row + shift_row


def exact_gelu(values):
    return jax.nn.gelu(values, approximate=False)


def to_low(values):
    return values.astype(BRAIN)


def block_scores(queries, key_rows, block_marks):
    score_scale = 1.0 / math.sqrt(queries.shape[2])
    scores = (
        jnp.einsum("qhd,khd->hqk", queries, key_rows, preferred_element_type=FLOAT_KIND)
        * score_scale
    )
    same_mark = block_marks[:, None] == block_marks[None, :]
    return jnp.where(same_mark[None], scores, -1e30)


def attend_forward(parts):
    queries, key_rows, values, block_marks = parts
    scores = block_scores(queries, key_rows, block_marks)
    row_top = jnp.max(scores, axis=-1, keepdims=True)
    log_total = row_top + jnp.log(jnp.sum(jnp.exp(scores - row_top), axis=-1, keepdims=True))
    weights = to_low(jnp.exp(scores - log_total))
    context = jnp.einsum("hqk,khd->qhd", weights, values, preferred_element_type=FLOAT_KIND)
    return (to_low(context), log_total)


def attend_backward(parts):
    queries, key_rows, values, block_marks, log_total, gradient_context = parts
    score_scale = 1.0 / math.sqrt(queries.shape[2])
    probability = jnp.exp(block_scores(queries, key_rows, block_marks) - log_total)
    gradient_values = jnp.einsum(
        "hqk,qhd->khd", to_low(probability), gradient_context, preferred_element_type=FLOAT_KIND
    )
    gradient_probs = jnp.einsum(
        "qhd,khd->hqk", gradient_context, values, preferred_element_type=FLOAT_KIND
    )
    row_dots = jnp.sum(probability * gradient_probs, axis=-1, keepdims=True)
    gradient_scores = to_low(probability * (gradient_probs - row_dots))
    gradient_queries = (
        jnp.einsum("hqk,khd->qhd", gradient_scores, key_rows, preferred_element_type=FLOAT_KIND)
        * score_scale
    )
    gradient_keys = (
        jnp.einsum("hqk,qhd->khd", gradient_scores, queries, preferred_element_type=FLOAT_KIND)
        * score_scale
    )
    return (gradient_queries, gradient_keys, gradient_values)


def column_sums(values):
    return jnp.sum(values.astype(FLOAT_KIND), axis=0)


def logit_gradients(
    question_row_block, target_row_list, passage_row_block, valid_entries, smoothing_divisor
):
    score_matrix = (
        jnp.einsum(
            "qd,sd->qs", question_row_block, passage_row_block, preferred_element_type=FLOAT_KIND
        )
        * smoothing_divisor
    )
    score_matrix = jnp.where(valid_entries[None, :], score_matrix, -1e30)
    row_top = jnp.max(score_matrix, axis=1, keepdims=True)
    logit_total = row_top + jnp.log(jnp.sum(jnp.exp(score_matrix - row_top), axis=1, keepdims=True))
    probability = jnp.exp(score_matrix - logit_total)
    target_hit = (
        jnp.arange(score_matrix.shape[1], dtype=jnp.int32)[None, :] == target_row_list[:, None]
    )
    return to_low(LOSS_WEIGHT * (probability - target_hit.astype(FLOAT_KIND)))


def bit_count(axis):
    return lax.axis_size(axis).bit_length() - 1


def split_by_bit(value, bit):
    half = value.shape[0] // 2
    keep = lax.dynamic_slice_in_dim(value, bit * half, half, 0)
    send = lax.dynamic_slice_in_dim(value, (1 - bit) * half, half, 0)
    return keep, send


def joined_by_bit(mine, other, bit):
    low_part = jnp.where(bit == 0, mine, other)
    high_part = jnp.where(bit == 0, other, mine)
    return jnp.concatenate([low_part, high_part], axis=0)


def scatter_sum(value, axis):
    index = lax.axis_index(axis)
    for apart in range(bit_count(axis)):
        keep, send = split_by_bit(value, (index >> apart) & 1)
        arrived = swapped(send, axis, apart)
        value = to_low(keep.astype(FLOAT_KIND) + arrived.astype(FLOAT_KIND))
    return value


def gather_all(value, axis):
    index = lax.axis_index(axis)
    for apart in reversed(range(bit_count(axis))):
        value = joined_by_bit(value, swapped(value, axis, apart), (index >> apart) & 1)
    return value


def total_sum(value, axis):
    for apart in range(bit_count(axis)):
        value = value + swapped(value, axis, apart)
    return value


def weight_total(value):
    return gather_all(scatter_sum(to_low(value), "batch"), "batch").astype(FLOAT_KIND)


def shards(
    tokens,
    cotangent,
    projection,
    offsets,
    merger,
    adjust,
    scaling,
    centering,
    expansion,
    lifting,
    contraction,
    settling,
    rescale,
    recenter,
    segments,
    passage_starts,
    passage_counts,
    positives,
):
    enc_index = lax.axis_index("enc")
    is_passage = enc_index == 1
    rows_in = tokens[0]
    row_count, feature_breadth = rows_in.shape
    head_count = HEADS
    head_size = feature_breadth // head_count
    block_count = row_count // BLOCK
    focus_weighting_array = projection[0]
    merge_matrix = merger[0]
    expand_matrix = expansion[0]
    shrink_matrix = contraction[0]
    offset_row = offsets[0].astype(FLOAT_KIND)
    adjust_row = adjust[0].astype(FLOAT_KIND)
    scaling_row = scaling[0].astype(FLOAT_KIND)
    centering_row = centering[0].astype(FLOAT_KIND)
    lifting_row = lifting[0].astype(FLOAT_KIND)
    settling_row = settling[0].astype(FLOAT_KIND)
    rescale_row = rescale[0].astype(FLOAT_KIND)
    recenter_row = recenter[0].astype(FLOAT_KIND)
    position = jnp.arange(row_count, dtype=jnp.int32)
    token_marks = jnp.where(is_passage, segments, position // QLEN)
    block_marks = token_marks.reshape(block_count, BLOCK)
    full_bias = jnp.concatenate(
        [
            offset_row[:feature_breadth],
            jnp.zeros((feature_breadth,), FLOAT_KIND),
            offset_row[feature_breadth:],
        ]
    )
    packed = to_low(
        jnp.dot(rows_in, focus_weighting_array, preferred_element_type=FLOAT_KIND) + full_bias
    )
    parted = packed.reshape(block_count, BLOCK, 3, head_count, head_size)
    queries = parted[:, :, 0]
    key_rows = parted[:, :, 1]
    values = parted[:, :, 2]
    context, log_total = lax.map(attend_forward, (queries, key_rows, values, block_marks))
    context = context.reshape(row_count, feature_breadth)
    attended = jnp.dot(context, merge_matrix, preferred_element_type=FLOAT_KIND) + adjust_row
    normed_one, first_back = jax.vjp(
        layer_norm, rows_in.astype(FLOAT_KIND) + attended, scaling_row, centering_row
    )
    first_low = to_low(normed_one)
    hidden = jnp.dot(first_low, expand_matrix, preferred_element_type=FLOAT_KIND) + lifting_row
    activated = to_low(exact_gelu(hidden))
    shrunk = jnp.dot(activated, shrink_matrix, preferred_element_type=FLOAT_KIND) + settling_row
    encoded, second_back = jax.vjp(layer_norm, normed_one + shrunk, rescale_row, recenter_row)
    encoded_low = to_low(encoded)
    slot_count = passage_starts.shape[0]
    slot_index = jnp.arange(slot_count, dtype=jnp.int32)
    summary_rows = jnp.where(is_passage, passage_starts, slot_index * QLEN)
    picker = summary_rows[:, None] == position[None, :]
    summary_local = to_low(
        jnp.dot(picker.astype(BRAIN), encoded_low, preferred_element_type=FLOAT_KIND)
    )
    smoothing_divisor = SHARPNESS_DIVISOR / math.sqrt(feature_breadth)
    lane = jnp.arange(128, dtype=jnp.int32)[None, :]
    target_column = positives[:, None]
    digits = jnp.where(lane == 0, target_column // 128, jnp.where(lane == 1, target_column % 128, 0))
    parcel = jnp.concatenate([summary_local, digits.astype(BRAIN)], axis=1)
    both = joined_by_bit(parcel[None], swapped(parcel, "enc", 0)[None], enc_index)
    index = lax.axis_index("batch")
    for apart in range(bit_count("batch")):
        mine_bit = (index >> apart) & 1
        other = swapped(both, "batch", apart)
        both = jnp.concatenate(
            [jnp.where(mine_bit == 0, both, other), jnp.where(mine_bit == 0, other, both)], axis=1
        )
    question_all = both[0, :, :feature_breadth]
    passage_all = both[1, :, :feature_breadth]
    digits_all = both[0, :, feature_breadth : feature_breadth + 2].astype(jnp.int32)
    target_all = digits_all[:, 0] * 128 + digits_all[:, 1]
    valid_entries = (slot_index[None, :] < passage_counts[:, None]).reshape(-1)
    logits_gradient = logit_gradients(
        question_all, target_all, passage_all, valid_entries, smoothing_divisor
    )
    own_rows = jnp.where(
        is_passage,
        lax.dynamic_slice_in_dim(logits_gradient, index * slot_count, slot_count, 1).T,
        lax.dynamic_slice_in_dim(logits_gradient, index * slot_count, slot_count, 0),
    )
    gradient_summary = (
        jnp.dot(
            own_rows,
            jnp.where(is_passage, question_all, passage_all),
            preferred_element_type=FLOAT_KIND,
        )
        * smoothing_divisor
    )
    gradient_encoded = cotangent[0].astype(FLOAT_KIND) + jnp.einsum(
        "ct,cd->td", picker.astype(FLOAT_KIND), gradient_summary, precision=lax.Precision.HIGHEST
    )
    gradient_two, gradient_rescale, gradient_recenter = second_back(gradient_encoded)
    gradient_shrunk = to_low(gradient_two)
    gradient_settling = column_sums(gradient_shrunk)
    gradient_contraction = jnp.einsum(
        "tf,td->fd", activated, gradient_shrunk, preferred_element_type=FLOAT_KIND
    )
    gradient_activated = jnp.einsum(
        "td,fd->tf", gradient_shrunk, shrink_matrix, preferred_element_type=FLOAT_KIND
    )
    gelu_again, gelu_back = jax.vjp(exact_gelu, hidden)
    gradient_hidden = to_low(gelu_back(gradient_activated)[0])
    gradient_lifting = column_sums(gradient_hidden)
    gradient_expansion = jnp.einsum(
        "td,tf->df", first_low, gradient_hidden, preferred_element_type=FLOAT_KIND
    )
    gradient_first = gradient_two + jnp.einsum(
        "tf,df->td", gradient_hidden, expand_matrix, preferred_element_type=FLOAT_KIND
    )
    gradient_one, gradient_scaling, gradient_centering = first_back(gradient_first)
    gradient_attended = to_low(gradient_one)
    gradient_adjust = column_sums(gradient_attended)
    gradient_merger = jnp.einsum(
        "tc,td->cd", context, gradient_attended, preferred_element_type=FLOAT_KIND
    )
    gradient_context = to_low(
        jnp.einsum("td,cd->tc", gradient_attended, merge_matrix, preferred_element_type=FLOAT_KIND)
    )
    gradient_context = gradient_context.reshape(block_count, BLOCK, head_count, head_size)
    gradient_queries, gradient_keys, gradient_values = lax.map(
        attend_backward, (queries, key_rows, values, block_marks, log_total, gradient_context)
    )
    gradient_packed = to_low(
        jnp.stack([gradient_queries, gradient_keys, gradient_values], axis=2).reshape(
            row_count, 3 * feature_breadth
        )
    )
    packed_sums = column_sums(gradient_packed)
    gradient_offsets = jnp.concatenate(
        [packed_sums[:feature_breadth], packed_sums[2 * feature_breadth :]]
    )
    gradient_projection = jnp.einsum(
        "td,te->de", rows_in, gradient_packed, preferred_element_type=FLOAT_KIND
    )
    tokens_gradient = gradient_one + jnp.einsum(
        "te,de->td", gradient_packed, focus_weighting_array, preferred_element_type=FLOAT_KIND
    )
    small = (
        gradient_offsets,
        gradient_adjust,
        gradient_scaling,
        gradient_centering,
        gradient_lifting,
        gradient_settling,
        gradient_rescale,
        gradient_recenter,
    )
    small_total = total_sum(jnp.concatenate(small), "batch")
    small_parts = []
    place = 0
    for part in small:
        small_parts.append(small_total[place : place + part.shape[0]])
        place += part.shape[0]
    total_contraction = weight_total(gradient_contraction)
    total_expansion = weight_total(gradient_expansion)
    total_merger = weight_total(gradient_merger)
    total_projection = weight_total(gradient_projection)
    attend_total = (total_projection, small_parts[0], total_merger, *small_parts[1:4])
    expand_total = (total_expansion, small_parts[4], total_contraction, *small_parts[5:8])
    return (
        to_low(encoded)[None],
        tokens_gradient[None],
        attend_total[0][None],
        attend_total[1][None],
        attend_total[2][None],
        attend_total[3][None],
        attend_total[4][None],
        attend_total[5][None],
        expand_total[0][None],
        expand_total[1][None],
        expand_total[2][None],
        expand_total[3][None],
        expand_total[4][None],
        expand_total[5][None],
    )


def solution(mesh):
    return jax.shard_map(
        shards,
        mesh=mesh,
        in_specs=(
            P("enc", "batch", None),
            P("enc", "batch", None),
            P("enc", None, None),
            P("enc", None),
            P("enc", None, None),
            P("enc", None),
            P("enc", None),
            P("enc", None),
            P("enc", None, None),
            P("enc", None),
            P("enc", None, None),
            P("enc", None),
            P("enc", None),
            P("enc", None),
            P("batch"),
            P("batch"),
            P(),
            P("batch"),
        ),
        out_specs=(
            P("enc", "batch", None),
            P("enc", "batch", None),
            P("enc", None, None),
            P("enc", None),
            P("enc", None, None),
            P("enc", None),
            P("enc", None),
            P("enc", None),
            P("enc", None, None),
            P("enc", None),
            P("enc", None, None),
            P("enc", None),
            P("enc", None),
            P("enc", None),
        ),
        check_vma=False,
    )
```

```python
import functools
import math

import jax
import jax.numpy as jnp
from jax import lax
from jax.experimental import pallas as pl
from jax.experimental.pallas import tpu as pltpu
from jax.sharding import PartitionSpec as P

QLEN = 64
ROWS = 256
HEAD = 64
TILE = 8
LANES = 128
EPSILON = 1e-12
SHARPNESS_DIVISOR = 2.0
LOSS_WEIGHT = 2.0
HIDDEN_SCORE = -1e30
FLOAT_KIND = jnp.float32
BRAIN = jnp.bfloat16

TAIL = tuple(
    0.5 * a for a in (0.254829592, -0.284496736, 1.421413741, -1.453152027, 1.061405429)
)
TAIL_SLOPE = 0.3275911 / math.sqrt(2.0)
DENSITY = 1.0 / math.sqrt(2.0 * math.pi)


def dot(left, right):
    return jnp.dot(left, right, preferred_element_type=FLOAT_KIND)


def dot_rows(left, right):
    return lax.dot_general(left, right, (((1,), (1,)), ((), ())), preferred_element_type=FLOAT_KIND)


def dot_columns(left, right):
    return lax.dot_general(left, right, (((0,), (0,)), ((), ())), preferred_element_type=FLOAT_KIND)


def whole(shape):
    return pl.BlockSpec(shape, lambda *_: (0,) * len(shape))


def row_block(rows, columns):
    return pl.BlockSpec((rows, columns), lambda i, *_: (i, 0))


def cost(flops, moved, transcendentals=0):
    return pl.CostEstimate(flops=flops, bytes_accessed=moved, transcendentals=transcendentals)


def wide(ref):
    return ref[...].astype(FLOAT_KIND)


def row_sum(values):
    return jnp.sum(values, axis=0, keepdims=True)


def normalized(values):
    centered = values - jnp.mean(values, axis=1, keepdims=True)
    spread = jnp.mean(centered * centered, axis=1, keepdims=True)
    scale = lax.rsqrt(spread + EPSILON)
    return centered * scale, scale


def norm_backward(gradient, normal, inverse, gain):
    scaled = gradient * gain
    return (
        scaled
        - jnp.mean(scaled, axis=1, keepdims=True)
        - normal * jnp.mean(scaled * normal, axis=1, keepdims=True)
    ) * inverse


def gelu_and_slope(hidden):
    bell = jnp.exp(hidden * hidden * -0.5)
    t = 1.0 / (1.0 + TAIL_SLOPE * jnp.abs(hidden))
    series = TAIL[3] + t * TAIL[4]
    series = TAIL[2] + t * series
    series = TAIL[1] + t * series
    series = TAIL[0] + t * series
    tail = t * series * bell
    below = jnp.where(hidden < 0.0, tail, 1.0 - tail)
    return hidden * below, below + hidden * bell * DENSITY


def attend_kernel(
    enc_ref,
    x_ref,
    project_ref,
    offset_ref,
    segment_ref,
    merge_ref,
    adjust_ref,
    gain_ref,
    shift_ref,
    packed_ref,
    weight_ref,
    context_ref,
    normal_ref,
    inverse_ref,
    low_ref,
):
    width = x_ref.shape[1]
    x = x_ref[...]
    for part in range(3):
        columns = slice(part * width, (part + 1) * width)
        sums = dot(x, project_ref[:, columns])
        if part != 1:
            at = 0 if part == 0 else width
            sums = sums + offset_ref[:, at : at + width].astype(FLOAT_KIND)
        packed_ref[:, columns] = sums.astype(BRAIN)
    position = lax.broadcasted_iota(jnp.int32, (1, ROWS), 1)
    marks = jnp.where(enc_ref[0] == 1, segment_ref[...], position // QLEN).astype(FLOAT_KIND)
    spread_marks = jnp.broadcast_to(marks, (ROWS, ROWS))
    hide = jnp.where(spread_marks == spread_marks.T, 0.0, HIDDEN_SCORE)
    low_lane = lax.broadcasted_iota(jnp.int32, (1, LANES), 1) < HEAD
    scale = 1.0 / math.sqrt(HEAD)
    for pair in range(width // LANES):
        at = LANES * pair
        queries = packed_ref[:, at : at + LANES] * scale
        keys = packed_ref[:, width + at : width + at + LANES]
        values = packed_ref[:, 2 * width + at : 2 * width + at + LANES]
        context = []
        for half in range(2):
            mine = low_lane if half == 0 else ~low_lane
            own = jnp.where(mine, queries, jnp.zeros_like(queries))
            scores = dot_rows(own, keys) + hide
            top = jnp.max(scores, axis=1, keepdims=True)
            raised = jnp.exp(scores - top)
            weights = (raised * (1.0 / jnp.sum(raised, axis=1, keepdims=True))).astype(BRAIN)
            weight_ref[2 * pair + half] = weights
            context.append(dot(weights, values))
        context_ref[:, at : at + LANES] = jnp.where(low_lane, context[0], context[1]).astype(BRAIN)
    attended = dot(context_ref[...], merge_ref[...]) + wide(adjust_ref)
    normal, inverse = normalized(x.astype(FLOAT_KIND) + attended)
    normal_ref[...] = normal
    inverse_ref[...] = inverse
    low_ref[...] = (normal * wide(gain_ref) + wide(shift_ref)).astype(BRAIN)


def attend(enc, x, project, offsets, segments, merge, adjust, gain, shift):
    count, width = x.shape
    blocks = count // ROWS
    heads = width // HEAD
    return pl.pallas_call(
        attend_kernel,
        grid_spec=pltpu.PrefetchScalarGridSpec(
            num_scalar_prefetch=1,
            grid=(blocks,),
            in_specs=[
                row_block(ROWS, width),
                whole(project.shape),
                whole(offsets.shape),
                pl.BlockSpec((1, ROWS), lambda i, *_: (0, i)),
                whole(merge.shape),
                whole(adjust.shape),
                whole(gain.shape),
                whole(shift.shape),
            ],
            out_specs=[
                row_block(ROWS, 3 * width),
                pl.BlockSpec((None, heads, ROWS, ROWS), lambda i, *_: (i, 0, 0, 0)),
                row_block(ROWS, width),
                row_block(ROWS, width),
                row_block(ROWS, 1),
                row_block(ROWS, width),
            ],
        ),
        out_shape=[
            jax.ShapeDtypeStruct((count, 3 * width), BRAIN),
            jax.ShapeDtypeStruct((blocks, heads, ROWS, ROWS), BRAIN),
            jax.ShapeDtypeStruct((count, width), BRAIN),
            jax.ShapeDtypeStruct((count, width), FLOAT_KIND),
            jax.ShapeDtypeStruct((count, 1), FLOAT_KIND),
            jax.ShapeDtypeStruct((count, width), BRAIN),
        ],
        cost_estimate=cost(10 * count * width * width, 24 * count * width, count * ROWS * heads),
        name="attend",
    )(enc, x, project, offsets, segments, merge, adjust, gain, shift)


def summary_kernel(
    enc_ref,
    start_ref,
    target_ref,
    normal_ref,
    gain_one_ref,
    shift_one_ref,
    expand_ref,
    lift_ref,
    shrink_ref,
    settle_ref,
    gain_two_ref,
    shift_two_ref,
    out_ref,
    tile_ref,
    row_ref,
    low_ref,
    total_ref,
    copy_sem,
):
    slots, width = row_ref.shape
    step = pl.program_id(0)

    @pl.when(step == 0)
    def _():
        copies = [
            pltpu.make_async_copy(
                normal_ref.at[jnp.where(enc_ref[0] == 1, start_ref[slot], slot * QLEN) // TILE],
                tile_ref.at[slot],
                copy_sem.at[slot],
            )
            for slot in range(slots)
        ]
        for copy in copies:
            copy.start()
        for copy in copies:
            copy.wait()
        rows = tile_ref[:, 0, :] * wide(gain_one_ref) + wide(shift_one_ref)
        row_ref[...] = rows
        low_ref[...] = rows.astype(BRAIN)
        total_ref[...] = jnp.zeros_like(total_ref)

    activated, _ = gelu_and_slope(dot(low_ref[...], expand_ref[...]) + wide(lift_ref))
    total_ref[...] += dot(activated.astype(BRAIN), shrink_ref[...])

    @pl.when(step == pl.num_programs(0) - 1)
    def _():
        normal, _ = normalized(row_ref[...] + (total_ref[...] + wide(settle_ref)))
        out_ref[:, :width] = (normal * wide(gain_two_ref) + wide(shift_two_ref)).astype(BRAIN)
        lane = lax.broadcasted_iota(jnp.int32, (slots, LANES), 1)
        place = lax.broadcasted_iota(jnp.int32, (slots, LANES), 0)
        digits = jnp.zeros((slots, LANES), jnp.int32)
        for slot in range(slots):
            target = target_ref[slot]
            pair = jnp.where(lane == 0, target // LANES, jnp.where(lane == 1, target % LANES, 0))
            digits = jnp.where(place == slot, pair, digits)
        out_ref[:, width:] = digits.astype(FLOAT_KIND).astype(BRAIN)


def summarize(enc, starts, targets, normal, first, expand, lift, shrink, settle, second, tn=512):
    count, width = normal.shape
    hidden = expand.shape[1]
    slots = starts.shape[0]
    row = whole((1, width))
    return pl.pallas_call(
        summary_kernel,
        grid_spec=pltpu.PrefetchScalarGridSpec(
            num_scalar_prefetch=3,
            grid=(hidden // tn,),
            in_specs=[
                pl.BlockSpec(memory_space=pl.ANY),
                row,
                row,
                pl.BlockSpec((width, tn), lambda i, *_: (0, i)),
                pl.BlockSpec((1, tn), lambda i, *_: (0, i)),
                pl.BlockSpec((tn, width), lambda i, *_: (i, 0)),
                row,
                row,
                row,
            ],
            out_specs=whole((slots, width + LANES)),
            scratch_shapes=[
                pltpu.VMEM((slots, TILE, width), FLOAT_KIND),
                pltpu.VMEM((slots, width), FLOAT_KIND),
                pltpu.VMEM((slots, width), BRAIN),
                pltpu.VMEM((slots, width), FLOAT_KIND),
                pltpu.SemaphoreType.DMA((slots,)),
            ],
        ),
        out_shape=jax.ShapeDtypeStruct((slots, width + LANES), BRAIN),
        cost_estimate=cost(4 * slots * width * hidden, 4 * width * hidden, slots * hidden),
        name="summarize",
    )(
        enc,
        starts,
        targets,
        normal.reshape(count // TILE, TILE, width),
        *first,
        expand,
        lift,
        shrink,
        settle,
        *second,
    )


def widen_kernel(low_ref, expand_ref, lift_ref, *refs):
    active_ref, slope_ref = refs[-2:]
    hidden = dot(low_ref[...], expand_ref[...]) + wide(lift_ref)
    activated, slope = gelu_and_slope(hidden)
    active_ref[...] = activated.astype(BRAIN)
    slope_ref[...] = slope.astype(BRAIN)


def widen(part, parts, low, expand, lift, before, tn=384):
    count, width = low.shape
    hidden = expand.shape[1]
    steps = hidden // parts // tn
    column = lambda rows: pl.BlockSpec((rows, tn), lambda i: (0, part * steps + i))
    kept = [] if before is None else list(before)
    return pl.pallas_call(
        widen_kernel,
        grid=(steps,),
        in_specs=[whole(low.shape), column(width), column(1)]
        + [pl.BlockSpec(memory_space=pl.ANY)] * len(kept),
        out_specs=[column(count), column(count)],
        out_shape=[jax.ShapeDtypeStruct((count, hidden), BRAIN)] * 2,
        input_output_aliases={3 + k: k for k in range(len(kept))},
        cost_estimate=cost(
            2 * count * width * hidden // parts, 4 * count * hidden // parts, count * hidden // parts
        ),
        name="widen",
    )(low, expand, lift, *kept)


def shrink_kernel(
    active_ref,
    shrink_ref,
    normal_ref,
    gain_one_ref,
    shift_one_ref,
    settle_ref,
    gain_two_ref,
    shift_two_ref,
    out_ref,
    inverse_ref,
    encoded_ref,
):
    normed = normal_ref[...] * wide(gain_one_ref) + wide(shift_one_ref)
    shrunk = dot(active_ref[...], shrink_ref[...]) + wide(settle_ref)
    normal, inverse = normalized(normed + shrunk)
    out_ref[...] = normal
    inverse_ref[...] = inverse
    encoded_ref[...] = (normal * wide(gain_two_ref) + wide(shift_two_ref)).astype(BRAIN)


def shrink_back_to_width(active, shrink, normal, first, settle, second, tm=256):
    count, hidden = active.shape
    width = shrink.shape[1]
    row = whole((1, width))
    return pl.pallas_call(
        shrink_kernel,
        grid=(count // tm,),
        in_specs=[row_block(tm, hidden), whole(shrink.shape), row_block(tm, width)] + [row] * 5,
        out_specs=[row_block(tm, width), row_block(tm, 1), row_block(tm, width)],
        out_shape=[
            jax.ShapeDtypeStruct((count, width), FLOAT_KIND),
            jax.ShapeDtypeStruct((count, 1), FLOAT_KIND),
            jax.ShapeDtypeStruct((count, width), BRAIN),
        ],
        cost_estimate=cost(2 * count * width * hidden, 2 * count * hidden + 10 * count * width),
        name="shrink",
    )(active, shrink, normal, *first, settle, *second)


def contrast_kernel(
    enc_ref,
    start_ref,
    every_ref,
    column_ref,
    normal_ref,
    inverse_ref,
    cotangent_ref,
    gain_ref,
    two_ref,
    low_ref,
    sums_ref,
    summary_ref,
    rows_ref,
):
    width = normal_ref.shape[1]
    slots = start_ref.shape[0]
    devices = every_ref.shape[0]
    step = pl.program_id(0)
    sharpness = SHARPNESS_DIVISOR / math.sqrt(width)

    def flat(which, at, count):
        return every_ref[pl.ds(at, count), which].reshape(count * slots, width + LANES)

    def logits_of(questions, passages):
        return jnp.where(
            column_ref[...] >= 0, dot_rows(questions, passages) * sharpness, HIDDEN_SCORE
        )

    def targets_of(rows):
        digits = rows[:, width:].astype(FLOAT_KIND)
        return (digits[:, 0:1] * LANES + digits[:, 1:2]).astype(jnp.int32)

    @pl.when(step == 0)
    def _():
        sums_ref[...] = jnp.zeros_like(sums_ref)

        @pl.when(enc_ref[0] == 0)
        def _():
            own = every_ref[0, 0]
            passages = flat(1, 0, devices)[:, :width]
            logits = logits_of(own[:, :width], passages)
            top = jnp.max(logits, axis=1, keepdims=True)
            raised = jnp.exp(logits - top)
            probability = raised / jnp.sum(raised, axis=1, keepdims=True)
            hit = (column_ref[...] == targets_of(own)).astype(FLOAT_KIND)
            gradient = (LOSS_WEIGHT * (probability - hit)).astype(BRAIN)
            summary_ref[...] = dot(gradient, passages) * sharpness

        @pl.when(enc_ref[0] == 1)
        def _():
            passages = flat(0, 0, devices)[:, :width]
            block = 16

            def part(at):
                rows = flat(1, at, block)
                questions = rows[:, :width]
                logits = logits_of(questions, passages)
                top = jnp.max(logits, axis=1, keepdims=True)
                total = jnp.sum(jnp.exp(logits - top), axis=1, keepdims=True)
                probability = jnp.exp(logits[:, :LANES] - top) / total
                hit = (column_ref[:, :LANES] == targets_of(rows)).astype(FLOAT_KIND)
                gradient = (LOSS_WEIGHT * (probability - hit)).astype(BRAIN)
                return dot_columns(gradient, questions)[:slots] * sharpness

            if devices == block:
                summary_ref[...] = part(0)
            else:
                summary_ref[...] = jnp.zeros_like(summary_ref)

                @pl.loop(0, devices // block)
                def _(k):
                    summary_ref[...] += part(k * block)

    rows_ref[...] = wide(cotangent_ref)
    tiles = rows_ref.shape[0] // TILE
    first = lax.broadcasted_iota(jnp.int32, (TILE, 1), 0) == 0
    for slot in range(slots):
        start = jnp.where(enc_ref[0] == 1, start_ref[slot], slot * QLEN)
        local = start // TILE - step * tiles
        inside = (local >= 0) & (local < tiles)
        at = pl.multiple_of(jnp.clip(local, 0, tiles - 1) * TILE, TILE)
        rows_ref[pl.ds(at, TILE), :] += jnp.where(
            first & inside, summary_ref[slot : slot + 1, :], 0.0
        )
    gradient = rows_ref[...]
    normal = normal_ref[...]
    sums_ref[0:1] += row_sum(gradient * normal)
    sums_ref[1:2] += row_sum(gradient)
    two = norm_backward(gradient, normal, inverse_ref[...], wide(gain_ref))
    two_ref[...] = two
    low = two.astype(BRAIN)
    low_ref[...] = low
    sums_ref[2:3] += row_sum(low.astype(FLOAT_KIND))


def contrast(enc, starts, every, columns, normal, inverse, cotangent, gain, tm=256):
    count, width = normal.shape
    slots = starts.shape[0]
    return pl.pallas_call(
        contrast_kernel,
        grid_spec=pltpu.PrefetchScalarGridSpec(
            num_scalar_prefetch=2,
            grid=(count // tm,),
            in_specs=[
                whole(every.shape),
                whole(columns.shape),
                row_block(tm, width),
                row_block(tm, 1),
                row_block(tm, width),
                whole(gain.shape),
            ],
            out_specs=[row_block(tm, width), row_block(tm, width), whole((TILE, width))],
            scratch_shapes=[
                pltpu.VMEM((slots, width), FLOAT_KIND),
                pltpu.VMEM((tm, width), FLOAT_KIND),
            ],
        ),
        out_shape=[
            jax.ShapeDtypeStruct((count, width), FLOAT_KIND),
            jax.ShapeDtypeStruct((count, width), BRAIN),
            jax.ShapeDtypeStruct((TILE, width), FLOAT_KIND),
        ],
        cost_estimate=cost(2 * every.size * 256, 12 * count * width),
        name="contrast",
    )(enc, starts, every, columns, normal, inverse, cotangent, gain)


def product_kernel(half_ref, left_ref, right_ref, out_ref):
    out_ref[...] = dot_columns(left_ref[...], right_ref[...]).astype(BRAIN)


def contraction_half(half, active, low, tn=768):
    count, hidden = active.shape
    width = low.shape[1]
    steps = hidden // 2 // tn
    return pl.pallas_call(
        product_kernel,
        grid_spec=pltpu.PrefetchScalarGridSpec(
            num_scalar_prefetch=1,
            grid=(steps,),
            in_specs=[
                pl.BlockSpec((count, tn), lambda i, half: (0, half[0] * steps + i)),
                whole(low.shape),
            ],
            out_specs=row_block(tn, width),
        ),
        out_shape=jax.ShapeDtypeStruct((hidden // 2, width), BRAIN),
        cost_estimate=cost(count * width * hidden, count * hidden + 2 * count * width),
        name="contraction_half",
    )(half, active, low)


def feed_kernel(
    half_ref,
    two_low_ref,
    shrink_ref,
    slope_ref,
    send_low_ref,
    keep_low_ref,
    expand_ref,
    two_ref,
    send_ref,
    keep_ref,
    lift_ref,
    first_ref,
):
    hidden = dot_rows(two_low_ref[...], shrink_ref[...]) * wide(slope_ref)
    low = hidden.astype(BRAIN)
    lift_ref[...] = row_sum(low.astype(FLOAT_KIND))
    send_ref[...] = dot_columns(send_low_ref[...], low).astype(BRAIN)
    keep_ref[...] = dot_columns(keep_low_ref[...], low).astype(BRAIN)

    @pl.when(pl.program_id(0) == 0)
    def _():
        first_ref[...] = two_ref[...]

    first_ref[...] += dot_rows(low, expand_ref[...])


def feed_back(half, two_low, shrink, slope, low, expand, two, tn=768):
    count, width = two.shape
    hidden = shrink.shape[0]
    split = width // 2
    column = lambda rows: pl.BlockSpec((rows, tn), lambda i, half: (0, i))
    return pl.pallas_call(
        feed_kernel,
        grid_spec=pltpu.PrefetchScalarGridSpec(
            num_scalar_prefetch=1,
            grid=(hidden // tn,),
            in_specs=[
                whole((count, width)),
                row_block(tn, width),
                column(count),
                pl.BlockSpec((count, split), lambda i, half: (0, half[0])),
                pl.BlockSpec((count, split), lambda i, half: (0, 1 - half[0])),
                column(width),
                whole((count, width)),
            ],
            out_specs=[column(split), column(split), column(1), whole((count, width))],
        ),
        out_shape=[
            jax.ShapeDtypeStruct((split, hidden), BRAIN),
            jax.ShapeDtypeStruct((split, hidden), BRAIN),
            jax.ShapeDtypeStruct((1, hidden), FLOAT_KIND),
            jax.ShapeDtypeStruct((count, width), FLOAT_KIND),
        ],
        cost_estimate=cost(6 * count * width * hidden, 2 * count * hidden + 14 * count * width),
        name="feed_back",
    )(half, two_low, shrink, slope, low, low, expand, two)


def attend_back_kernel(
    first_ref,
    normal_ref,
    inverse_ref,
    gain_ref,
    merge_ref,
    packed_ref,
    weight_ref,
    context_ref,
    one_ref,
    low_ref,
    packed_gradient_ref,
    sums_ref,
    packed_sums_ref,
    context_gradient_ref,
):
    width = normal_ref.shape[1]

    @pl.when(pl.program_id(0) == 0)
    def _():
        sums_ref[...] = jnp.zeros_like(sums_ref)
        packed_sums_ref[...] = jnp.zeros_like(packed_sums_ref)

    gradient = first_ref[...]
    normal = normal_ref[...]
    sums_ref[0:1] += row_sum(gradient * normal)
    sums_ref[1:2] += row_sum(gradient)
    one = norm_backward(gradient, normal, inverse_ref[...], wide(gain_ref))
    one_ref[...] = one
    low = one.astype(BRAIN)
    low_ref[...] = low
    sums_ref[2:3] += row_sum(low.astype(FLOAT_KIND))
    context_gradient_ref[...] = dot_rows(low, merge_ref[...]).astype(BRAIN)
    low_lane = lax.broadcasted_iota(jnp.int32, (1, LANES), 1) < HEAD
    scale = 1.0 / math.sqrt(HEAD)
    for pair in range(width // LANES):
        at = LANES * pair
        queries = packed_ref[:, at : at + LANES] * scale
        keys = packed_ref[:, width + at : width + at + LANES] * scale
        values = packed_ref[:, 2 * width + at : 2 * width + at + LANES]
        outer = context_gradient_ref[:, at : at + LANES]
        products = outer.astype(FLOAT_KIND) * context_ref[:, at : at + LANES].astype(FLOAT_KIND)
        found = ([], [], [])
        for half in range(2):
            mine = low_lane if half == 0 else ~low_lane
            weights = weight_ref[2 * pair + half]
            own = jnp.where(mine, outer, jnp.zeros_like(outer))
            row_dots = jnp.sum(jnp.where(mine, products, 0.0), axis=1, keepdims=True)
            inner = dot_rows(own, values) - row_dots
            scores = (weights.astype(FLOAT_KIND) * inner).astype(BRAIN)
            found[0].append(dot(scores, keys))
            found[1].append(dot_columns(scores, queries))
            found[2].append(dot_columns(weights, outer))
        for part in range(3):
            packed_gradient_ref[:, part * width + at : part * width + at + LANES] = jnp.where(
                low_lane, found[part][0], found[part][1]
            ).astype(BRAIN)
    packed_sums_ref[...] += row_sum(wide(packed_gradient_ref))


def attend_back(first, normal, inverse, gain, merge, packed, weights, context):
    count, width = normal.shape
    heads = width // HEAD
    return pl.pallas_call(
        attend_back_kernel,
        grid=(count // ROWS,),
        in_specs=[
            row_block(ROWS, width),
            row_block(ROWS, width),
            row_block(ROWS, 1),
            whole(gain.shape),
            whole(merge.shape),
            row_block(ROWS, 3 * width),
            pl.BlockSpec((None, heads, ROWS, ROWS), lambda i: (i, 0, 0, 0)),
            row_block(ROWS, width),
        ],
        out_specs=[
            row_block(ROWS, width),
            row_block(ROWS, width),
            row_block(ROWS, 3 * width),
            whole((TILE, width)),
            whole((1, 3 * width)),
        ],
        out_shape=[
            jax.ShapeDtypeStruct((count, width), FLOAT_KIND),
            jax.ShapeDtypeStruct((count, width), BRAIN),
            jax.ShapeDtypeStruct((count, 3 * width), BRAIN),
            jax.ShapeDtypeStruct((TILE, width), FLOAT_KIND),
            jax.ShapeDtypeStruct((1, 3 * width), FLOAT_KIND),
        ],
        scratch_shapes=[pltpu.VMEM((ROWS, width), BRAIN)],
        cost_estimate=cost(12 * count * width * width, 38 * count * width),
        name="attend_back",
    )(first, normal, inverse, gain, merge, packed, weights, context)


def merge_project_kernel(half_ref, context_ref, one_ref, x_ref, packed_ref, out_ref, *, split):
    @pl.when(pl.program_id(0) < split)
    def _():
        out_ref[...] = dot_columns(context_ref[...], one_ref[...]).astype(BRAIN)

    @pl.when(pl.program_id(0) >= split)
    def _():
        out_ref[...] = dot_columns(x_ref[...], packed_ref[...]).astype(BRAIN)


def merge_project_half(half, context, one, x, packed, tn=768):
    count, width = x.shape
    rows = width // 2
    split = width // tn
    return pl.pallas_call(
        functools.partial(merge_project_kernel, split=split),
        grid_spec=pltpu.PrefetchScalarGridSpec(
            num_scalar_prefetch=1,
            grid=(4 * width // tn,),
            in_specs=[
                pl.BlockSpec((count, rows), lambda i, half: (0, half[0])),
                pl.BlockSpec((count, tn), lambda i, half: (0, jnp.minimum(i, split - 1))),
                pl.BlockSpec((count, rows), lambda i, half: (0, half[0])),
                pl.BlockSpec((count, tn), lambda i, half: (0, jnp.maximum(i - split, 0))),
            ],
            out_specs=pl.BlockSpec((rows, tn), lambda i, half: (0, i)),
        ),
        out_shape=jax.ShapeDtypeStruct((rows, 4 * width), BRAIN),
        cost_estimate=cost(4 * count * width * width, 10 * count * width),
        name="merge_project_half",
    )(half, context, one, x, packed)


def tokens_kernel(one_ref, packed_ref, project_ref, out_ref):
    out_ref[...] = one_ref[...] + dot_rows(packed_ref[...], project_ref[...])


def tokens_back(one, packed, project, tm=256):
    count, width = one.shape
    return pl.pallas_call(
        tokens_kernel,
        grid=(count // tm,),
        in_specs=[row_block(tm, width), row_block(tm, 3 * width), whole(project.shape)],
        out_specs=row_block(tm, width),
        out_shape=jax.ShapeDtypeStruct((count, width), FLOAT_KIND),
        cost_estimate=cost(6 * count * width * width, 14 * count * width),
        name="tokens_back",
    )(one, packed, project)


def pack_kernel(packed_ref, attend_ref, lift_ref, output_ref, out_ref):
    width = attend_ref.shape[1]
    out_ref[...] = jnp.zeros_like(out_ref)
    out_ref[0:1] = packed_ref[:, :width]
    out_ref[1:2] = packed_ref[:, 2 * width :]
    out_ref[2:5] = attend_ref[0:3]
    for part in range(4):
        out_ref[5 + part : 6 + part] = lift_ref[:, part * width : (part + 1) * width]
    out_ref[9:12] = output_ref[0:3]


def pack_vectors(packed_sums, attend_sums, lift_sums, output_sums):
    width = attend_sums.shape[1]
    return pl.pallas_call(
        pack_kernel,
        out_shape=jax.ShapeDtypeStruct((16, width), FLOAT_KIND),
        name="pack_vectors",
    )(packed_sums, attend_sums, lift_sums, output_sums)


def unpack_kernel(mine_ref, other_ref, offset_ref, adjust_ref, scale_ref, center_ref, lift_ref, settle_ref, rescale_ref, recenter_ref):
    width = mine_ref.shape[1]
    total = mine_ref[...] + other_ref[...]
    offset_ref[:, :width] = total[0:1]
    offset_ref[:, width:] = total[1:2]
    scale_ref[...] = total[2:3]
    center_ref[...] = total[3:4]
    adjust_ref[...] = total[4:5]
    for part in range(4):
        lift_ref[:, part * width : (part + 1) * width] = total[5 + part : 6 + part]
    rescale_ref[...] = total[9:10]
    recenter_ref[...] = total[10:11]
    settle_ref[...] = total[11:12]


def unpack_vectors(mine, other):
    width = mine.shape[1]
    shapes = [2, 1, 1, 1, 4, 1, 1, 1]
    return pl.pallas_call(
        unpack_kernel,
        out_shape=[jax.ShapeDtypeStruct((1, k * width), FLOAT_KIND) for k in shapes],
        name="unpack_vectors",
    )(mine, other)


def place_half(half, value, columns, before, tm):
    rows = value.shape[0]
    steps = rows // tm
    kept = [] if before is None else list(before)

    def kernel(half_ref, value_ref, *refs):
        at = 0
        for out in refs[len(kept) :]:
            out[...] = value_ref[:, at : at + out.shape[-1]].astype(FLOAT_KIND)
            at += out.shape[-1]

    return pl.pallas_call(
        kernel,
        grid_spec=pltpu.PrefetchScalarGridSpec(
            num_scalar_prefetch=1,
            grid=(steps,),
            in_specs=[row_block(tm, value.shape[1])]
            + [pl.BlockSpec(memory_space=pl.ANY)] * len(kept),
            out_specs=[
                pl.BlockSpec((tm, size), lambda i, half: (half[0] * steps + i, 0))
                for size in columns
            ],
        ),
        out_shape=[jax.ShapeDtypeStruct((2 * rows, size), FLOAT_KIND) for size in columns],
        input_output_aliases={2 + k: k for k in range(len(kept))},
        cost_estimate=cost(0, 6 * value.size),
        name="place_half",
    )(half, value, *kept)


def swapped(value, axis, apart):
    mask = 2**apart
    pairs = [(source, source ^ mask) for source in range(lax.axis_size(axis))]
    return lax.ppermute(value, axis, pairs)


def bit_count(axis):
    return lax.axis_size(axis).bit_length() - 1


def to_low(values):
    return values.astype(BRAIN)


def part_sum(mine, other, bit):
    half = mine.shape[0] // 2
    left = lax.dynamic_slice_in_dim(mine, bit * half, half, 0).astype(FLOAT_KIND)
    right = lax.dynamic_slice_in_dim(other, bit * half, half, 0).astype(FLOAT_KIND)
    return to_low(left + right)


def joined_by_bit(mine, other, bit):
    low_part = jnp.where(bit == 0, mine, other)
    high_part = jnp.where(bit == 0, other, mine)
    return jnp.concatenate([low_part, high_part], axis=0)


class Sequence:
    def __init__(self):
        self.last = None

    def run(self, step, *inputs):
        if self.last is not None:
            *inputs, _ = lax.optimization_barrier((*inputs, self.last))
        result = step(*inputs)
        self.last = jax.tree.leaves(result)[0]
        return result


class Reduction:
    def __init__(self, index, columns, tm):
        self.index = index
        self.columns = columns
        self.tm = tm
        self.bits = bit_count("batch")

    def begin(self, send, keep):
        self.keep = keep
        self.other = swapped(send, "batch", 0)

    def scatter(self, sequence, apart):
        bit = (self.index >> apart) & 1
        send = sequence.run(lambda k, o: part_sum(k, o, 1 - bit), self.keep, self.other)
        self.keep = part_sum(self.keep, self.other, bit)
        self.other = swapped(send, "batch", apart)

    def finish(self, sequence):
        self.value = sequence.run(
            lambda k, o: to_low(k.astype(FLOAT_KIND) + o.astype(FLOAT_KIND)), self.keep, self.other
        )
        self.other = swapped(self.value, "batch", self.bits - 1)

    def gather(self, sequence, apart):
        bit = (self.index >> apart) & 1
        self.value = sequence.run(lambda v, o: joined_by_bit(v, o, bit), self.value, self.other)
        self.other = swapped(self.value, "batch", apart - 1)
        if apart == 1:
            half = (self.index & 1)[None]
            self.placed = place_half(half, self.value, self.columns, None, self.tm)

    def place(self, sequence):
        half = 1 - (self.index & 1)[None]
        return sequence.run(
            lambda o, *p: place_half(half, o, self.columns, p, self.tm), self.other, *self.placed
        )


def shards(
    tokens,
    cotangent,
    projection,
    offsets,
    merger,
    adjust,
    scaling,
    centering,
    expansion,
    lifting,
    contraction,
    settling,
    rescale,
    recenter,
    segments,
    passage_starts,
    passage_counts,
    positives,
):
    enc = lax.axis_index("enc").astype(jnp.int32)[None]
    index = lax.axis_index("batch").astype(jnp.int32)
    x = tokens[0]
    count, width = x.shape
    slots = passage_starts.shape[0]
    first = (scaling, centering)
    second = (rescale, recenter)
    keep_half = (index & 1)[None]
    send_half = 1 - keep_half

    sequence = Sequence()
    run = sequence.run
    packed, weights, context, normal_one, inverse_one, low = attend(
        enc, x, projection[0], offsets, segments[None], merger[0], adjust, *first
    )
    parcel = summarize(
        enc,
        passage_starts,
        positives,
        normal_one,
        first,
        expansion[0],
        lifting,
        contraction[0],
        settling,
        second,
    )
    sequence.last = parcel
    order = list(reversed(range(bit_count("batch"))))
    place = jnp.arange(lax.axis_size("batch"), dtype=jnp.int32)
    away = sum(((place >> k) & 1) << apart for k, apart in enumerate(order))
    device = (index ^ away)[:, None]
    slot = jnp.arange(slots, dtype=jnp.int32)[None, :]
    held = jnp.sum(jnp.where(device == place[None, :], passage_counts[None, :], 0), axis=1)
    columns = jnp.where(slot < held[:, None], device * slots + slot, -1).reshape(1, -1)

    parts = 4
    every = parcel[None]
    other = swapped(parcel, "enc", 0)[None]
    wide_pair = run(lambda v: widen(0, parts, v, expansion[0], lifting, None), low)
    every = run(lambda a, b: jnp.stack([a, b], axis=1), every, other)
    for part, apart in enumerate(order, 1):
        other = swapped(every, "batch", apart)
        if part < parts:
            wide_pair = run(
                lambda v, *p: widen(part, parts, v, expansion[0], lifting, p), low, *wide_pair
            )
        elif part == parts:
            active, slope = wide_pair
            normal_two, inverse_two, encoded = run(
                lambda a, n: shrink_back_to_width(a, contraction[0], n, first, settling, second),
                active,
                normal_one,
            )
        every = run(lambda a, b: jnp.concatenate([a, b], axis=0), every, other)
    two, two_low, output_sums = run(
        lambda *v: contrast(enc, passage_starts, *v, rescale),
        every,
        columns,
        normal_two,
        inverse_two,
        cotangent[0],
    )

    bits = bit_count("batch")
    shrink_sum = Reduction(index, (width,), 768)
    expand_sum = Reduction(index, (expansion.shape[2],), 192)
    project_sum = Reduction(index, (width, projection.shape[2]), 192)
    send = run(lambda a, t: contraction_half(send_half, a, t), active, two_low)
    keep = run(lambda a, t: contraction_half(keep_half, a, t), active, two_low)
    shrink_sum.begin(send, keep)
    shrink_sum.scatter(sequence, 1)
    send, keep, lift_sums, gradient_first = run(
        lambda t, s, g: feed_back(send_half, t, contraction[0], s, low, expansion[0], g),
        two_low,
        slope,
        two,
    )
    expand_sum.begin(send, keep)
    expand_sum.scatter(sequence, 1)
    shrink_sum.scatter(sequence, 2)
    one, one_low, packed_gradient, attend_sums, packed_sums = run(
        lambda g, n, i, p, w, c: attend_back(g, n, i, scaling, merger[0], p, w, c),
        gradient_first,
        normal_one,
        inverse_one,
        packed,
        weights,
        context,
    )
    for apart in range(3, bits):
        shrink_sum.scatter(sequence, apart)
    product = lambda half: run(
        lambda c, o, v, p: merge_project_half(half, c, o, v, p),
        context,
        one_low,
        x,
        packed_gradient,
    )
    send = product(send_half)
    keep = product(keep_half)
    project_sum.begin(send, keep)
    project_sum.scatter(sequence, 1)
    shrink_sum.finish(sequence)
    for apart in range(2, bits):
        expand_sum.scatter(sequence, apart)
    tokens_gradient = run(
        lambda o, p: tokens_back(o, p, projection[0]), one, packed_gradient
    )
    vectors = run(pack_vectors, packed_sums, attend_sums, lift_sums, output_sums)
    for apart in reversed(range(2, bits)):
        shrink_sum.gather(sequence, apart)
    expand_sum.finish(sequence)
    vectors = run(lambda a, b: a + b, vectors, swapped(vectors, "batch", 0))
    for apart in range(2, bits):
        project_sum.scatter(sequence, apart)
        expand_sum.gather(sequence, bits + 1 - apart)
        vectors = run(lambda a, b: a + b, vectors, swapped(vectors, "batch", apart - 1))
    project_sum.finish(sequence)
    for apart in reversed(range(2, bits)):
        project_sum.gather(sequence, apart)
    shrink_sum.gather(sequence, 1)
    vector_totals = run(unpack_vectors, vectors, swapped(vectors, "batch", bits - 1))
    expand_sum.gather(sequence, 1)
    (total_contraction,) = shrink_sum.place(sequence)
    project_sum.gather(sequence, 1)
    (total_expansion,) = expand_sum.place(sequence)
    total_merger, total_projection = project_sum.place(sequence)
    (
        total_offsets,
        total_adjust,
        total_scaling,
        total_centering,
        total_lifting,
        total_settling,
        total_rescale,
        total_recenter,
    ) = vector_totals
    return (
        encoded[None],
        tokens_gradient[None],
        total_projection[None],
        total_offsets,
        total_merger[None],
        total_adjust,
        total_scaling,
        total_centering,
        total_expansion[None],
        total_lifting,
        total_contraction[None],
        total_settling,
        total_rescale,
        total_recenter,
    )


def solution(mesh):
    matrix = P("enc", None, None)
    vector = P("enc", None)
    rows = P("enc", "batch", None)
    return jax.shard_map(
        shards,
        mesh=mesh,
        in_specs=(
            rows,
            rows,
            matrix,
            vector,
            matrix,
            vector,
            vector,
            vector,
            matrix,
            vector,
            matrix,
            vector,
            vector,
            vector,
            P("batch"),
            P("batch"),
            P(),
            P("batch"),
        ),
        out_specs=(
            rows,
            rows,
            matrix,
            vector,
            matrix,
            vector,
            vector,
            vector,
            matrix,
            vector,
            matrix,
            vector,
            vector,
            vector,
        ),
        check_vma=False,
    )
```

```python
import functools
import math

import jax
import jax.numpy as jnp
from jax import lax
from jax.experimental import pallas as pl
from jax.experimental.pallas import tpu as pltpu
from jax.sharding import PartitionSpec as P

QLEN = 64
ROWS = 256
HEAD = 64
TILE = 8
LANES = 128
PIECES = 4
PACKED = 16
ENC, KEEP, SEND = 0, 1, 2
MEGA = 2**20
EPSILON = 1e-12
SHARPNESS_DIVISOR = 2.0
LOSS_WEIGHT = 2.0
HIDDEN_SCORE = -1e30
FLOAT_KIND = jnp.float32
BRAIN = jnp.bfloat16

TAIL = tuple(
    0.5 * a for a in (0.254829592, -0.284496736, 1.421413741, -1.453152027, 1.061405429)
)
TAIL_SLOPE = 0.3275911 / math.sqrt(2.0)
DENSITY = 1.0 / math.sqrt(2.0 * math.pi)


def dot(left, right):
    return jnp.dot(left, right, preferred_element_type=FLOAT_KIND)


def dot_rows(left, right):
    return lax.dot_general(left, right, (((1,), (1,)), ((), ())), preferred_element_type=FLOAT_KIND)


def dot_columns(left, right):
    return lax.dot_general(left, right, (((0,), (0,)), ((), ())), preferred_element_type=FLOAT_KIND)


def whole(shape):
    return pl.BlockSpec(shape, lambda *_: (0,) * len(shape))


def row_block(rows, columns):
    return pl.BlockSpec((rows, columns), lambda i, *_: (i, 0))


def in_hbm(value):
    return pltpu.with_memory_space_constraint(value, pltpu.HBM)


def hbm_shape(shape, dtype):
    return pltpu.HBM(shape, dtype)


def cost(flops, moved, transcendentals=0):
    return pl.CostEstimate(flops=1, bytes_accessed=1, transcendentals=0)


def wide(ref):
    return ref[...].astype(FLOAT_KIND)


def row_sum(values):
    return jnp.sum(values, axis=0, keepdims=True)


def normalized(values):
    centered = values - jnp.mean(values, axis=1, keepdims=True)
    spread = jnp.mean(centered * centered, axis=1, keepdims=True)
    scale = lax.rsqrt(spread + EPSILON)
    return centered * scale, scale


def norm_backward(gradient, normal, inverse, gain):
    scaled = gradient * gain
    return (
        scaled
        - jnp.mean(scaled, axis=1, keepdims=True)
        - normal * jnp.mean(scaled * normal, axis=1, keepdims=True)
    ) * inverse


def gelu_and_slope(hidden):
    bell = jnp.exp(hidden * hidden * -0.5)
    t = 1.0 / (1.0 + TAIL_SLOPE * jnp.abs(hidden))
    series = TAIL[3] + t * TAIL[4]
    series = TAIL[2] + t * series
    series = TAIL[1] + t * series
    series = TAIL[0] + t * series
    tail = t * series * bell
    below = jnp.where(hidden < 0.0, tail, 1.0 - tail)
    return hidden * below, below + hidden * bell * DENSITY


def attend_kernel(
    flag_ref,
    x_ref,
    project_ref,
    offset_ref,
    segment_ref,
    merge_ref,
    adjust_ref,
    gain_ref,
    shift_ref,
    packed_ref,
    weight_ref,
    context_ref,
    normal_ref,
    inverse_ref,
    low_ref,
):
    width = x_ref.shape[1]
    x = x_ref[...]
    for part in range(3):
        columns = slice(part * width, (part + 1) * width)
        sums = dot(x, project_ref[:, columns])
        if part != 1:
            at = 0 if part == 0 else width
            sums = sums + offset_ref[:, at : at + width].astype(FLOAT_KIND)
        packed_ref[:, columns] = sums.astype(BRAIN)
    position = lax.broadcasted_iota(jnp.int32, (1, ROWS), 1)
    marks = jnp.where(flag_ref[ENC] == 1, segment_ref[...], position // QLEN).astype(FLOAT_KIND)
    spread_marks = jnp.broadcast_to(marks, (ROWS, ROWS))
    hide = jnp.where(spread_marks == spread_marks.T, 0.0, HIDDEN_SCORE)
    low_lane = lax.broadcasted_iota(jnp.int32, (1, LANES), 1) < HEAD
    scale = 1.0 / math.sqrt(HEAD)
    for pair in range(width // LANES):
        at = LANES * pair
        queries = packed_ref[:, at : at + LANES] * scale
        keys = packed_ref[:, width + at : width + at + LANES]
        values = packed_ref[:, 2 * width + at : 2 * width + at + LANES]
        context = []
        for half in range(2):
            mine = low_lane if half == 0 else ~low_lane
            own = jnp.where(mine, queries, jnp.zeros_like(queries))
            scores = dot_rows(own, keys) + hide
            top = jnp.max(scores, axis=1, keepdims=True)
            raised = jnp.exp(scores - top)
            weights = (raised * (1.0 / jnp.sum(raised, axis=1, keepdims=True))).astype(BRAIN)
            weight_ref[2 * pair + half] = weights
            context.append(dot(weights, values))
        context_ref[:, at : at + LANES] = jnp.where(low_lane, context[0], context[1]).astype(BRAIN)
    attended = dot(context_ref[...], merge_ref[...]) + wide(adjust_ref)
    normal, inverse = normalized(x.astype(FLOAT_KIND) + attended)
    normal_ref[...] = normal
    inverse_ref[...] = inverse
    low_ref[...] = (normal * wide(gain_ref) + wide(shift_ref)).astype(BRAIN)


def attend(enc, x, project, offsets, segments, merge, adjust, gain, shift):
    count, width = x.shape
    blocks = count // ROWS
    heads = width // HEAD
    return pl.pallas_call(
        attend_kernel,
        grid_spec=pltpu.PrefetchScalarGridSpec(
            num_scalar_prefetch=1,
            grid=(blocks,),
            in_specs=[
                row_block(ROWS, width),
                whole(project.shape),
                whole(offsets.shape),
                pl.BlockSpec((1, ROWS), lambda i, *_: (0, i)),
                whole(merge.shape),
                whole(adjust.shape),
                whole(gain.shape),
                whole(shift.shape),
            ],
            out_specs=[
                row_block(ROWS, 3 * width),
                pl.BlockSpec((None, heads, ROWS, ROWS), lambda i, *_: (i, 0, 0, 0)),
                row_block(ROWS, width),
                row_block(ROWS, width),
                row_block(ROWS, 1),
                row_block(ROWS, width),
            ],
        ),
        out_shape=[
            hbm_shape((count, 3 * width), BRAIN),
            hbm_shape((blocks, heads, ROWS, ROWS), BRAIN),
            hbm_shape((count, width), BRAIN),
            hbm_shape((count, width), FLOAT_KIND),
            hbm_shape((count, 1), FLOAT_KIND),
            jax.ShapeDtypeStruct((count, width), BRAIN),
        ],
        cost_estimate=cost(10 * count * width * width, 24 * count * width, count * ROWS * heads),
        compiler_params=pltpu.CompilerParams(vmem_limit_bytes=30 * MEGA),
        name="attend",
    )(enc, x, project, offsets, segments, merge, adjust, gain, shift)


def summary_kernel(
    flag_ref,
    start_ref,
    target_ref,
    normal_ref,
    gain_one_ref,
    shift_one_ref,
    expand_ref,
    lift_ref,
    shrink_ref,
    settle_ref,
    gain_two_ref,
    shift_two_ref,
    out_ref,
    tile_ref,
    row_ref,
    low_ref,
    total_ref,
    copy_sem,
):
    slots, width = row_ref.shape
    step = pl.program_id(0)

    @pl.when(step == 0)
    def _():
        copies = [
            pltpu.make_async_copy(
                normal_ref.at[jnp.where(flag_ref[ENC] == 1, start_ref[slot], slot * QLEN) // TILE],
                tile_ref.at[slot],
                copy_sem.at[slot],
            )
            for slot in range(slots)
        ]
        for copy in copies:
            copy.start()
        for copy in copies:
            copy.wait()
        rows = tile_ref[:, 0, :] * wide(gain_one_ref) + wide(shift_one_ref)
        row_ref[...] = rows
        low_ref[...] = rows.astype(BRAIN)
        total_ref[...] = jnp.zeros_like(total_ref)

    activated, _ = gelu_and_slope(dot(low_ref[...], expand_ref[...]) + wide(lift_ref))
    total_ref[...] += dot(activated.astype(BRAIN), shrink_ref[...])

    @pl.when(step == pl.num_programs(0) - 1)
    def _():
        normal, _ = normalized(row_ref[...] + (total_ref[...] + wide(settle_ref)))
        out_ref[:, :width] = (normal * wide(gain_two_ref) + wide(shift_two_ref)).astype(BRAIN)
        lane = lax.broadcasted_iota(jnp.int32, (slots, LANES), 1)
        place = lax.broadcasted_iota(jnp.int32, (slots, LANES), 0)
        digits = jnp.zeros((slots, LANES), jnp.int32)
        for slot in range(slots):
            target = target_ref[slot]
            pair = jnp.where(lane == 0, target // LANES, jnp.where(lane == 1, target % LANES, 0))
            digits = jnp.where(place == slot, pair, digits)
        out_ref[:, width:] = digits.astype(FLOAT_KIND).astype(BRAIN)


def summarize(enc, starts, targets, normal, first, expand, lift, shrink, settle, second, tn=512):
    count, width = normal.shape
    hidden = expand.shape[1]
    slots = starts.shape[0]
    row = whole((1, width))
    return pl.pallas_call(
        summary_kernel,
        grid_spec=pltpu.PrefetchScalarGridSpec(
            num_scalar_prefetch=3,
            grid=(hidden // tn,),
            in_specs=[
                pl.BlockSpec(memory_space=pl.ANY),
                row,
                row,
                pl.BlockSpec((width, tn), lambda i, *_: (0, i)),
                pl.BlockSpec((1, tn), lambda i, *_: (0, i)),
                pl.BlockSpec((tn, width), lambda i, *_: (i, 0)),
                row,
                row,
                row,
            ],
            out_specs=whole((slots, width + LANES)),
            scratch_shapes=[
                pltpu.VMEM((slots, TILE, width), FLOAT_KIND),
                pltpu.VMEM((slots, width), FLOAT_KIND),
                pltpu.VMEM((slots, width), BRAIN),
                pltpu.VMEM((slots, width), FLOAT_KIND),
                pltpu.SemaphoreType.DMA((slots,)),
            ],
        ),
        out_shape=jax.ShapeDtypeStruct((slots, width + LANES), BRAIN),
        cost_estimate=cost(4 * slots * width * hidden, 4 * width * hidden, slots * hidden),
        compiler_params=pltpu.CompilerParams(vmem_limit_bytes=16 * MEGA),
        name="summarize",
    )(
        enc,
        starts,
        targets,
        normal.reshape(count // TILE, TILE, width),
        *first,
        expand,
        lift,
        shrink,
        settle,
        *second,
    )


def widen_kernel(low_ref, expand_ref, lift_ref, *refs):
    active_ref, slope_ref = refs[-2:]
    hidden = dot(low_ref[...], expand_ref[...]) + wide(lift_ref)
    activated, slope = gelu_and_slope(hidden)
    active_ref[...] = activated.astype(BRAIN)
    slope_ref[...] = slope.astype(BRAIN)


def widen(part, parts, low, expand, lift, before, tn=384):
    count, width = low.shape
    hidden = expand.shape[1]
    steps = hidden // parts // tn
    column = lambda rows: pl.BlockSpec((rows, tn), lambda i: (0, part * steps + i))
    kept = [] if before is None else list(before)
    return pl.pallas_call(
        widen_kernel,
        grid=(steps,),
        in_specs=[whole(low.shape), column(width), column(1)]
        + [pl.BlockSpec(memory_space=pl.ANY)] * len(kept),
        out_specs=[column(count), column(count)],
        out_shape=[jax.ShapeDtypeStruct((count, hidden), BRAIN)] * 2,
        input_output_aliases={3 + k: k for k in range(len(kept))},
        cost_estimate=cost(
            2 * count * width * hidden // parts, 4 * count * hidden // parts, count * hidden // parts
        ),
        compiler_params=pltpu.CompilerParams(vmem_limit_bytes=12 * MEGA),
        name="widen",
    )(low, expand, lift, *kept)


def shrink_kernel(
    active_ref,
    shrink_ref,
    normal_ref,
    gain_one_ref,
    shift_one_ref,
    settle_ref,
    gain_two_ref,
    shift_two_ref,
    out_ref,
    inverse_ref,
    encoded_ref,
):
    normed = normal_ref[...] * wide(gain_one_ref) + wide(shift_one_ref)
    shrunk = dot(active_ref[...], shrink_ref[...]) + wide(settle_ref)
    normal, inverse = normalized(normed + shrunk)
    out_ref[...] = normal
    inverse_ref[...] = inverse
    encoded_ref[...] = (normal * wide(gain_two_ref) + wide(shift_two_ref)).astype(BRAIN)


def shrink_back_to_width(active, shrink, normal, first, settle, second, tm=256):
    count, hidden = active.shape
    width = shrink.shape[1]
    row = whole((1, width))
    return pl.pallas_call(
        shrink_kernel,
        grid=(count // tm,),
        in_specs=[row_block(tm, hidden), whole(shrink.shape), row_block(tm, width)] + [row] * 5,
        out_specs=[row_block(tm, width), row_block(tm, 1), row_block(tm, width)],
        out_shape=[
            jax.ShapeDtypeStruct((count, width), FLOAT_KIND),
            jax.ShapeDtypeStruct((count, 1), FLOAT_KIND),
            jax.ShapeDtypeStruct((count, width), BRAIN),
        ],
        cost_estimate=cost(2 * count * width * hidden, 2 * count * hidden + 10 * count * width),
        compiler_params=pltpu.CompilerParams(vmem_limit_bytes=28 * MEGA),
        name="shrink",
    )(active, shrink, normal, *first, settle, *second)


def contrast_kernel(
    flag_ref,
    start_ref,
    every_ref,
    column_ref,
    normal_ref,
    inverse_ref,
    cotangent_ref,
    gain_ref,
    two_ref,
    low_ref,
    sums_ref,
    summary_ref,
    rows_ref,
):
    width = normal_ref.shape[1]
    slots = start_ref.shape[0]
    devices = every_ref.shape[0]
    step = pl.program_id(0)
    sharpness = SHARPNESS_DIVISOR / math.sqrt(width)

    def flat(which, at, count):
        return every_ref[pl.ds(at, count), which].reshape(count * slots, width + LANES)

    def logits_of(questions, passages):
        return jnp.where(
            column_ref[...] >= 0, dot_rows(questions, passages) * sharpness, HIDDEN_SCORE
        )

    def targets_of(rows):
        digits = rows[:, width:].astype(FLOAT_KIND)
        return (digits[:, 0:1] * LANES + digits[:, 1:2]).astype(jnp.int32)

    @pl.when(step == 0)
    def _():
        sums_ref[...] = jnp.zeros_like(sums_ref)

        @pl.when(flag_ref[ENC] == 0)
        def _():
            own = every_ref[0, 0]
            passages = flat(1, 0, devices)[:, :width]
            logits = logits_of(own[:, :width], passages)
            top = jnp.max(logits, axis=1, keepdims=True)
            raised = jnp.exp(logits - top)
            probability = raised / jnp.sum(raised, axis=1, keepdims=True)
            hit = (column_ref[...] == targets_of(own)).astype(FLOAT_KIND)
            gradient = (LOSS_WEIGHT * (probability - hit)).astype(BRAIN)
            summary_ref[...] = dot(gradient, passages) * sharpness

        @pl.when(flag_ref[ENC] == 1)
        def _():
            passages = flat(0, 0, devices)[:, :width]
            block = 16

            def part(at):
                rows = flat(1, at, block)
                questions = rows[:, :width]
                logits = logits_of(questions, passages)
                top = jnp.max(logits, axis=1, keepdims=True)
                total = jnp.sum(jnp.exp(logits - top), axis=1, keepdims=True)
                probability = jnp.exp(logits[:, :LANES] - top) / total
                hit = (column_ref[:, :LANES] == targets_of(rows)).astype(FLOAT_KIND)
                gradient = (LOSS_WEIGHT * (probability - hit)).astype(BRAIN)
                return dot_columns(gradient, questions)[:slots] * sharpness

            if devices == block:
                summary_ref[...] = part(0)
            else:
                summary_ref[...] = jnp.zeros_like(summary_ref)

                @pl.loop(0, devices // block)
                def _(k):
                    summary_ref[...] += part(k * block)

    rows_ref[...] = wide(cotangent_ref)
    tiles = rows_ref.shape[0] // TILE
    first = lax.broadcasted_iota(jnp.int32, (TILE, 1), 0) == 0
    for slot in range(slots):
        start = jnp.where(flag_ref[ENC] == 1, start_ref[slot], slot * QLEN)
        local = start // TILE - step * tiles
        inside = (local >= 0) & (local < tiles)
        at = pl.multiple_of(jnp.clip(local, 0, tiles - 1) * TILE, TILE)
        rows_ref[pl.ds(at, TILE), :] += jnp.where(
            first & inside, summary_ref[slot : slot + 1, :], 0.0
        )
    gradient = rows_ref[...]
    normal = normal_ref[...]
    sums_ref[0:1] += row_sum(gradient * normal)
    sums_ref[1:2] += row_sum(gradient)
    two = norm_backward(gradient, normal, inverse_ref[...], wide(gain_ref))
    two_ref[...] = two
    low = two.astype(BRAIN)
    low_ref[...] = low
    sums_ref[2:3] += row_sum(low.astype(FLOAT_KIND))


def contrast(enc, starts, every, columns, normal, inverse, cotangent, gain, tm=256):
    count, width = normal.shape
    slots = starts.shape[0]
    return pl.pallas_call(
        contrast_kernel,
        grid_spec=pltpu.PrefetchScalarGridSpec(
            num_scalar_prefetch=2,
            grid=(count // tm,),
            in_specs=[
                whole(every.shape),
                whole(columns.shape),
                row_block(tm, width),
                row_block(tm, 1),
                row_block(tm, width),
                whole(gain.shape),
            ],
            out_specs=[row_block(tm, width), row_block(tm, width), whole((TILE, width))],
            scratch_shapes=[
                pltpu.VMEM((slots, width), FLOAT_KIND),
                pltpu.VMEM((tm, width), FLOAT_KIND),
            ],
        ),
        out_shape=[
            jax.ShapeDtypeStruct((count, width), FLOAT_KIND),
            jax.ShapeDtypeStruct((count, width), BRAIN),
            jax.ShapeDtypeStruct((TILE, width), FLOAT_KIND),
        ],
        cost_estimate=cost(2 * every.size * 256, 12 * count * width),
        compiler_params=pltpu.CompilerParams(vmem_limit_bytes=16 * MEGA),
        name="contrast",
    )(enc, starts, every, columns, normal, inverse, cotangent, gain)


def contraction_kernel(flag_ref, low_ref, active_ref, *refs):
    turned_ref = refs[-1]
    step = pl.program_id(0)

    @pl.when(step == 0)
    def _():
        turned_ref[...] = low_ref[...].T

    value = dot(turned_ref[...], active_ref[...]).astype(BRAIN)
    for piece, out_ref in enumerate(refs[:-1]):

        @pl.when(step == piece)
        def _():
            out_ref[...] = value


def contraction_half(flags, side, active, low):
    count, hidden = active.shape
    width = low.shape[1]
    rows = width // 2
    tn = hidden // PIECES
    return pl.pallas_call(
        contraction_kernel,
        grid_spec=pltpu.PrefetchScalarGridSpec(
            num_scalar_prefetch=1,
            grid=(PIECES,),
            in_specs=[
                pl.BlockSpec((count, rows), lambda i, flag: (0, flag[side])),
                pl.BlockSpec((count, tn), lambda i, flag: (0, i)),
            ],
            out_specs=[whole((rows, tn))] * PIECES,
            scratch_shapes=[pltpu.VMEM((rows, count), BRAIN)],
        ),
        out_shape=[jax.ShapeDtypeStruct((rows, tn), BRAIN)] * PIECES,
        cost_estimate=cost(count * width * hidden, count * hidden + 2 * count * width),
        compiler_params=pltpu.CompilerParams(vmem_limit_bytes=20 * MEGA),
        name="contraction_half",
    )(flags, low, active)


def feed_kernel(
    flag_ref,
    two_low_ref,
    shrink_ref,
    slope_ref,
    low_ref,
    expand_ref,
    two_ref,
    lift_ref,
    first_ref,
    *refs,
):
    pieces, turned_ref = refs[:-1], refs[-1]
    rows = turned_ref.shape[1]
    step = pl.program_id(0)

    @pl.when(step == 0)
    def _():
        first_ref[...] = two_ref[...]
        for side in range(2):

            @pl.when(flag_ref[SEND] == side)
            def _():
                turned_ref[0] = low_ref[:, side * rows : (side + 1) * rows].T
                turned_ref[1] = low_ref[:, (1 - side) * rows : (2 - side) * rows].T

    hidden = dot_rows(two_low_ref[...], shrink_ref[...]) * wide(slope_ref)
    low = hidden.astype(BRAIN)
    lift_ref[...] = row_sum(low.astype(FLOAT_KIND))
    first_ref[...] += dot_rows(low, expand_ref[...])
    for side in range(2):
        value = dot(turned_ref[side], low).astype(BRAIN)
        for piece in range(PIECES):

            @pl.when(step == piece)
            def _():
                pieces[side * PIECES + piece][...] = value


def feed_back(flags, two_low, shrink, slope, low, expand, two):
    count, width = two.shape
    hidden = shrink.shape[0]
    rows = width // 2
    tn = hidden // PIECES
    column = lambda rows: pl.BlockSpec((rows, tn), lambda i, *_: (0, i))
    return pl.pallas_call(
        feed_kernel,
        grid_spec=pltpu.PrefetchScalarGridSpec(
            num_scalar_prefetch=1,
            grid=(PIECES,),
            in_specs=[
                whole((count, width)),
                row_block(tn, width),
                column(count),
                whole((count, width)),
                column(width),
                whole((count, width)),
            ],
            out_specs=[column(1), whole((count, width))] + [whole((rows, tn))] * 2 * PIECES,
            scratch_shapes=[pltpu.VMEM((2, rows, count), BRAIN)],
        ),
        out_shape=[
            jax.ShapeDtypeStruct((1, hidden), FLOAT_KIND),
            jax.ShapeDtypeStruct((count, width), FLOAT_KIND),
        ]
        + [jax.ShapeDtypeStruct((rows, tn), BRAIN)] * 2 * PIECES,
        cost_estimate=cost(6 * count * width * hidden, 2 * count * hidden + 14 * count * width),
        compiler_params=pltpu.CompilerParams(vmem_limit_bytes=40 * MEGA),
        name="feed_back",
    )(flags, two_low, shrink, slope, low, expand, two)


def attend_back_kernel(
    first_ref,
    normal_ref,
    inverse_ref,
    gain_ref,
    merge_ref,
    packed_ref,
    weight_ref,
    context_ref,
    one_ref,
    low_ref,
    packed_gradient_ref,
    sums_ref,
    packed_sums_ref,
    context_gradient_ref,
):
    width = normal_ref.shape[1]

    @pl.when(pl.program_id(0) == 0)
    def _():
        sums_ref[...] = jnp.zeros_like(sums_ref)
        packed_sums_ref[...] = jnp.zeros_like(packed_sums_ref)

    gradient = first_ref[...]
    normal = normal_ref[...]
    sums_ref[0:1] += row_sum(gradient * normal)
    sums_ref[1:2] += row_sum(gradient)
    one = norm_backward(gradient, normal, inverse_ref[...], wide(gain_ref))
    one_ref[...] = one
    low = one.astype(BRAIN)
    low_ref[...] = low
    sums_ref[2:3] += row_sum(low.astype(FLOAT_KIND))
    context_gradient_ref[...] = dot_rows(low, merge_ref[...]).astype(BRAIN)
    low_lane = lax.broadcasted_iota(jnp.int32, (1, LANES), 1) < HEAD
    scale = 1.0 / math.sqrt(HEAD)
    for pair in range(width // LANES):
        at = LANES * pair
        queries = packed_ref[:, at : at + LANES] * scale
        keys = packed_ref[:, width + at : width + at + LANES] * scale
        values = packed_ref[:, 2 * width + at : 2 * width + at + LANES]
        outer = context_gradient_ref[:, at : at + LANES]
        products = outer.astype(FLOAT_KIND) * context_ref[:, at : at + LANES].astype(FLOAT_KIND)
        found = ([], [], [])
        for half in range(2):
            mine = low_lane if half == 0 else ~low_lane
            weights = weight_ref[2 * pair + half]
            own = jnp.where(mine, outer, jnp.zeros_like(outer))
            row_dots = jnp.sum(jnp.where(mine, products, 0.0), axis=1, keepdims=True)
            inner = dot_rows(own, values) - row_dots
            scores = (weights.astype(FLOAT_KIND) * inner).astype(BRAIN)
            found[0].append(dot(scores, keys))
            found[1].append(dot_columns(scores, queries))
            found[2].append(dot_columns(weights, outer))
        for part in range(3):
            packed_gradient_ref[:, part * width + at : part * width + at + LANES] = jnp.where(
                low_lane, found[part][0], found[part][1]
            ).astype(BRAIN)
    packed_sums_ref[...] += row_sum(wide(packed_gradient_ref))


def attend_back(first, normal, inverse, gain, merge, packed, weights, context):
    count, width = normal.shape
    heads = width // HEAD
    return pl.pallas_call(
        attend_back_kernel,
        grid=(count // ROWS,),
        in_specs=[
            row_block(ROWS, width),
            row_block(ROWS, width),
            row_block(ROWS, 1),
            whole(gain.shape),
            whole(merge.shape),
            row_block(ROWS, 3 * width),
            pl.BlockSpec((None, heads, ROWS, ROWS), lambda i: (i, 0, 0, 0)),
            row_block(ROWS, width),
        ],
        out_specs=[
            row_block(ROWS, width),
            row_block(ROWS, width),
            row_block(ROWS, 3 * width),
            whole((TILE, width)),
            whole((1, 3 * width)),
        ],
        out_shape=[
            jax.ShapeDtypeStruct((count, width), FLOAT_KIND),
            jax.ShapeDtypeStruct((count, width), BRAIN),
            jax.ShapeDtypeStruct((count, 3 * width), BRAIN),
            jax.ShapeDtypeStruct((TILE, width), FLOAT_KIND),
            jax.ShapeDtypeStruct((1, 3 * width), FLOAT_KIND),
        ],
        scratch_shapes=[pltpu.VMEM((ROWS, width), BRAIN)],
        cost_estimate=cost(12 * count * width * width, 38 * count * width),
        compiler_params=pltpu.CompilerParams(vmem_limit_bytes=30 * MEGA),
        name="attend_back",
    )(first, normal, inverse, gain, merge, packed, weights, context)


def merge_project_kernel(flag_ref, context_ref, one_ref, x_ref, packed_ref, *refs):
    pieces, turned_ref = refs[:-1], refs[-1]
    step = pl.program_id(0)

    @pl.when(step == 0)
    def _():
        turned_ref[...] = context_ref[...].T
        pieces[0][...] = dot(turned_ref[...], one_ref[...]).astype(BRAIN)
        turned_ref[...] = x_ref[...].T

    @pl.when(step > 0)
    def _():
        value = dot(turned_ref[...], packed_ref[...]).astype(BRAIN)
        for piece in range(1, PIECES):

            @pl.when(step == piece)
            def _():
                pieces[piece][...] = value


def merge_project_half(flags, side, context, one, x, packed):
    count, width = x.shape
    rows = width // 2
    return pl.pallas_call(
        merge_project_kernel,
        grid_spec=pltpu.PrefetchScalarGridSpec(
            num_scalar_prefetch=1,
            grid=(PIECES,),
            in_specs=[
                pl.BlockSpec((count, rows), lambda i, flag: (0, flag[side])),
                whole((count, width)),
                pl.BlockSpec((count, rows), lambda i, flag: (0, flag[side])),
                pl.BlockSpec((count, width), lambda i, flag: (0, jnp.maximum(i - 1, 0))),
            ],
            out_specs=[whole((rows, width))] * PIECES,
            scratch_shapes=[pltpu.VMEM((rows, count), BRAIN)],
        ),
        out_shape=[jax.ShapeDtypeStruct((rows, width), BRAIN)] * PIECES,
        cost_estimate=cost(4 * count * width * width, 10 * count * width),
        compiler_params=pltpu.CompilerParams(vmem_limit_bytes=24 * MEGA),
        name="merge_project_half",
    )(flags, context, one, x, packed)


def fold_kernel(flag_ref, *refs, count, side):
    keep, other, outs = refs[:count], refs[count : 2 * count], refs[2 * count :]
    rows = outs[0].shape[0]
    columns = outs[0].shape[1] // count
    for out_ref, half in zip(outs, (1 - flag_ref[side], flag_ref[side])):
        at = pl.multiple_of(half * rows, rows)
        for piece in range(count):
            total = keep[piece][pl.ds(at, rows), :].astype(FLOAT_KIND) + other[piece][
                pl.ds(at, rows), :
            ].astype(FLOAT_KIND)
            out_ref[:, piece * columns : (piece + 1) * columns] = total.astype(BRAIN)


def folded(flags, apart, keep, other):
    rows, columns = keep[0].shape
    count = len(keep)
    if rows % (2 * PACKED):
        (mine,), (theirs,) = keep, other
        bit = flags[SEND + apart]
        return part_sum(mine, theirs, 1 - bit), part_sum(mine, theirs, bit)
    shape = jax.ShapeDtypeStruct((rows // 2, count * columns), BRAIN)
    return pl.pallas_call(
        functools.partial(fold_kernel, count=count, side=SEND + apart),
        grid_spec=pltpu.PrefetchScalarGridSpec(
            num_scalar_prefetch=1,
            grid=(1,),
            in_specs=[whole((rows, columns))] * 2 * count,
            out_specs=[whole(shape.shape)] * 2,
        ),
        out_shape=[shape, shape],
        cost_estimate=cost(1, 1),
        compiler_params=pltpu.CompilerParams(vmem_limit_bytes=12 * MEGA),
        name="fold",
    )(flags, *keep, *other)


def add_kernel(mine_ref, other_ref, out_ref):
    out_ref[...] = (wide(mine_ref) + wide(other_ref)).astype(out_ref.dtype)


def added(mine, other):
    return pl.pallas_call(
        add_kernel,
        out_shape=jax.ShapeDtypeStruct(mine.shape, mine.dtype),
        cost_estimate=cost(1, 1),
        compiler_params=pltpu.CompilerParams(vmem_limit_bytes=4 * MEGA),
        name="add",
    )(mine, other)


def join_kernel(flag_ref, mine_ref, other_ref, out_ref, *, side):
    rows = mine_ref.shape[0]
    out_ref[pl.ds(pl.multiple_of(flag_ref[side] * rows, rows), rows), :] = mine_ref[...]
    out_ref[pl.ds(pl.multiple_of((1 - flag_ref[side]) * rows, rows), rows), :] = other_ref[...]


def joined(flags, apart, mine, other):
    rows, columns = mine.shape
    if rows % PACKED:
        return joined_by_bit(mine, other, flags[SEND + apart])
    return pl.pallas_call(
        functools.partial(join_kernel, side=SEND + apart),
        grid_spec=pltpu.PrefetchScalarGridSpec(
            num_scalar_prefetch=1,
            grid=(1,),
            in_specs=[whole(mine.shape)] * 2,
            out_specs=whole((2 * rows, columns)),
        ),
        out_shape=jax.ShapeDtypeStruct((2 * rows, columns), BRAIN),
        cost_estimate=cost(1, 1),
        compiler_params=pltpu.CompilerParams(vmem_limit_bytes=12 * MEGA),
        name="join",
    )(flags, mine, other)


def tokens_kernel(one_ref, packed_ref, project_ref, out_ref):
    out_ref[...] = one_ref[...] + dot_rows(packed_ref[...], project_ref[...])


def tokens_back(one, packed, project, tm=256):
    count, width = one.shape
    return pl.pallas_call(
        tokens_kernel,
        grid=(count // tm,),
        in_specs=[row_block(tm, width), row_block(tm, 3 * width), whole(project.shape)],
        out_specs=row_block(tm, width),
        out_shape=jax.ShapeDtypeStruct((count, width), FLOAT_KIND),
        cost_estimate=cost(6 * count * width * width, 14 * count * width),
        compiler_params=pltpu.CompilerParams(vmem_limit_bytes=22 * MEGA),
        name="tokens_back",
    )(one, packed, project)


def pack_kernel(packed_ref, attend_ref, lift_ref, output_ref, out_ref):
    width = attend_ref.shape[1]
    out_ref[...] = jnp.zeros_like(out_ref)
    out_ref[0:1] = packed_ref[:, :width]
    out_ref[1:2] = packed_ref[:, 2 * width :]
    out_ref[2:5] = attend_ref[0:3]
    for part in range(4):
        out_ref[5 + part : 6 + part] = lift_ref[:, part * width : (part + 1) * width]
    out_ref[9:12] = output_ref[0:3]


def pack_vectors(packed_sums, attend_sums, lift_sums, output_sums):
    width = attend_sums.shape[1]
    return pl.pallas_call(
        pack_kernel,
        out_shape=jax.ShapeDtypeStruct((16, width), FLOAT_KIND),
        cost_estimate=cost(1, 1),
        compiler_params=pltpu.CompilerParams(vmem_limit_bytes=4 * MEGA),
        name="pack_vectors",
    )(packed_sums, attend_sums, lift_sums, output_sums)


def unpack_kernel(mine_ref, other_ref, offset_ref, adjust_ref, scale_ref, center_ref, lift_ref, settle_ref, rescale_ref, recenter_ref):
    width = mine_ref.shape[1]
    total = mine_ref[...] + other_ref[...]
    offset_ref[:, :width] = total[0:1]
    offset_ref[:, width:] = total[1:2]
    scale_ref[...] = total[2:3]
    center_ref[...] = total[3:4]
    adjust_ref[...] = total[4:5]
    for part in range(4):
        lift_ref[:, part * width : (part + 1) * width] = total[5 + part : 6 + part]
    rescale_ref[...] = total[9:10]
    recenter_ref[...] = total[10:11]
    settle_ref[...] = total[11:12]


def unpack_vectors(mine, other):
    width = mine.shape[1]
    shapes = [2, 1, 1, 1, 4, 1, 1, 1]
    return pl.pallas_call(
        unpack_kernel,
        out_shape=[jax.ShapeDtypeStruct((1, k * width), FLOAT_KIND) for k in shapes],
        cost_estimate=cost(1, 1),
        compiler_params=pltpu.CompilerParams(vmem_limit_bytes=4 * MEGA),
        name="unpack_vectors",
    )(mine, other)


def place_kernel(flag_ref, value_ref, *refs, kept):
    at = 0
    for out_ref in refs[kept:]:
        columns = out_ref.shape[1]
        out_ref[...] = value_ref[:, at : at + columns].astype(FLOAT_KIND)
        at += columns


def place_half(flags, side, value, columns, before, tm=192):
    rows = value.shape[0]
    steps = rows // tm
    kept = [] if before is None else list(before)
    return pl.pallas_call(
        functools.partial(place_kernel, kept=len(kept)),
        grid_spec=pltpu.PrefetchScalarGridSpec(
            num_scalar_prefetch=1,
            grid=(steps,),
            in_specs=[row_block(tm, value.shape[1])]
            + [pl.BlockSpec(memory_space=pl.ANY)] * len(kept),
            out_specs=[
                pl.BlockSpec((tm, size), lambda i, flag: (flag[side] * steps + i, 0))
                for size in columns
            ],
        ),
        out_shape=[jax.ShapeDtypeStruct((2 * rows, size), FLOAT_KIND) for size in columns],
        input_output_aliases={2 + k: k for k in range(len(kept))},
        cost_estimate=cost(1, 1),
        compiler_params=pltpu.CompilerParams(vmem_limit_bytes=20 * MEGA),
        name="place_half",
    )(flags, value, *kept)


def place_turned_kernel(flag_ref, value_ref, *refs):
    refs[-1][...] = value_ref[...].astype(FLOAT_KIND).T


def place_turned_half(flags, side, value, before, tm=1536):
    rows, columns = value.shape
    kept = [] if before is None else list(before)
    return pl.pallas_call(
        place_turned_kernel,
        grid_spec=pltpu.PrefetchScalarGridSpec(
            num_scalar_prefetch=1,
            grid=(columns // tm,),
            in_specs=[pl.BlockSpec((rows, tm), lambda i, flag: (0, i))]
            + [pl.BlockSpec(memory_space=pl.ANY)] * len(kept),
            out_specs=[pl.BlockSpec((tm, rows), lambda i, flag: (i, flag[side]))],
        ),
        out_shape=[jax.ShapeDtypeStruct((columns, 2 * rows), FLOAT_KIND)],
        input_output_aliases={2 + k: k for k in range(len(kept))},
        cost_estimate=cost(1, 1),
        compiler_params=pltpu.CompilerParams(vmem_limit_bytes=20 * MEGA),
        name="place_turned_half",
    )(flags, value, *kept)


def swapped(value, axis, apart):
    mask = 2**apart
    pairs = [(source, source ^ mask) for source in range(lax.axis_size(axis))]
    return lax.ppermute(value, axis, pairs)


def bit_count(axis):
    return lax.axis_size(axis).bit_length() - 1


def to_low(values):
    return values.astype(BRAIN)


def part_sum(mine, other, bit):
    half = mine.shape[0] // 2
    left = lax.dynamic_slice_in_dim(mine, bit * half, half, 0).astype(FLOAT_KIND)
    right = lax.dynamic_slice_in_dim(other, bit * half, half, 0).astype(FLOAT_KIND)
    return to_low(left + right)


def joined_by_bit(mine, other, bit):
    low_part = jnp.where(bit == 0, mine, other)
    high_part = jnp.where(bit == 0, other, mine)
    return jnp.concatenate([low_part, high_part], axis=0)


class Sequence:
    def __init__(self):
        self.last = None

    def run(self, step, *inputs):
        if self.last is not None:
            *inputs, _ = lax.optimization_barrier((*inputs, self.last))
        result = step(*inputs)
        self.last = jax.tree.leaves(result)[0]
        return result


class Reduction:
    def __init__(self, sequence, flags, put):
        self.run = sequence.run
        self.flags = flags
        self.put = put
        bits = bit_count("batch")
        self.steps = [lambda k=k: self.scatter(k) for k in range(1, bits)]
        self.steps.append(self.finish)
        self.steps += [lambda k=k: self.gather(k) for k in reversed(range(1, bits))]
        self.steps.append(self.place)

    def advance(self):
        self.steps.pop(0)()

    def begin(self, send, keep):
        self.keep = list(keep)
        self.other = [swapped(piece, "batch", 0) for piece in send]

    def scatter(self, apart):
        count = len(self.keep)
        send, keep = self.run(
            lambda *v: folded(self.flags, apart, v[:count], v[count:]), *self.keep, *self.other
        )
        self.keep = [keep]
        self.other = [swapped(send, "batch", apart)]

    def finish(self):
        self.value = self.run(added, *self.keep, *self.other)
        self.other = swapped(self.value, "batch", bit_count("batch") - 1)

    def gather(self, apart):
        self.value = self.run(
            lambda v, o: joined(self.flags, apart, v, o), self.value, self.other
        )
        self.other = swapped(self.value, "batch", apart - 1)
        if apart == 1:
            self.placed = self.run(lambda v: self.put(self.flags, KEEP, v, None), self.value)

    def place(self):
        self.total = self.run(
            lambda o, *p: self.put(self.flags, SEND, o, p), self.other, *self.placed
        )


def shards(
    tokens,
    cotangent,
    projection,
    offsets,
    merger,
    adjust,
    scaling,
    centering,
    expansion,
    lifting,
    contraction,
    settling,
    rescale,
    recenter,
    segments,
    passage_starts,
    passage_counts,
    positives,
):
    index = lax.axis_index("batch").astype(jnp.int32)
    slots = passage_starts.shape[0]
    bits = bit_count("batch")
    flags = jnp.stack(
        [lax.axis_index("enc").astype(jnp.int32), index & 1, 1 - (index & 1)]
        + [(index >> apart) & 1 for apart in range(1, bits)]
    )
    order = list(reversed(range(bits)))
    place = jnp.arange(lax.axis_size("batch"), dtype=jnp.int32)
    away = sum(((place >> k) & 1) << apart for k, apart in enumerate(order))
    device = (index ^ away)[:, None]
    slot = jnp.arange(slots, dtype=jnp.int32)[None, :]
    held = jnp.sum(jnp.where(device == place[None, :], passage_counts[None, :], 0), axis=1)
    columns = jnp.where(slot < held[:, None], device * slots + slot, -1).reshape(1, -1)
    flags, columns, tokens = lax.optimization_barrier((flags, columns, tokens))
    width = tokens.shape[2]
    x, project, merge, expand, shrink, outer = (
        in_hbm(v[0]) for v in (tokens, projection, merger, expansion, contraction, cotangent)
    )
    first = (in_hbm(scaling), in_hbm(centering))
    second = (in_hbm(rescale), in_hbm(recenter))
    adjust, lifting, settling, offsets = (
        in_hbm(v) for v in (adjust, lifting, settling, offsets)
    )

    sequence = Sequence()
    run = sequence.run
    packed, weights, context, normal_one, inverse_one, low = attend(
        flags, x, project, offsets, in_hbm(segments[None]), merge, adjust, *first
    )
    parcel = summarize(
        flags,
        passage_starts,
        positives,
        normal_one,
        first,
        expand,
        lifting,
        shrink,
        settling,
        second,
    )
    sequence.last = parcel
    parts = 4
    every = parcel[None]
    other = swapped(parcel, "enc", 0)[None]
    wide_pair = run(lambda v: widen(0, parts, v, expand, lifting, None), low)
    every = run(lambda a, b: jnp.stack([a, b], axis=1), every, other)
    for part, apart in enumerate(order, 1):
        other = swapped(every, "batch", apart)
        if part < parts:
            wide_pair = run(
                lambda v, *p: widen(part, parts, v, expand, lifting, p), low, *wide_pair
            )
        elif part == parts:
            active, slope = wide_pair
            normal_two, inverse_two, encoded = run(
                lambda a, n: shrink_back_to_width(a, shrink, n, first, settling, second),
                active,
                normal_one,
            )
        every = run(lambda a, b: jnp.concatenate([a, b], axis=0), every, other)
    two, two_low, output_sums = run(
        lambda *v: contrast(flags, passage_starts, *v, outer, second[0]),
        every,
        columns,
        normal_two,
        inverse_two,
    )

    shrink_sum = Reduction(sequence, flags, place_turned_half)
    expand_sum = Reduction(
        sequence, flags, lambda f, s, v, p: place_half(f, s, v, (expansion.shape[2],), p)
    )
    project_sum = Reduction(
        sequence, flags, lambda f, s, v, p: place_half(f, s, v, (width, projection.shape[2]), p)
    )
    send = run(lambda a, t: contraction_half(flags, SEND, a, t), active, two_low)
    keep = run(lambda a, t: contraction_half(flags, KEEP, a, t), active, two_low)
    shrink_sum.begin(send, keep)
    shrink_sum.advance()
    lift_sums, gradient_first, *both = run(
        lambda t, s, g: feed_back(flags, t, shrink, s, low, expand, g),
        two_low,
        slope,
        two,
    )
    expand_sum.begin(both[:PIECES], both[PIECES:])
    expand_sum.advance()
    shrink_sum.advance()
    one, one_low, packed_gradient, attend_sums, packed_sums = run(
        lambda g, n, i, p, w, c: attend_back(g, n, i, first[0], merge, p, w, c),
        gradient_first,
        normal_one,
        inverse_one,
        packed,
        weights,
        context,
    )
    shrink_sum.advance()
    product = lambda side: run(
        lambda c, o, p: merge_project_half(flags, side, c, o, x, p),
        context,
        one_low,
        packed_gradient,
    )
    send = product(SEND)
    expand_sum.advance()
    keep = product(KEEP)
    project_sum.begin(send, keep)
    project_sum.advance()
    shrink_sum.advance()
    expand_sum.advance()
    tokens_gradient = run(lambda o, p: tokens_back(o, p, project), one, packed_gradient)
    shrink_sum.advance()
    expand_sum.advance()
    vectors = [run(pack_vectors, packed_sums, attend_sums, lift_sums, output_sums)]
    vectors.append(swapped(vectors[0], "batch", 0))

    def vectors_advance(apart):
        vectors[0] = run(added, *vectors)
        vectors[1] = swapped(vectors[0], "batch", apart)

    project_sum.advance()
    shrink_sum.advance()
    expand_sum.advance()
    vectors_advance(1)
    project_sum.advance()
    expand_sum.advance()
    for apart in range(2, bits - 1):
        vectors_advance(apart)
    project_sum.advance()
    shrink_sum.advance()
    project_sum.advance()
    vectors_advance(bits - 1)
    shrink_sum.advance()
    project_sum.advance()
    expand_sum.advance()
    vector_totals = run(unpack_vectors, *vectors)
    for reduction in (shrink_sum, expand_sum, project_sum):
        while reduction.steps:
            reduction.advance()
    (total_contraction,) = shrink_sum.total
    (total_expansion,) = expand_sum.total
    total_merger, total_projection = project_sum.total
    (
        total_offsets,
        total_adjust,
        total_scaling,
        total_centering,
        total_lifting,
        total_settling,
        total_rescale,
        total_recenter,
    ) = vector_totals
    return (
        encoded[None],
        tokens_gradient[None],
        total_projection[None],
        total_offsets,
        total_merger[None],
        total_adjust,
        total_scaling,
        total_centering,
        total_expansion[None],
        total_lifting,
        total_contraction[None],
        total_settling,
        total_rescale,
        total_recenter,
    )


def solution(mesh):
    matrix = P("enc", None, None)
    vector = P("enc", None)
    rows = P("enc", "batch", None)
    return jax.shard_map(
        shards,
        mesh=mesh,
        in_specs=(
            rows,
            rows,
            matrix,
            vector,
            matrix,
            vector,
            vector,
            vector,
            matrix,
            vector,
            matrix,
            vector,
            vector,
            vector,
            P("batch"),
            P("batch"),
            P(),
            P("batch"),
        ),
        out_specs=(
            rows,
            rows,
            matrix,
            vector,
            matrix,
            vector,
            vector,
            vector,
            matrix,
            vector,
            matrix,
            vector,
            vector,
            vector,
        ),
        check_vma=False,
    )
```

```python
import functools
import math

import jax
import jax.numpy as jnp
from jax import lax
from jax.experimental import pallas as pl
from jax.experimental.pallas import tpu as pltpu
from jax.sharding import PartitionSpec as P

QLEN = 64
ROWS = 256
HEAD = 64
TILE = 8
LANES = 128
PIECES = 4
PACKED = 16
PLAN = (
    "C4", "c", "F2", "c", "e4", "A2", "c", "S3", "e3", "c2", "P", "K3",
    "m1", "e3", "T", "v", "c3", "e2", "m3", "c3", "m1", "e", "m1", "c1",
    "m3", "e", "v1", "m1", "c", "e", "v", "m", "e2", "m4",
)
LINKS = (2, 2, 2)
LEVELS = (1, 2 * 10**9, 6 * 10**9, 2 * 10**10, 10**11)
ENC, KEEP, SEND, STAGES = 0, 1, 2, 3
MEGA = 2**20
EPSILON = 1e-12
SHARPNESS_DIVISOR = 2.0
LOSS_WEIGHT = 2.0
HIDDEN_SCORE = -1e30
FLOAT_KIND = jnp.float32
BRAIN = jnp.bfloat16

TAIL = tuple(
    0.5 * a for a in (0.254829592, -0.284496736, 1.421413741, -1.453152027, 1.061405429)
)
TAIL_SLOPE = 0.3275911 / math.sqrt(2.0)
DENSITY = 1.0 / math.sqrt(2.0 * math.pi)


def dot(left, right):
    return jnp.dot(left, right, preferred_element_type=FLOAT_KIND)


def dot_rows(left, right):
    return lax.dot_general(left, right, (((1,), (1,)), ((), ())), preferred_element_type=FLOAT_KIND)


def dot_columns(left, right):
    return lax.dot_general(left, right, (((0,), (0,)), ((), ())), preferred_element_type=FLOAT_KIND)


def whole(shape):
    return pl.BlockSpec(shape, lambda *_: (0,) * len(shape))


def row_block(rows, columns):
    return pl.BlockSpec((rows, columns), lambda i, *_: (i, 0))


def in_hbm(value):
    return pltpu.with_memory_space_constraint(value, pltpu.HBM)


def hbm_shape(shape, dtype):
    return pltpu.HBM(shape, dtype)


def cost(flops, moved, transcendentals=0):
    return pl.CostEstimate(flops=flops, bytes_accessed=1, transcendentals=0)


def wide(ref):
    return ref[...].astype(FLOAT_KIND)


def row_sum(values):
    return jnp.sum(values, axis=0, keepdims=True)


def normalized(values):
    centered = values - jnp.mean(values, axis=1, keepdims=True)
    spread = jnp.mean(centered * centered, axis=1, keepdims=True)
    scale = lax.rsqrt(spread + EPSILON)
    return centered * scale, scale


def norm_backward(gradient, normal, inverse, gain):
    scaled = gradient * gain
    return (
        scaled
        - jnp.mean(scaled, axis=1, keepdims=True)
        - normal * jnp.mean(scaled * normal, axis=1, keepdims=True)
    ) * inverse


def both_heads(values):
    low_lane = lax.broadcasted_iota(jnp.int32, (1, LANES), 1) < HEAD
    nothing = jnp.zeros_like(values)
    return jnp.concatenate(
        [jnp.where(low_lane, values, nothing), jnp.where(low_lane, nothing, values)], axis=0
    )


def gelu_and_slope(hidden):
    bell = jnp.exp(hidden * hidden * -0.5)
    t = 1.0 / (1.0 + TAIL_SLOPE * jnp.abs(hidden))
    series = TAIL[3] + t * TAIL[4]
    series = TAIL[2] + t * series
    series = TAIL[1] + t * series
    series = TAIL[0] + t * series
    tail = t * series * bell
    below = jnp.where(hidden < 0.0, tail, 1.0 - tail)
    return hidden * below, below + hidden * bell * DENSITY


def attend_kernel(
    flag_ref,
    x_ref,
    project_ref,
    offset_ref,
    segment_ref,
    merge_ref,
    adjust_ref,
    gain_ref,
    shift_ref,
    packed_ref,
    weight_ref,
    context_ref,
    normal_ref,
    inverse_ref,
    low_ref,
):
    width = x_ref.shape[1]
    x = x_ref[...]
    for part in range(3):
        columns = slice(part * width, (part + 1) * width)
        sums = dot(x, project_ref[:, columns])
        if part != 1:
            at = 0 if part == 0 else width
            sums = sums + offset_ref[:, at : at + width].astype(FLOAT_KIND)
        packed_ref[:, columns] = sums.astype(BRAIN)
    position = lax.broadcasted_iota(jnp.int32, (1, ROWS), 1)
    marks = jnp.where(flag_ref[ENC] == 1, segment_ref[...], position // QLEN).astype(FLOAT_KIND)
    spread_marks = jnp.broadcast_to(marks, (ROWS, ROWS))
    hide = jnp.where(spread_marks == spread_marks.T, 0.0, HIDDEN_SCORE)
    hide = jnp.concatenate([hide, hide], axis=0)
    low_lane = lax.broadcasted_iota(jnp.int32, (1, LANES), 1) < HEAD
    scale = 1.0 / math.sqrt(HEAD)
    for pair in range(width // LANES):
        at = LANES * pair
        queries = both_heads(packed_ref[:, at : at + LANES] * scale)
        keys = packed_ref[:, width + at : width + at + LANES]
        values = packed_ref[:, 2 * width + at : 2 * width + at + LANES]
        scores = dot_rows(queries, keys) + hide
        raised = jnp.exp(scores - jnp.max(scores, axis=1, keepdims=True))
        weights = (raised * (1.0 / jnp.sum(raised, axis=1, keepdims=True))).astype(BRAIN)
        weight_ref[pair] = weights.T
        context = dot(weights, values)
        context = jnp.where(low_lane, context[:ROWS], context[ROWS:])
        context_ref[:, at : at + LANES] = context.astype(BRAIN)
    attended = dot(context_ref[...], merge_ref[...]) + wide(adjust_ref)
    normal, inverse = normalized(x.astype(FLOAT_KIND) + attended)
    normal_ref[...] = normal
    inverse_ref[...] = inverse
    low_ref[...] = (normal * wide(gain_ref) + wide(shift_ref)).astype(BRAIN)


def attend(enc, x, project, offsets, segments, merge, adjust, gain, shift):
    count, width = x.shape
    blocks = count // ROWS
    heads = width // HEAD
    return pl.pallas_call(
        attend_kernel,
        grid_spec=pltpu.PrefetchScalarGridSpec(
            num_scalar_prefetch=1,
            grid=(blocks,),
            in_specs=[
                row_block(ROWS, width),
                whole(project.shape),
                whole(offsets.shape),
                pl.BlockSpec((1, ROWS), lambda i, *_: (0, i)),
                whole(merge.shape),
                whole(adjust.shape),
                whole(gain.shape),
                whole(shift.shape),
            ],
            out_specs=[
                row_block(ROWS, 3 * width),
                pl.BlockSpec((None, heads // 2, ROWS, 2 * ROWS), lambda i, *_: (i, 0, 0, 0)),
                row_block(ROWS, width),
                row_block(ROWS, width),
                row_block(ROWS, 1),
                row_block(ROWS, width),
            ],
        ),
        out_shape=[
            jax.ShapeDtypeStruct((count, 3 * width), BRAIN),
            jax.ShapeDtypeStruct((blocks, heads // 2, ROWS, 2 * ROWS), BRAIN),
            jax.ShapeDtypeStruct((count, width), BRAIN),
            jax.ShapeDtypeStruct((count, width), FLOAT_KIND),
            jax.ShapeDtypeStruct((count, 1), FLOAT_KIND),
            jax.ShapeDtypeStruct((count, width), BRAIN),
        ],
        cost_estimate=cost(1, 1),
        compiler_params=pltpu.CompilerParams(vmem_limit_bytes=17 * MEGA),
        name="attend",
    )(enc, x, project, offsets, segments, merge, adjust, gain, shift)


def summary_kernel(
    flag_ref,
    start_ref,
    target_ref,
    normal_ref,
    gain_one_ref,
    shift_one_ref,
    expand_ref,
    lift_ref,
    shrink_ref,
    settle_ref,
    gain_two_ref,
    shift_two_ref,
    out_ref,
    tile_ref,
    row_ref,
    low_ref,
    total_ref,
    copy_sem,
):
    slots, width = row_ref.shape
    step = pl.program_id(0)

    @pl.when(step == 0)
    def _():
        copies = [
            pltpu.make_async_copy(
                normal_ref.at[jnp.where(flag_ref[ENC] == 1, start_ref[slot], slot * QLEN) // TILE],
                tile_ref.at[slot],
                copy_sem.at[slot],
            )
            for slot in range(slots)
        ]
        for copy in copies:
            copy.start()
        for copy in copies:
            copy.wait()
        rows = tile_ref[:, 0, :] * wide(gain_one_ref) + wide(shift_one_ref)
        row_ref[...] = rows
        low_ref[...] = rows.astype(BRAIN)
        total_ref[...] = jnp.zeros_like(total_ref)

    activated, _ = gelu_and_slope(dot(low_ref[...], expand_ref[...]) + wide(lift_ref))
    total_ref[...] += dot(activated.astype(BRAIN), shrink_ref[...])

    @pl.when(step == pl.num_programs(0) - 1)
    def _():
        normal, _ = normalized(row_ref[...] + (total_ref[...] + wide(settle_ref)))
        out_ref[:, :width] = (normal * wide(gain_two_ref) + wide(shift_two_ref)).astype(BRAIN)
        lane = lax.broadcasted_iota(jnp.int32, (slots, LANES), 1)
        place = lax.broadcasted_iota(jnp.int32, (slots, LANES), 0)
        digits = jnp.zeros((slots, LANES), jnp.int32)
        for slot in range(slots):
            target = target_ref[slot]
            pair = jnp.where(lane == 0, target // LANES, jnp.where(lane == 1, target % LANES, 0))
            digits = jnp.where(place == slot, pair, digits)
        out_ref[:, width:] = digits.astype(FLOAT_KIND).astype(BRAIN)


def summarize(enc, starts, targets, normal, first, expand, lift, shrink, settle, second, tn=1024):
    count, width = normal.shape
    hidden = expand.shape[1]
    slots = starts.shape[0]
    row = whole((1, width))
    return pl.pallas_call(
        summary_kernel,
        grid_spec=pltpu.PrefetchScalarGridSpec(
            num_scalar_prefetch=3,
            grid=(hidden // tn,),
            in_specs=[
                pl.BlockSpec(memory_space=pl.ANY),
                row,
                row,
                pl.BlockSpec((width, tn), lambda i, *_: (0, i)),
                pl.BlockSpec((1, tn), lambda i, *_: (0, i)),
                pl.BlockSpec((tn, width), lambda i, *_: (i, 0)),
                row,
                row,
                row,
            ],
            out_specs=whole((slots, width + LANES)),
            scratch_shapes=[
                pltpu.VMEM((slots, TILE, width), FLOAT_KIND),
                pltpu.VMEM((slots, width), FLOAT_KIND),
                pltpu.VMEM((slots, width), BRAIN),
                pltpu.VMEM((slots, width), FLOAT_KIND),
                pltpu.SemaphoreType.DMA((slots,)),
            ],
        ),
        out_shape=jax.ShapeDtypeStruct((slots, width + LANES), BRAIN),
        cost_estimate=cost(1, 1),
        compiler_params=pltpu.CompilerParams(vmem_limit_bytes=10 * MEGA),
        name="summarize",
    )(
        enc,
        starts,
        targets,
        normal.reshape(count // TILE, TILE, width),
        *first,
        expand,
        lift,
        shrink,
        settle,
        *second,
    )


def widen_kernel(low_ref, expand_ref, lift_ref, *refs):
    active_ref, slope_ref = refs[-2:]

    @pl.loop(0, low_ref.shape[0] // ROWS)
    def _(block):
        rows = pl.ds(pl.multiple_of(block * ROWS, ROWS), ROWS)
        hidden = dot(low_ref[rows, :], expand_ref[...]) + wide(lift_ref)
        activated, slope = gelu_and_slope(hidden)
        active_ref[rows, :] = activated.astype(BRAIN)
        slope_ref[rows, :] = slope.astype(BRAIN)


def widen(part, parts, low, expand, lift, before, tn=768):
    count, width = low.shape
    hidden = expand.shape[1]
    steps = hidden // parts // tn
    column = lambda rows: pl.BlockSpec((rows, tn), lambda i: (0, part * steps + i))
    kept = [] if before is None else list(before)
    return pl.pallas_call(
        widen_kernel,
        grid=(steps,),
        in_specs=[whole(low.shape), column(width), column(1)]
        + [pl.BlockSpec(memory_space=pl.ANY)] * len(kept),
        out_specs=[column(count), column(count)],
        out_shape=[jax.ShapeDtypeStruct((count, hidden), BRAIN)] * 2,
        input_output_aliases={3 + k: k for k in range(len(kept))},
        cost_estimate=cost(1, 1),
        compiler_params=pltpu.CompilerParams(vmem_limit_bytes=10 * MEGA),
        name="widen",
    )(low, expand, lift, *kept)


def shrink_kernel(
    active_ref,
    shrink_ref,
    normal_ref,
    gain_one_ref,
    shift_one_ref,
    settle_ref,
    gain_two_ref,
    shift_two_ref,
    out_ref,
    inverse_ref,
    encoded_ref,
):
    normed = normal_ref[...] * wide(gain_one_ref) + wide(shift_one_ref)
    shrunk = dot(active_ref[...], shrink_ref[...]) + wide(settle_ref)
    normal, inverse = normalized(normed + shrunk)
    out_ref[...] = normal
    inverse_ref[...] = inverse
    encoded_ref[...] = (normal * wide(gain_two_ref) + wide(shift_two_ref)).astype(BRAIN)


def shrink_back_to_width(active, shrink, normal, first, settle, second, tm=256):
    count, hidden = active.shape
    width = shrink.shape[1]
    row = whole((1, width))
    return pl.pallas_call(
        shrink_kernel,
        grid=(count // tm,),
        in_specs=[row_block(tm, hidden), whole(shrink.shape), row_block(tm, width)] + [row] * 5,
        out_specs=[row_block(tm, width), row_block(tm, 1), row_block(tm, width)],
        out_shape=[
            jax.ShapeDtypeStruct((count, width), FLOAT_KIND),
            jax.ShapeDtypeStruct((count, 1), FLOAT_KIND),
            jax.ShapeDtypeStruct((count, width), BRAIN),
        ],
        cost_estimate=cost(1, 1),
        compiler_params=pltpu.CompilerParams(vmem_limit_bytes=14 * MEGA),
        name="shrink",
    )(active, shrink, normal, *first, settle, *second)


def contrast_kernel(
    flag_ref,
    start_ref,
    every_ref,
    column_ref,
    normal_ref,
    inverse_ref,
    cotangent_ref,
    gain_ref,
    two_ref,
    low_ref,
    sums_ref,
    summary_ref,
    rows_ref,
):
    width = normal_ref.shape[1]
    slots = start_ref.shape[0]
    devices = every_ref.shape[0]
    step = pl.program_id(0)
    sharpness = SHARPNESS_DIVISOR / math.sqrt(width)

    def flat(which, at, count):
        return every_ref[pl.ds(at, count), which].reshape(count * slots, width + LANES)

    def logits_of(questions, passages):
        return jnp.where(
            column_ref[...] >= 0, dot_rows(questions, passages) * sharpness, HIDDEN_SCORE
        )

    def targets_of(rows):
        digits = rows[:, width:].astype(FLOAT_KIND)
        return (digits[:, 0:1] * LANES + digits[:, 1:2]).astype(jnp.int32)

    @pl.when(step == 0)
    def _():
        sums_ref[...] = jnp.zeros_like(sums_ref)

        @pl.when(flag_ref[ENC] == 0)
        def _():
            own = every_ref[0, 0]
            passages = flat(1, 0, devices)[:, :width]
            logits = logits_of(own[:, :width], passages)
            top = jnp.max(logits, axis=1, keepdims=True)
            raised = jnp.exp(logits - top)
            probability = raised / jnp.sum(raised, axis=1, keepdims=True)
            hit = (column_ref[...] == targets_of(own)).astype(FLOAT_KIND)
            gradient = (LOSS_WEIGHT * (probability - hit)).astype(BRAIN)
            summary_ref[...] = dot(gradient, passages) * sharpness

        @pl.when(flag_ref[ENC] == 1)
        def _():
            passages = flat(0, 0, devices)[:, :width]
            block = 16

            def part(at):
                rows = flat(1, at, block)
                questions = rows[:, :width]
                logits = logits_of(questions, passages)
                top = jnp.max(logits, axis=1, keepdims=True)
                total = jnp.sum(jnp.exp(logits - top), axis=1, keepdims=True)
                probability = jnp.exp(logits[:, :LANES] - top) / total
                hit = (column_ref[:, :LANES] == targets_of(rows)).astype(FLOAT_KIND)
                gradient = (LOSS_WEIGHT * (probability - hit)).astype(BRAIN)
                return dot_columns(gradient, questions)[:slots] * sharpness

            if devices == block:
                summary_ref[...] = part(0)
            else:
                summary_ref[...] = jnp.zeros_like(summary_ref)

                @pl.loop(0, devices // block)
                def _(k):
                    summary_ref[...] += part(k * block)

    rows_ref[...] = wide(cotangent_ref)
    tiles = rows_ref.shape[0] // TILE
    first = lax.broadcasted_iota(jnp.int32, (TILE, 1), 0) == 0
    for slot in range(slots):
        start = jnp.where(flag_ref[ENC] == 1, start_ref[slot], slot * QLEN)
        local = start // TILE - step * tiles
        inside = (local >= 0) & (local < tiles)
        at = pl.multiple_of(jnp.clip(local, 0, tiles - 1) * TILE, TILE)
        rows_ref[pl.ds(at, TILE), :] += jnp.where(
            first & inside, summary_ref[slot : slot + 1, :], 0.0
        )
    gradient = rows_ref[...]
    normal = normal_ref[...]
    sums_ref[0:1] += row_sum(gradient * normal)
    sums_ref[1:2] += row_sum(gradient)
    two = norm_backward(gradient, normal, inverse_ref[...], wide(gain_ref))
    two_ref[...] = two
    low = two.astype(BRAIN)
    low_ref[...] = low
    sums_ref[2:3] += row_sum(low.astype(FLOAT_KIND))


def contrast(enc, starts, every, columns, normal, inverse, cotangent, gain, tm=256):
    count, width = normal.shape
    slots = starts.shape[0]
    return pl.pallas_call(
        contrast_kernel,
        grid_spec=pltpu.PrefetchScalarGridSpec(
            num_scalar_prefetch=2,
            grid=(count // tm,),
            in_specs=[
                whole(every.shape),
                whole(columns.shape),
                row_block(tm, width),
                row_block(tm, 1),
                row_block(tm, width),
                whole(gain.shape),
            ],
            out_specs=[row_block(tm, width), row_block(tm, width), whole((TILE, width))],
            scratch_shapes=[
                pltpu.VMEM((slots, width), FLOAT_KIND),
                pltpu.VMEM((tm, width), FLOAT_KIND),
            ],
        ),
        out_shape=[
            jax.ShapeDtypeStruct((count, width), FLOAT_KIND),
            jax.ShapeDtypeStruct((count, width), BRAIN),
            jax.ShapeDtypeStruct((TILE, width), FLOAT_KIND),
        ],
        cost_estimate=cost(1, 1),
        compiler_params=pltpu.CompilerParams(vmem_limit_bytes=8 * MEGA),
        name="contrast",
    )(enc, starts, every, columns, normal, inverse, cotangent, gain)


def contraction_kernel(flag_ref, low_ref, active_ref, *refs):
    turned_ref = refs[-1]
    step = pl.program_id(0)

    @pl.when(step == 0)
    def _():
        turned_ref[...] = low_ref[...].T

    value = dot(turned_ref[...], active_ref[...]).astype(BRAIN)
    for piece, out_ref in enumerate(refs[:-1]):

        @pl.when(step == piece)
        def _():
            out_ref[...] = value


def contraction_half(side, active, low, weight=1):
    count, hidden = active.shape
    width = low.shape[1]
    rows = width // 2
    tn = hidden // PIECES
    return pl.pallas_call(
        contraction_kernel,
        grid_spec=pltpu.PrefetchScalarGridSpec(
            num_scalar_prefetch=1,
            grid=(PIECES,),
            in_specs=[
                pl.BlockSpec((count, rows), lambda i, flag: (0, flag[0])),
                pl.BlockSpec((count, tn), lambda i, flag: (0, i)),
            ],
            out_specs=[whole((rows, tn))] * PIECES,
            scratch_shapes=[pltpu.VMEM((rows, count), BRAIN)],
        ),
        out_shape=[jax.ShapeDtypeStruct((rows, tn), BRAIN)] * PIECES,
        cost_estimate=cost(weight, 1),
        compiler_params=pltpu.CompilerParams(vmem_limit_bytes=8 * MEGA),
        name="contraction_half",
    )(side, low, active)


def feed_kernel(
    flag_ref,
    two_low_ref,
    shrink_ref,
    slope_ref,
    low_ref,
    expand_ref,
    two_ref,
    lift_ref,
    first_ref,
    *refs,
):
    pieces, turned_ref = refs[:-1], refs[-1]
    rows = turned_ref.shape[1]
    step = pl.program_id(0)

    @pl.when(step == 0)
    def _():
        first_ref[...] = two_ref[...]
        for side in range(2):

            @pl.when(flag_ref[SEND] == side)
            def _():
                turned_ref[0] = low_ref[:, side * rows : (side + 1) * rows].T
                turned_ref[1] = low_ref[:, (1 - side) * rows : (2 - side) * rows].T

    hidden = dot_rows(two_low_ref[...], shrink_ref[...]) * wide(slope_ref)
    low = hidden.astype(BRAIN)
    lift_ref[...] = row_sum(low.astype(FLOAT_KIND))
    first_ref[...] += dot_rows(low, expand_ref[...])
    for side in range(2):
        value = dot(turned_ref[side], low).astype(BRAIN)
        for piece in range(PIECES):

            @pl.when(step == piece)
            def _():
                pieces[side * PIECES + piece][...] = value


def feed_back(flags, two_low, shrink, slope, low, expand, two, weight=1):
    count, width = two.shape
    hidden = shrink.shape[0]
    rows = width // 2
    tn = hidden // PIECES
    column = lambda rows: pl.BlockSpec((rows, tn), lambda i, *_: (0, i))
    return pl.pallas_call(
        feed_kernel,
        grid_spec=pltpu.PrefetchScalarGridSpec(
            num_scalar_prefetch=1,
            grid=(PIECES,),
            in_specs=[
                whole((count, width)),
                row_block(tn, width),
                column(count),
                whole((count, width)),
                column(width),
                whole((count, width)),
            ],
            out_specs=[column(1), whole((count, width))] + [whole((rows, tn))] * 2 * PIECES,
            scratch_shapes=[pltpu.VMEM((2, rows, count), BRAIN)],
        ),
        out_shape=[
            jax.ShapeDtypeStruct((1, hidden), FLOAT_KIND),
            jax.ShapeDtypeStruct((count, width), FLOAT_KIND),
        ]
        + [jax.ShapeDtypeStruct((rows, tn), BRAIN)] * 2 * PIECES,
        cost_estimate=cost(weight, 1),
        compiler_params=pltpu.CompilerParams(vmem_limit_bytes=14 * MEGA),
        name="feed_back",
    )(flags, two_low, shrink, slope, low, expand, two)


def attend_back_kernel(
    first_ref,
    normal_ref,
    inverse_ref,
    gain_ref,
    merge_ref,
    packed_ref,
    weight_ref,
    one_ref,
    low_ref,
    packed_gradient_ref,
    sums_ref,
    packed_sums_ref,
    context_gradient_ref,
):
    width = normal_ref.shape[1]

    @pl.when(pl.program_id(0) == 0)
    def _():
        sums_ref[...] = jnp.zeros_like(sums_ref)
        packed_sums_ref[...] = jnp.zeros_like(packed_sums_ref)

    gradient = first_ref[...]
    normal = normal_ref[...]
    sums_ref[0:1] += row_sum(gradient * normal)
    sums_ref[1:2] += row_sum(gradient)
    one = norm_backward(gradient, normal, inverse_ref[...], wide(gain_ref))
    one_ref[...] = one
    low = one.astype(BRAIN)
    low_ref[...] = low
    sums_ref[2:3] += row_sum(low.astype(FLOAT_KIND))
    context_gradient_ref[...] = dot_rows(low, merge_ref[...]).astype(BRAIN)
    low_row = lax.broadcasted_iota(jnp.int32, (LANES, 1), 0) < HEAD
    scale = 1.0 / math.sqrt(HEAD)
    for pair in range(width // LANES):
        at = LANES * pair
        queries = both_heads(packed_ref[:, at : at + LANES] * scale)
        keys = packed_ref[:, width + at : width + at + LANES] * scale
        values = packed_ref[:, 2 * width + at : 2 * width + at + LANES]
        outer = both_heads(context_gradient_ref[:, at : at + LANES])
        weights = weight_ref[pair]
        probability = weights.astype(FLOAT_KIND)
        inner = dot_rows(values, outer)
        scores = (probability * (inner - row_sum(probability * inner))).astype(BRAIN)
        turned = dot(keys.T, scores)
        found = (
            jnp.where(low_row, turned[:, :ROWS], turned[:, ROWS:]).T,
            dot(scores, queries),
            dot(weights, outer),
        )
        for part in range(3):
            columns = slice(part * width + at, part * width + at + LANES)
            packed_gradient_ref[:, columns] = found[part].astype(BRAIN)
    packed_sums_ref[...] += row_sum(wide(packed_gradient_ref))


def attend_back(first, normal, inverse, gain, merge, packed, weights, weight=1):
    count, width = normal.shape
    heads = width // HEAD
    return pl.pallas_call(
        attend_back_kernel,
        grid=(count // ROWS,),
        in_specs=[
            row_block(ROWS, width),
            row_block(ROWS, width),
            row_block(ROWS, 1),
            whole(gain.shape),
            whole(merge.shape),
            row_block(ROWS, 3 * width),
            pl.BlockSpec((None, heads // 2, ROWS, 2 * ROWS), lambda i: (i, 0, 0, 0)),
        ],
        out_specs=[
            row_block(ROWS, width),
            row_block(ROWS, width),
            row_block(ROWS, 3 * width),
            whole((TILE, width)),
            whole((1, 3 * width)),
        ],
        out_shape=[
            jax.ShapeDtypeStruct((count, width), FLOAT_KIND),
            jax.ShapeDtypeStruct((count, width), BRAIN),
            jax.ShapeDtypeStruct((count, 3 * width), BRAIN),
            jax.ShapeDtypeStruct((TILE, width), FLOAT_KIND),
            jax.ShapeDtypeStruct((1, 3 * width), FLOAT_KIND),
        ],
        scratch_shapes=[pltpu.VMEM((ROWS, width), BRAIN)],
        cost_estimate=cost(weight, 1),
        compiler_params=pltpu.CompilerParams(vmem_limit_bytes=11 * MEGA),
        name="attend_back",
    )(first, normal, inverse, gain, merge, packed, weights)


def merge_project_kernel(flag_ref, context_ref, one_ref, x_ref, packed_ref, *refs):
    pieces, turned_ref = refs[:-1], refs[-1]
    step = pl.program_id(0)

    @pl.when(step == 0)
    def _():
        turned_ref[...] = context_ref[...].T
        pieces[0][...] = dot(turned_ref[...], one_ref[...]).astype(BRAIN)
        turned_ref[...] = x_ref[...].T

    @pl.when(step > 0)
    def _():
        value = dot(turned_ref[...], packed_ref[...]).astype(BRAIN)
        for piece in range(1, PIECES):

            @pl.when(step == piece)
            def _():
                pieces[piece][...] = value


def merge_project_half(side, context, one, x, packed, weight=1):
    count, width = x.shape
    rows = width // 2
    return pl.pallas_call(
        merge_project_kernel,
        grid_spec=pltpu.PrefetchScalarGridSpec(
            num_scalar_prefetch=1,
            grid=(PIECES,),
            in_specs=[
                pl.BlockSpec((count, rows), lambda i, flag: (0, flag[0])),
                whole((count, width)),
                pl.BlockSpec((count, rows), lambda i, flag: (0, flag[0])),
                pl.BlockSpec((count, width), lambda i, flag: (0, jnp.maximum(i - 1, 0))),
            ],
            out_specs=[whole((rows, width))] * PIECES,
            scratch_shapes=[pltpu.VMEM((rows, count), BRAIN)],
        ),
        out_shape=[jax.ShapeDtypeStruct((rows, width), BRAIN)] * PIECES,
        cost_estimate=cost(weight, 1),
        compiler_params=pltpu.CompilerParams(vmem_limit_bytes=10 * MEGA),
        name="merge_project_half",
    )(side, context, one, x, packed)


def fold_kernel(flag_ref, *refs, count, side):
    keep, other, outs = refs[:count], refs[count : 2 * count], refs[2 * count :]
    rows = outs[0].shape[0]
    columns = outs[0].shape[1] // count
    for out_ref, half in zip(outs, (1 - flag_ref[side], flag_ref[side])):

        @pl.loop(0, rows // PACKED)
        def _(block):
            to = pl.ds(pl.multiple_of(block * PACKED, PACKED), PACKED)
            at = pl.ds(pl.multiple_of(half * rows + block * PACKED, PACKED), PACKED)
            for piece in range(count):
                total = wide(keep[piece].at[at]) + wide(other[piece].at[at])
                out_ref[to, piece * columns : (piece + 1) * columns] = total.astype(BRAIN)


def folded(flags, place, keep, other, weight):
    rows, columns = keep[0].shape
    count = len(keep)
    if rows % (2 * PACKED):
        (mine,), (theirs,) = keep, other
        bit = flags[place]
        return part_sum(mine, theirs, 1 - bit), part_sum(mine, theirs, bit)
    shape = jax.ShapeDtypeStruct((rows // 2, count * columns), BRAIN)
    return pl.pallas_call(
        functools.partial(fold_kernel, count=count, side=place),
        grid_spec=pltpu.PrefetchScalarGridSpec(
            num_scalar_prefetch=1,
            grid=(1,),
            in_specs=[whole((rows, columns))] * 2 * count,
            out_specs=[whole(shape.shape)] * 2,
        ),
        out_shape=[shape, shape],
        cost_estimate=cost(weight, 1),
        compiler_params=pltpu.CompilerParams(vmem_limit_bytes=5 * MEGA),
        name="fold",
    )(flags, *keep, *other)


def add_kernel(mine_ref, other_ref, out_ref):
    out_ref[...] = (wide(mine_ref) + wide(other_ref)).astype(out_ref.dtype)


def added(mine, other, weight=1):
    return pl.pallas_call(
        add_kernel,
        out_shape=jax.ShapeDtypeStruct(mine.shape, mine.dtype),
        cost_estimate=cost(weight, 1),
        compiler_params=pltpu.CompilerParams(vmem_limit_bytes=2 * MEGA),
        name="add",
    )(mine, other)


def join_kernel(flag_ref, mine_ref, other_ref, out_ref, *, side):
    rows = mine_ref.shape[0]
    out_ref[pl.ds(pl.multiple_of(flag_ref[side] * rows, rows), rows), :] = mine_ref[...]
    out_ref[pl.ds(pl.multiple_of((1 - flag_ref[side]) * rows, rows), rows), :] = other_ref[...]


def joined(flags, place, mine, other, weight):
    rows, columns = mine.shape
    if rows % PACKED:
        return joined_by_bit(mine, other, flags[place])
    return pl.pallas_call(
        functools.partial(join_kernel, side=place),
        grid_spec=pltpu.PrefetchScalarGridSpec(
            num_scalar_prefetch=1,
            grid=(1,),
            in_specs=[whole(mine.shape)] * 2,
            out_specs=whole((2 * rows, columns)),
        ),
        out_shape=jax.ShapeDtypeStruct((2 * rows, columns), BRAIN),
        cost_estimate=cost(weight, 1),
        compiler_params=pltpu.CompilerParams(vmem_limit_bytes=4 * MEGA),
        name="join",
    )(flags, mine, other)


def tokens_kernel(one_ref, packed_ref, project_ref, out_ref):
    out_ref[...] = one_ref[...] + dot_rows(packed_ref[...], project_ref[...])


def tokens_back(one, packed, project, tm=256, weight=1):
    count, width = one.shape
    return pl.pallas_call(
        tokens_kernel,
        grid=(count // tm,),
        in_specs=[row_block(tm, width), row_block(tm, 3 * width), whole(project.shape)],
        out_specs=row_block(tm, width),
        out_shape=jax.ShapeDtypeStruct((count, width), FLOAT_KIND),
        cost_estimate=cost(weight, 1),
        compiler_params=pltpu.CompilerParams(vmem_limit_bytes=13 * MEGA),
        name="tokens_back",
    )(one, packed, project)


def pack_kernel(packed_ref, attend_ref, lift_ref, output_ref, out_ref):
    width = attend_ref.shape[1]
    out_ref[...] = jnp.zeros_like(out_ref)
    out_ref[0:1] = packed_ref[:, :width]
    out_ref[1:2] = packed_ref[:, 2 * width :]
    out_ref[2:5] = attend_ref[0:3]
    for part in range(4):
        out_ref[5 + part : 6 + part] = lift_ref[:, part * width : (part + 1) * width]
    out_ref[9:12] = output_ref[0:3]


def pack_vectors(packed_sums, attend_sums, lift_sums, output_sums):
    width = attend_sums.shape[1]
    return pl.pallas_call(
        pack_kernel,
        out_shape=jax.ShapeDtypeStruct((16, width), FLOAT_KIND),
        cost_estimate=cost(1, 1),
        compiler_params=pltpu.CompilerParams(vmem_limit_bytes=2 * MEGA),
        name="pack_vectors",
    )(packed_sums, attend_sums, lift_sums, output_sums)


def unpack_kernel(mine_ref, other_ref, offset_ref, adjust_ref, scale_ref, center_ref, lift_ref, settle_ref, rescale_ref, recenter_ref):
    width = mine_ref.shape[1]
    total = mine_ref[...] + other_ref[...]
    offset_ref[:, :width] = total[0:1]
    offset_ref[:, width:] = total[1:2]
    scale_ref[...] = total[2:3]
    center_ref[...] = total[3:4]
    adjust_ref[...] = total[4:5]
    for part in range(4):
        lift_ref[:, part * width : (part + 1) * width] = total[5 + part : 6 + part]
    rescale_ref[...] = total[9:10]
    recenter_ref[...] = total[10:11]
    settle_ref[...] = total[11:12]


def unpack_vectors(mine, other):
    width = mine.shape[1]
    shapes = [2, 1, 1, 1, 4, 1, 1, 1]
    return pl.pallas_call(
        unpack_kernel,
        out_shape=[jax.ShapeDtypeStruct((1, k * width), FLOAT_KIND) for k in shapes],
        cost_estimate=cost(1, 1),
        compiler_params=pltpu.CompilerParams(vmem_limit_bytes=2 * MEGA),
        name="unpack_vectors",
    )(mine, other)


def place_kernel(flag_ref, value_ref, *refs, kept):
    at = 0
    for out_ref in refs[kept:]:
        columns = out_ref.shape[1]
        out_ref[...] = value_ref[:, at : at + columns].astype(FLOAT_KIND)
        at += columns


def place_half(flags, side, value, columns, before, tm=192):
    rows = value.shape[0]
    steps = rows // tm
    kept = [] if before is None else list(before)
    return pl.pallas_call(
        functools.partial(place_kernel, kept=len(kept)),
        grid_spec=pltpu.PrefetchScalarGridSpec(
            num_scalar_prefetch=1,
            grid=(steps,),
            in_specs=[row_block(tm, value.shape[1])]
            + [pl.BlockSpec(memory_space=pl.ANY)] * len(kept),
            out_specs=[
                pl.BlockSpec((tm, size), lambda i, flag: (flag[side] * steps + i, 0))
                for size in columns
            ],
        ),
        out_shape=[jax.ShapeDtypeStruct((2 * rows, size), FLOAT_KIND) for size in columns],
        input_output_aliases={2 + k: k for k in range(len(kept))},
        cost_estimate=cost(1, 1),
        compiler_params=pltpu.CompilerParams(vmem_limit_bytes=10 * MEGA),
        name="place_half",
    )(flags, value, *kept)


def place_turned_kernel(flag_ref, value_ref, *refs):
    refs[-1][...] = value_ref[...].astype(FLOAT_KIND).T


def place_turned_half(flags, side, value, before, tm=1536):
    rows, columns = value.shape
    kept = [] if before is None else list(before)
    return pl.pallas_call(
        place_turned_kernel,
        grid_spec=pltpu.PrefetchScalarGridSpec(
            num_scalar_prefetch=1,
            grid=(columns // tm,),
            in_specs=[pl.BlockSpec((rows, tm), lambda i, flag: (0, i))]
            + [pl.BlockSpec(memory_space=pl.ANY)] * len(kept),
            out_specs=[pl.BlockSpec((tm, rows), lambda i, flag: (i, flag[side]))],
        ),
        out_shape=[jax.ShapeDtypeStruct((columns, 2 * rows), FLOAT_KIND)],
        input_output_aliases={2 + k: k for k in range(len(kept))},
        cost_estimate=cost(1, 1),
        compiler_params=pltpu.CompilerParams(vmem_limit_bytes=14 * MEGA),
        name="place_turned_half",
    )(flags, value, *kept)


def swapped(value, axis, apart):
    mask = 2**apart
    pairs = [(source, source ^ mask) for source in range(lax.axis_size(axis))]
    return lax.ppermute(value, axis, pairs)


def swapped_by_core(value, stage):
    count = lax.axis_size("batch")
    pairs = [(source, source ^ (1 << stage[source & 1])) for source in range(count)]
    return lax.ppermute(value, "batch", pairs)


def bit_count(axis):
    return lax.axis_size(axis).bit_length() - 1


def to_low(values):
    return values.astype(BRAIN)


def part_sum(mine, other, bit):
    half = mine.shape[0] // 2
    left = lax.dynamic_slice_in_dim(mine, bit * half, half, 0).astype(FLOAT_KIND)
    right = lax.dynamic_slice_in_dim(other, bit * half, half, 0).astype(FLOAT_KIND)
    return to_low(left + right)


def joined_by_bit(mine, other, bit):
    low_part = jnp.where(bit == 0, mine, other)
    high_part = jnp.where(bit == 0, other, mine)
    return jnp.concatenate([low_part, high_part], axis=0)


class Sequence:
    def __init__(self):
        self.last = None

    def run(self, step, *inputs):
        if self.last is not None:
            *inputs, _ = lax.optimization_barrier((*inputs, self.last))
        result = step(*inputs)
        self.last = jax.tree.leaves(result)[0]
        return result


class Reduction:
    def __init__(self, sequence, flags, stages, at, put):
        self.run = sequence.run
        self.flags = flags
        self.stages = stages
        self.at = at
        self.put = put
        count = len(stages)
        self.steps = [functools.partial(self.scatter, k) for k in range(count)]
        self.steps.append(self.finish)
        self.steps += [functools.partial(self.gather, k) for k in reversed(range(count))]
        self.steps.append(self.place)

    def advance(self, weight=1):
        self.steps.pop(0)(weight)

    def begin(self, send, keep):
        self.keep = list(keep)
        self.other = [swapped(piece, "batch", 0) for piece in send]

    def scatter(self, stage, weight):
        count = len(self.keep)
        send, keep = self.run(
            lambda *v: folded(self.flags, self.at + stage, v[:count], v[count:], weight),
            *self.keep,
            *self.other,
        )
        self.keep = [keep]
        self.other = [swapped_by_core(send, self.stages[stage])]

    def finish(self, weight):
        self.value = self.run(lambda a, b: added(a, b, weight), *self.keep, *self.other)
        self.other = swapped_by_core(self.value, self.stages[-1])

    def gather(self, stage, weight):
        self.value = self.run(
            lambda v, o: joined(self.flags, self.at + stage, v, o, weight), self.value, self.other
        )
        if stage > 0:
            self.other = swapped_by_core(self.value, self.stages[stage - 1])
            return
        self.other = swapped(self.value, "batch", 0)
        self.placed = self.run(lambda v: self.put(self.flags, KEEP, v, None), self.value)

    def place(self, weight):
        self.total = self.run(
            lambda o, *p: self.put(self.flags, SEND, o, p), self.other, *self.placed
        )


def shards(
    tokens,
    cotangent,
    projection,
    offsets,
    merger,
    adjust,
    scaling,
    centering,
    expansion,
    lifting,
    contraction,
    settling,
    rescale,
    recenter,
    segments,
    passage_starts,
    passage_counts,
    positives,
):
    index = lax.axis_index("batch").astype(jnp.int32)
    slots = passage_starts.shape[0]
    bits = bit_count("batch")
    plain = [(apart, apart) for apart in range(1, bits)]
    mixed = [(apart, other) for (apart, _), (other, _) in zip(plain, plain[1:] + plain[:1])]
    kinds = (plain, mixed, [(odd, even) for even, odd in mixed])
    flags = jnp.stack(
        [lax.axis_index("enc").astype(jnp.int32), index & 1, 1 - (index & 1)]
        + [
            (index >> jnp.where(index & 1 == 0, even, odd)) & 1
            for stages in kinds
            for even, odd in stages
        ]
    )
    order = list(reversed(range(bits)))
    place = jnp.arange(lax.axis_size("batch"), dtype=jnp.int32)
    away = sum(((place >> k) & 1) << apart for k, apart in enumerate(order))
    device = (index ^ away)[:, None]
    slot = jnp.arange(slots, dtype=jnp.int32)[None, :]
    held = jnp.sum(jnp.where(device == place[None, :], passage_counts[None, :], 0), axis=1)
    columns = jnp.where(slot < held[:, None], device * slots + slot, -1).reshape(1, -1)
    keep_side = (index & 1)[None]
    flags, keep_side, send_side, columns, tokens = lax.optimization_barrier(
        (flags, keep_side, 1 - keep_side, columns, tokens)
    )
    width = tokens.shape[2]
    x, project, merge, expand, shrink, outer = (
        in_hbm(tokens[0]),
        in_hbm(projection[0]),
        in_hbm(merger[0]),
        expansion[0],
        in_hbm(contraction[0]),
        in_hbm(cotangent[0]),
    )
    first = (in_hbm(scaling), in_hbm(centering))
    second = (in_hbm(rescale), in_hbm(recenter))
    adjust, lifting, settling, offsets = (
        in_hbm(v) for v in (adjust, lifting, settling, offsets)
    )

    sequence = Sequence()
    run = sequence.run
    packed, weights, context, normal_one, inverse_one, low = attend(
        flags, x, project, offsets, in_hbm(segments[None]), merge, adjust, *first
    )
    parcel = summarize(
        flags,
        passage_starts,
        positives,
        normal_one,
        first,
        expand,
        lifting,
        shrink,
        settling,
        second,
    )
    sequence.last = parcel
    parts = 4
    every = parcel[None]
    other = swapped(parcel, "enc", 0)[None]
    wide_pair = run(lambda v: widen(0, parts, v, expand, lifting, None), low)
    every = run(lambda a, b: jnp.stack([a, b], axis=1), every, other)
    for part, apart in enumerate(order, 1):
        other = swapped(every, "batch", apart)
        if part < parts:
            wide_pair = run(
                lambda v, *p: widen(part, parts, v, expand, lifting, p), low, *wide_pair
            )
        elif part == parts:
            active, slope = wide_pair
            normal_two, inverse_two, encoded = run(
                lambda a, n: shrink_back_to_width(a, shrink, n, first, settling, second),
                active,
                normal_one,
            )
        every = run(lambda a, b: jnp.concatenate([a, b], axis=0), every, other)
    two, two_low, output_sums = run(
        lambda *v: contrast(flags, passage_starts, *v, outer, second[0]),
        every,
        columns,
        normal_two,
        inverse_two,
    )

    puts = (
        place_turned_half,
        lambda f, s, v, p: place_half(f, s, v, (expansion.shape[2],), p),
        lambda f, s, v, p: place_half(f, s, v, (width, projection.shape[2]), p),
    )
    shrink_sum, expand_sum, project_sum = (
        Reduction(sequence, flags, kinds[kind], STAGES + kind * len(plain), put)
        for kind, put in zip(LINKS, puts)
    )
    product = lambda side: run(
        lambda c, o, p: merge_project_half(side, c, o, x, p, weight),
        context,
        one_low,
        packed_gradient,
    )
    vectors = []
    apart = 0
    for step in PLAN:
        weight = LEVELS[int(step[1:] or 0)]
        kind = step[0]
        if kind == "C":
            send = run(lambda a, t: contraction_half(send_side, a, t, weight), active, two_low)
            keep = run(lambda a, t: contraction_half(keep_side, a, t, weight), active, two_low)
            shrink_sum.begin(send, keep)
        elif kind == "F":
            lift_sums, gradient_first, *both = run(
                lambda t, s, g: feed_back(flags, t, shrink, s, low, expand, g, weight),
                two_low,
                slope,
                two,
            )
            expand_sum.begin(both[:PIECES], both[PIECES:])
        elif kind == "A":
            one, one_low, packed_gradient, attend_sums, packed_sums = run(
                lambda g, n, i, p, w: attend_back(g, n, i, first[0], merge, p, w, weight),
                gradient_first,
                normal_one,
                inverse_one,
                packed,
                weights,
            )
        elif kind == "S":
            send = product(send_side)
        elif kind == "K":
            keep = product(keep_side)
            project_sum.begin(send, keep)
        elif kind == "T":
            tokens_gradient = run(lambda o, p: tokens_back(o, p, project, weight=weight), one, packed_gradient)
        elif kind == "P":
            vectors = [run(pack_vectors, packed_sums, attend_sums, lift_sums, output_sums)]
            vectors.append(swapped(vectors[0], "batch", apart))
        elif kind == "v":
            apart += 1
            vectors = [run(lambda a, b, w=weight: added(a, b, w), *vectors)]
            vectors.append(swapped(vectors[0], "batch", apart))
        else:
            {"c": shrink_sum, "e": expand_sum, "m": project_sum}[kind].advance(weight)
    while apart < bits - 1:
        apart += 1
        vectors = [run(added, *vectors)]
        vectors.append(swapped(vectors[0], "batch", apart))
    vector_totals = run(unpack_vectors, *vectors)
    for reduction in (shrink_sum, expand_sum, project_sum):
        while reduction.steps:
            reduction.advance()
    (total_contraction,) = shrink_sum.total
    (total_expansion,) = expand_sum.total
    total_merger, total_projection = project_sum.total
    (
        total_offsets,
        total_adjust,
        total_scaling,
        total_centering,
        total_lifting,
        total_settling,
        total_rescale,
        total_recenter,
    ) = vector_totals
    return (
        encoded[None],
        tokens_gradient[None],
        total_projection[None],
        total_offsets,
        total_merger[None],
        total_adjust,
        total_scaling,
        total_centering,
        total_expansion[None],
        total_lifting,
        total_contraction[None],
        total_settling,
        total_rescale,
        total_recenter,
    )


def solution(mesh):
    matrix = P("enc", None, None)
    vector = P("enc", None)
    rows = P("enc", "batch", None)
    return jax.shard_map(
        shards,
        mesh=mesh,
        in_specs=(
            rows,
            rows,
            matrix,
            vector,
            matrix,
            vector,
            vector,
            vector,
            matrix,
            vector,
            matrix,
            vector,
            vector,
            vector,
            P("batch"),
            P("batch"),
            P(),
            P("batch"),
        ),
        out_specs=(
            rows,
            rows,
            matrix,
            vector,
            matrix,
            vector,
            vector,
            vector,
            matrix,
            vector,
            matrix,
            vector,
            vector,
            vector,
        ),
        check_vma=False,
    )
```

```python
import functools
import math

import jax
import jax.numpy as jnp
from jax import lax
from jax.experimental import pallas as pl
from jax.experimental.pallas import tpu as pltpu
from jax.sharding import PartitionSpec as P

QLEN = 64
ROWS = 256
HEAD = 64
TILE = 8
LANES = 128
PIECES = 4
PACKED = 16
PLAN = (
    "C4", "c", "F2", "c", "e4", "A2", "c", "S3", "e3", "c2", "P", "K3",
    "m1", "e3", "T", "v", "c3", "e2", "m3", "c3", "m1", "e", "m1", "c1",
    "m3", "e", "v1", "m1", "c", "e", "v", "m", "e2", "m4",
)
LINKS = (2, 2, 2)
LEVELS = (1, 2 * 10**9, 6 * 10**9, 2 * 10**10, 10**11)
ENC, KEEP, SEND, STAGES = 0, 1, 2, 3
MEGA = 2**20
EPSILON = 1e-12
SHARPNESS_DIVISOR = 2.0
LOSS_WEIGHT = 2.0
HIDDEN_SCORE = -1e30
FLOAT_KIND = jnp.float32
BRAIN = jnp.bfloat16

TAIL = tuple(
    0.5 * a for a in (0.254829592, -0.284496736, 1.421413741, -1.453152027, 1.061405429)
)
TAIL_SLOPE = 0.3275911 / math.sqrt(2.0)
DENSITY = 1.0 / math.sqrt(2.0 * math.pi)


def dot(left, right):
    return jnp.dot(left, right, preferred_element_type=FLOAT_KIND)


def dot_rows(left, right):
    return lax.dot_general(left, right, (((1,), (1,)), ((), ())), preferred_element_type=FLOAT_KIND)


def dot_columns(left, right):
    return lax.dot_general(left, right, (((0,), (0,)), ((), ())), preferred_element_type=FLOAT_KIND)


def whole(shape):
    return pl.BlockSpec(shape, lambda *_: (0,) * len(shape))


def row_block(rows, columns):
    return pl.BlockSpec((rows, columns), lambda i, *_: (i, 0))


def in_hbm(value):
    return pltpu.with_memory_space_constraint(value, pltpu.HBM)


def hbm_shape(shape, dtype):
    return pltpu.HBM(shape, dtype)


def cost(flops, moved, transcendentals=0):
    return pl.CostEstimate(flops=flops, bytes_accessed=1, transcendentals=0)


def wide(ref):
    return ref[...].astype(FLOAT_KIND)


def row_sum(values):
    return jnp.sum(values, axis=0, keepdims=True)


def normalized(values):
    centered = values - jnp.mean(values, axis=1, keepdims=True)
    spread = jnp.mean(centered * centered, axis=1, keepdims=True)
    scale = lax.rsqrt(spread + EPSILON)
    return centered * scale, scale


def norm_backward(gradient, normal, inverse, gain):
    scaled = gradient * gain
    return (
        scaled
        - jnp.mean(scaled, axis=1, keepdims=True)
        - normal * jnp.mean(scaled * normal, axis=1, keepdims=True)
    ) * inverse


def both_heads(values):
    low_lane = lax.broadcasted_iota(jnp.int32, (1, LANES), 1) < HEAD
    nothing = jnp.zeros_like(values)
    return jnp.concatenate(
        [jnp.where(low_lane, values, nothing), jnp.where(low_lane, nothing, values)], axis=0
    )


def gelu_and_slope(hidden):
    bell = jnp.exp(hidden * hidden * -0.5)
    t = 1.0 / (1.0 + TAIL_SLOPE * jnp.abs(hidden))
    series = TAIL[3] + t * TAIL[4]
    series = TAIL[2] + t * series
    series = TAIL[1] + t * series
    series = TAIL[0] + t * series
    tail = t * series * bell
    below = jnp.where(hidden < 0.0, tail, 1.0 - tail)
    return hidden * below, below + hidden * bell * DENSITY


def attend_kernel(
    flag_ref,
    x_ref,
    project_ref,
    offset_ref,
    segment_ref,
    merge_ref,
    adjust_ref,
    gain_ref,
    shift_ref,
    packed_ref,
    weight_ref,
    context_ref,
    normal_ref,
    inverse_ref,
    low_ref,
):
    width = x_ref.shape[1]
    x = x_ref[...]
    for part in range(3):
        columns = slice(part * width, (part + 1) * width)
        sums = dot(x, project_ref[:, columns])
        if part != 1:
            at = 0 if part == 0 else width
            sums = sums + offset_ref[:, at : at + width].astype(FLOAT_KIND)
        packed_ref[:, columns] = sums.astype(BRAIN)
    position = lax.broadcasted_iota(jnp.int32, (1, ROWS), 1)
    marks = jnp.where(flag_ref[ENC] == 1, segment_ref[...], position // QLEN).astype(FLOAT_KIND)
    spread_marks = jnp.broadcast_to(marks, (ROWS, ROWS))
    hide = jnp.where(spread_marks == spread_marks.T, 0.0, HIDDEN_SCORE)
    hide = jnp.concatenate([hide, hide], axis=0)
    low_lane = lax.broadcasted_iota(jnp.int32, (1, LANES), 1) < HEAD
    scale = 1.0 / math.sqrt(HEAD)
    for pair in range(width // LANES):
        at = LANES * pair
        queries = both_heads(packed_ref[:, at : at + LANES] * scale)
        keys = packed_ref[:, width + at : width + at + LANES]
        values = packed_ref[:, 2 * width + at : 2 * width + at + LANES]
        scores = dot_rows(queries, keys) + hide
        raised = jnp.exp(scores - jnp.max(scores, axis=1, keepdims=True))
        weights = (raised * (1.0 / jnp.sum(raised, axis=1, keepdims=True))).astype(BRAIN)
        weight_ref[pair] = weights.T
        context = dot(weights, values)
        context = jnp.where(low_lane, context[:ROWS], context[ROWS:])
        context_ref[:, at : at + LANES] = context.astype(BRAIN)
    attended = dot(context_ref[...], merge_ref[...]) + wide(adjust_ref)
    normal, inverse = normalized(x.astype(FLOAT_KIND) + attended)
    normal_ref[...] = normal
    inverse_ref[...] = inverse
    low_ref[...] = (normal * wide(gain_ref) + wide(shift_ref)).astype(BRAIN)


def attend(enc, x, project, offsets, segments, merge, adjust, gain, shift):
    count, width = x.shape
    blocks = count // ROWS
    heads = width // HEAD
    return pl.pallas_call(
        attend_kernel,
        grid_spec=pltpu.PrefetchScalarGridSpec(
            num_scalar_prefetch=1,
            grid=(blocks,),
            in_specs=[
                row_block(ROWS, width),
                whole(project.shape),
                whole(offsets.shape),
                pl.BlockSpec((1, ROWS), lambda i, *_: (0, i)),
                whole(merge.shape),
                whole(adjust.shape),
                whole(gain.shape),
                whole(shift.shape),
            ],
            out_specs=[
                row_block(ROWS, 3 * width),
                pl.BlockSpec((None, heads // 2, ROWS, 2 * ROWS), lambda i, *_: (i, 0, 0, 0)),
                row_block(ROWS, width),
                row_block(ROWS, width),
                row_block(ROWS, 1),
                row_block(ROWS, width),
            ],
        ),
        out_shape=[
            jax.ShapeDtypeStruct((count, 3 * width), BRAIN),
            jax.ShapeDtypeStruct((blocks, heads // 2, ROWS, 2 * ROWS), BRAIN),
            jax.ShapeDtypeStruct((count, width), BRAIN),
            jax.ShapeDtypeStruct((count, width), FLOAT_KIND),
            jax.ShapeDtypeStruct((count, 1), FLOAT_KIND),
            jax.ShapeDtypeStruct((count, width), BRAIN),
        ],
        cost_estimate=cost(1, 1),
        compiler_params=pltpu.CompilerParams(vmem_limit_bytes=17 * MEGA),
        name="attend",
    )(enc, x, project, offsets, segments, merge, adjust, gain, shift)


def summary_kernel(
    flag_ref,
    start_ref,
    target_ref,
    normal_ref,
    gain_one_ref,
    shift_one_ref,
    expand_ref,
    lift_ref,
    shrink_ref,
    settle_ref,
    gain_two_ref,
    shift_two_ref,
    out_ref,
    tile_ref,
    row_ref,
    low_ref,
    total_ref,
    copy_sem,
):
    slots, width = row_ref.shape
    step = pl.program_id(0)

    @pl.when(step == 0)
    def _():
        copies = [
            pltpu.make_async_copy(
                normal_ref.at[jnp.where(flag_ref[ENC] == 1, start_ref[slot], slot * QLEN) // TILE],
                tile_ref.at[slot],
                copy_sem.at[slot],
            )
            for slot in range(slots)
        ]
        for copy in copies:
            copy.start()
        for copy in copies:
            copy.wait()
        rows = tile_ref[:, 0, :] * wide(gain_one_ref) + wide(shift_one_ref)
        row_ref[...] = rows
        low_ref[...] = rows.astype(BRAIN)
        total_ref[...] = jnp.zeros_like(total_ref)

    activated, _ = gelu_and_slope(dot(low_ref[...], expand_ref[...]) + wide(lift_ref))
    total_ref[...] += dot(activated.astype(BRAIN), shrink_ref[...])

    @pl.when(step == pl.num_programs(0) - 1)
    def _():
        normal, _ = normalized(row_ref[...] + (total_ref[...] + wide(settle_ref)))
        out_ref[:, :width] = (normal * wide(gain_two_ref) + wide(shift_two_ref)).astype(BRAIN)
        lane = lax.broadcasted_iota(jnp.int32, (slots, LANES), 1)
        place = lax.broadcasted_iota(jnp.int32, (slots, LANES), 0)
        digits = jnp.zeros((slots, LANES), jnp.int32)
        for slot in range(slots):
            target = target_ref[slot]
            pair = jnp.where(lane == 0, target // LANES, jnp.where(lane == 1, target % LANES, 0))
            digits = jnp.where(place == slot, pair, digits)
        out_ref[:, width:] = digits.astype(FLOAT_KIND).astype(BRAIN)


def summarize(enc, starts, targets, normal, first, expand, lift, shrink, settle, second, tn=1024):
    count, width = normal.shape
    hidden = expand.shape[1]
    slots = starts.shape[0]
    row = whole((1, width))
    return pl.pallas_call(
        summary_kernel,
        grid_spec=pltpu.PrefetchScalarGridSpec(
            num_scalar_prefetch=3,
            grid=(hidden // tn,),
            in_specs=[
                pl.BlockSpec(memory_space=pl.ANY),
                row,
                row,
                pl.BlockSpec((width, tn), lambda i, *_: (0, i)),
                pl.BlockSpec((1, tn), lambda i, *_: (0, i)),
                pl.BlockSpec((tn, width), lambda i, *_: (i, 0)),
                row,
                row,
                row,
            ],
            out_specs=whole((slots, width + LANES)),
            scratch_shapes=[
                pltpu.VMEM((slots, TILE, width), FLOAT_KIND),
                pltpu.VMEM((slots, width), FLOAT_KIND),
                pltpu.VMEM((slots, width), BRAIN),
                pltpu.VMEM((slots, width), FLOAT_KIND),
                pltpu.SemaphoreType.DMA((slots,)),
            ],
        ),
        out_shape=jax.ShapeDtypeStruct((slots, width + LANES), BRAIN),
        cost_estimate=cost(1, 1),
        compiler_params=pltpu.CompilerParams(vmem_limit_bytes=10 * MEGA),
        name="summarize",
    )(
        enc,
        starts,
        targets,
        normal.reshape(count // TILE, TILE, width),
        *first,
        expand,
        lift,
        shrink,
        settle,
        *second,
    )


def widen_kernel(low_ref, expand_ref, lift_ref, *refs):
    active_ref, slope_ref = refs[-2:]

    @pl.loop(0, low_ref.shape[0] // ROWS)
    def _(block):
        rows = pl.ds(pl.multiple_of(block * ROWS, ROWS), ROWS)
        hidden = dot(low_ref[rows, :], expand_ref[...]) + wide(lift_ref)
        activated, slope = gelu_and_slope(hidden)
        active_ref[rows, :] = activated.astype(BRAIN)
        slope_ref[rows, :] = slope.astype(BRAIN)


def widen(part, parts, low, expand, lift, before, tn=768):
    count, width = low.shape
    hidden = expand.shape[1]
    steps = hidden // parts // tn
    column = lambda rows: pl.BlockSpec((rows, tn), lambda i: (0, part * steps + i))
    kept = [] if before is None else list(before)
    return pl.pallas_call(
        widen_kernel,
        grid=(steps,),
        in_specs=[whole(low.shape), column(width), column(1)]
        + [pl.BlockSpec(memory_space=pl.ANY)] * len(kept),
        out_specs=[column(count), column(count)],
        out_shape=[jax.ShapeDtypeStruct((count, hidden), BRAIN)] * 2,
        input_output_aliases={3 + k: k for k in range(len(kept))},
        cost_estimate=cost(1, 1),
        compiler_params=pltpu.CompilerParams(vmem_limit_bytes=10 * MEGA),
        name="widen",
    )(low, expand, lift, *kept)


def shrink_kernel(
    active_ref,
    shrink_ref,
    normal_ref,
    gain_one_ref,
    shift_one_ref,
    settle_ref,
    gain_two_ref,
    shift_two_ref,
    out_ref,
    inverse_ref,
    encoded_ref,
):
    normed = normal_ref[...] * wide(gain_one_ref) + wide(shift_one_ref)
    shrunk = dot(active_ref[...], shrink_ref[...]) + wide(settle_ref)
    normal, inverse = normalized(normed + shrunk)
    out_ref[...] = normal
    inverse_ref[...] = inverse
    encoded_ref[...] = (normal * wide(gain_two_ref) + wide(shift_two_ref)).astype(BRAIN)


def shrink_back_to_width(active, shrink, normal, first, settle, second, tm=256):
    count, hidden = active.shape
    width = shrink.shape[1]
    row = whole((1, width))
    return pl.pallas_call(
        shrink_kernel,
        grid=(count // tm,),
        in_specs=[row_block(tm, hidden), whole(shrink.shape), row_block(tm, width)] + [row] * 5,
        out_specs=[row_block(tm, width), row_block(tm, 1), row_block(tm, width)],
        out_shape=[
            jax.ShapeDtypeStruct((count, width), FLOAT_KIND),
            jax.ShapeDtypeStruct((count, 1), FLOAT_KIND),
            jax.ShapeDtypeStruct((count, width), BRAIN),
        ],
        cost_estimate=cost(1, 1),
        compiler_params=pltpu.CompilerParams(vmem_limit_bytes=8 * MEGA),
        name="shrink",
    )(active, shrink, normal, *first, settle, *second)


def contrast_kernel(
    flag_ref,
    start_ref,
    every_ref,
    column_ref,
    normal_ref,
    inverse_ref,
    cotangent_ref,
    gain_ref,
    two_ref,
    low_ref,
    sums_ref,
    summary_ref,
    rows_ref,
):
    width = normal_ref.shape[1]
    slots = start_ref.shape[0]
    devices = every_ref.shape[0]
    step = pl.program_id(0)
    sharpness = SHARPNESS_DIVISOR / math.sqrt(width)

    def flat(which, at, count):
        return every_ref[pl.ds(at, count), which].reshape(count * slots, width + LANES)

    def logits_of(questions, passages):
        return jnp.where(
            column_ref[...] >= 0, dot_rows(questions, passages) * sharpness, HIDDEN_SCORE
        )

    def targets_of(rows):
        digits = rows[:, width:].astype(FLOAT_KIND)
        return (digits[:, 0:1] * LANES + digits[:, 1:2]).astype(jnp.int32)

    @pl.when(step == 0)
    def _():
        sums_ref[...] = jnp.zeros_like(sums_ref)

        @pl.when(flag_ref[ENC] == 0)
        def _():
            own = every_ref[0, 0]
            passages = flat(1, 0, devices)[:, :width]
            logits = logits_of(own[:, :width], passages)
            top = jnp.max(logits, axis=1, keepdims=True)
            raised = jnp.exp(logits - top)
            probability = raised / jnp.sum(raised, axis=1, keepdims=True)
            hit = (column_ref[...] == targets_of(own)).astype(FLOAT_KIND)
            gradient = (LOSS_WEIGHT * (probability - hit)).astype(BRAIN)
            summary_ref[...] = dot(gradient, passages) * sharpness

        @pl.when(flag_ref[ENC] == 1)
        def _():
            passages = flat(0, 0, devices)[:, :width]
            block = 16

            def part(at):
                rows = flat(1, at, block)
                questions = rows[:, :width]
                logits = logits_of(questions, passages)
                top = jnp.max(logits, axis=1, keepdims=True)
                total = jnp.sum(jnp.exp(logits - top), axis=1, keepdims=True)
                probability = jnp.exp(logits[:, :LANES] - top) / total
                hit = (column_ref[:, :LANES] == targets_of(rows)).astype(FLOAT_KIND)
                gradient = (LOSS_WEIGHT * (probability - hit)).astype(BRAIN)
                return dot_columns(gradient, questions)[:slots] * sharpness

            if devices == block:
                summary_ref[...] = part(0)
            else:
                summary_ref[...] = jnp.zeros_like(summary_ref)

                @pl.loop(0, devices // block)
                def _(k):
                    summary_ref[...] += part(k * block)

    rows_ref[...] = wide(cotangent_ref)
    tiles = rows_ref.shape[0] // TILE
    first = lax.broadcasted_iota(jnp.int32, (TILE, 1), 0) == 0
    for slot in range(slots):
        start = jnp.where(flag_ref[ENC] == 1, start_ref[slot], slot * QLEN)
        local = start // TILE - step * tiles
        inside = (local >= 0) & (local < tiles)
        at = pl.multiple_of(jnp.clip(local, 0, tiles - 1) * TILE, TILE)
        rows_ref[pl.ds(at, TILE), :] += jnp.where(
            first & inside, summary_ref[slot : slot + 1, :], 0.0
        )
    gradient = rows_ref[...]
    normal = normal_ref[...]
    sums_ref[0:1] += row_sum(gradient * normal)
    sums_ref[1:2] += row_sum(gradient)
    two = norm_backward(gradient, normal, inverse_ref[...], wide(gain_ref))
    two_ref[...] = two
    low = two.astype(BRAIN)
    low_ref[...] = low
    sums_ref[2:3] += row_sum(low.astype(FLOAT_KIND))


def contrast(enc, starts, every, columns, normal, inverse, cotangent, gain, tm=256):
    count, width = normal.shape
    slots = starts.shape[0]
    return pl.pallas_call(
        contrast_kernel,
        grid_spec=pltpu.PrefetchScalarGridSpec(
            num_scalar_prefetch=2,
            grid=(count // tm,),
            in_specs=[
                whole(every.shape),
                whole(columns.shape),
                row_block(tm, width),
                row_block(tm, 1),
                row_block(tm, width),
                whole(gain.shape),
            ],
            out_specs=[row_block(tm, width), row_block(tm, width), whole((TILE, width))],
            scratch_shapes=[
                pltpu.VMEM((slots, width), FLOAT_KIND),
                pltpu.VMEM((tm, width), FLOAT_KIND),
            ],
        ),
        out_shape=[
            jax.ShapeDtypeStruct((count, width), FLOAT_KIND),
            jax.ShapeDtypeStruct((count, width), BRAIN),
            jax.ShapeDtypeStruct((TILE, width), FLOAT_KIND),
        ],
        cost_estimate=cost(1, 1),
        compiler_params=pltpu.CompilerParams(vmem_limit_bytes=8 * MEGA),
        name="contrast",
    )(enc, starts, every, columns, normal, inverse, cotangent, gain)


def contraction_kernel(flag_ref, low_ref, active_ref, *refs):
    turned_ref = refs[-1]
    step = pl.program_id(0)

    @pl.when(step == 0)
    def _():
        turned_ref[...] = low_ref[...].T

    value = dot(turned_ref[...], active_ref[...]).astype(BRAIN)
    for piece, out_ref in enumerate(refs[:-1]):

        @pl.when(step == piece)
        def _():
            out_ref[...] = value


def contraction_half(side, active, low, weight=1):
    count, hidden = active.shape
    width = low.shape[1]
    rows = width // 2
    tn = hidden // PIECES
    return pl.pallas_call(
        contraction_kernel,
        grid_spec=pltpu.PrefetchScalarGridSpec(
            num_scalar_prefetch=1,
            grid=(PIECES,),
            in_specs=[
                pl.BlockSpec((count, rows), lambda i, flag: (0, flag[0])),
                pl.BlockSpec((count, tn), lambda i, flag: (0, i)),
            ],
            out_specs=[whole((rows, tn))] * PIECES,
            scratch_shapes=[pltpu.VMEM((rows, count), BRAIN)],
        ),
        out_shape=[jax.ShapeDtypeStruct((rows, tn), BRAIN)] * PIECES,
        cost_estimate=cost(weight, 1),
        compiler_params=pltpu.CompilerParams(vmem_limit_bytes=8 * MEGA),
        name="contraction_half",
    )(side, low, active)


def feed_kernel(
    flag_ref,
    two_low_ref,
    shrink_ref,
    slope_ref,
    low_ref,
    expand_ref,
    two_ref,
    lift_ref,
    first_ref,
    *refs,
):
    pieces, turned_ref = refs[:-1], refs[-1]
    rows = turned_ref.shape[1]
    step = pl.program_id(0)

    @pl.when(step == 0)
    def _():
        first_ref[...] = two_ref[...]
        for side in range(2):

            @pl.when(flag_ref[SEND] == side)
            def _():
                turned_ref[0] = low_ref[:, side * rows : (side + 1) * rows].T
                turned_ref[1] = low_ref[:, (1 - side) * rows : (2 - side) * rows].T

    hidden = dot_rows(two_low_ref[...], shrink_ref[...]) * wide(slope_ref)
    low = hidden.astype(BRAIN)
    lift_ref[...] = row_sum(low.astype(FLOAT_KIND))
    first_ref[...] += dot_rows(low, expand_ref[...])
    for side in range(2):
        value = dot(turned_ref[side], low).astype(BRAIN)
        for piece in range(PIECES):

            @pl.when(step == piece)
            def _():
                pieces[side * PIECES + piece][...] = value


def feed_back(flags, two_low, shrink, slope, low, expand, two, weight=1):
    count, width = two.shape
    hidden = shrink.shape[0]
    rows = width // 2
    tn = hidden // PIECES
    column = lambda rows: pl.BlockSpec((rows, tn), lambda i, *_: (0, i))
    return pl.pallas_call(
        feed_kernel,
        grid_spec=pltpu.PrefetchScalarGridSpec(
            num_scalar_prefetch=1,
            grid=(PIECES,),
            in_specs=[
                whole((count, width)),
                row_block(tn, width),
                column(count),
                whole((count, width)),
                column(width),
                whole((count, width)),
            ],
            out_specs=[column(1), whole((count, width))] + [whole((rows, tn))] * 2 * PIECES,
            scratch_shapes=[pltpu.VMEM((2, rows, count), BRAIN)],
        ),
        out_shape=[
            jax.ShapeDtypeStruct((1, hidden), FLOAT_KIND),
            jax.ShapeDtypeStruct((count, width), FLOAT_KIND),
        ]
        + [jax.ShapeDtypeStruct((rows, tn), BRAIN)] * 2 * PIECES,
        cost_estimate=cost(weight, 1),
        compiler_params=pltpu.CompilerParams(vmem_limit_bytes=14 * MEGA),
        name="feed_back",
    )(flags, two_low, shrink, slope, low, expand, two)


def attend_back_kernel(
    first_ref,
    normal_ref,
    inverse_ref,
    gain_ref,
    merge_ref,
    packed_ref,
    weight_ref,
    one_ref,
    low_ref,
    packed_gradient_ref,
    sums_ref,
    packed_sums_ref,
    context_gradient_ref,
):
    width = normal_ref.shape[1]

    @pl.when(pl.program_id(0) == 0)
    def _():
        sums_ref[...] = jnp.zeros_like(sums_ref)
        packed_sums_ref[...] = jnp.zeros_like(packed_sums_ref)

    gradient = first_ref[...]
    normal = normal_ref[...]
    sums_ref[0:1] += row_sum(gradient * normal)
    sums_ref[1:2] += row_sum(gradient)
    one = norm_backward(gradient, normal, inverse_ref[...], wide(gain_ref))
    one_ref[...] = one
    low = one.astype(BRAIN)
    low_ref[...] = low
    sums_ref[2:3] += row_sum(low.astype(FLOAT_KIND))
    context_gradient_ref[...] = dot_rows(low, merge_ref[...]).astype(BRAIN)
    low_row = lax.broadcasted_iota(jnp.int32, (LANES, 1), 0) < HEAD
    scale = 1.0 / math.sqrt(HEAD)
    for pair in range(width // LANES):
        at = LANES * pair
        queries = both_heads(packed_ref[:, at : at + LANES] * scale)
        keys = packed_ref[:, width + at : width + at + LANES] * scale
        values = packed_ref[:, 2 * width + at : 2 * width + at + LANES]
        outer = both_heads(context_gradient_ref[:, at : at + LANES])
        weights = weight_ref[pair]
        probability = weights.astype(FLOAT_KIND)
        inner = dot_rows(values, outer)
        scores = (probability * (inner - row_sum(probability * inner))).astype(BRAIN)
        turned = dot(keys.T, scores)
        found = (
            jnp.where(low_row, turned[:, :ROWS], turned[:, ROWS:]).T,
            dot(scores, queries),
            dot(weights, outer),
        )
        for part in range(3):
            columns = slice(part * width + at, part * width + at + LANES)
            packed_gradient_ref[:, columns] = found[part].astype(BRAIN)
    packed_sums_ref[...] += row_sum(wide(packed_gradient_ref))


def attend_back(first, normal, inverse, gain, merge, packed, weights, weight=1):
    count, width = normal.shape
    heads = width // HEAD
    return pl.pallas_call(
        attend_back_kernel,
        grid=(count // ROWS,),
        in_specs=[
            row_block(ROWS, width),
            row_block(ROWS, width),
            row_block(ROWS, 1),
            whole(gain.shape),
            whole(merge.shape),
            row_block(ROWS, 3 * width),
            pl.BlockSpec((None, heads // 2, ROWS, 2 * ROWS), lambda i: (i, 0, 0, 0)),
        ],
        out_specs=[
            row_block(ROWS, width),
            row_block(ROWS, width),
            row_block(ROWS, 3 * width),
            whole((TILE, width)),
            whole((1, 3 * width)),
        ],
        out_shape=[
            jax.ShapeDtypeStruct((count, width), FLOAT_KIND),
            jax.ShapeDtypeStruct((count, width), BRAIN),
            jax.ShapeDtypeStruct((count, 3 * width), BRAIN),
            jax.ShapeDtypeStruct((TILE, width), FLOAT_KIND),
            jax.ShapeDtypeStruct((1, 3 * width), FLOAT_KIND),
        ],
        scratch_shapes=[pltpu.VMEM((ROWS, width), BRAIN)],
        cost_estimate=cost(weight, 1),
        compiler_params=pltpu.CompilerParams(vmem_limit_bytes=11 * MEGA),
        name="attend_back",
    )(first, normal, inverse, gain, merge, packed, weights)


def merge_project_kernel(flag_ref, context_ref, one_ref, x_ref, packed_ref, *refs):
    pieces, turned_ref = refs[:-1], refs[-1]
    step = pl.program_id(0)

    @pl.when(step == 0)
    def _():
        turned_ref[...] = context_ref[...].T
        pieces[0][...] = dot(turned_ref[...], one_ref[...]).astype(BRAIN)
        turned_ref[...] = x_ref[...].T

    @pl.when(step > 0)
    def _():
        value = dot(turned_ref[...], packed_ref[...]).astype(BRAIN)
        for piece in range(1, PIECES):

            @pl.when(step == piece)
            def _():
                pieces[piece][...] = value


def merge_project_half(side, context, one, x, packed, weight=1):
    count, width = x.shape
    rows = width // 2
    return pl.pallas_call(
        merge_project_kernel,
        grid_spec=pltpu.PrefetchScalarGridSpec(
            num_scalar_prefetch=1,
            grid=(PIECES,),
            in_specs=[
                pl.BlockSpec((count, rows), lambda i, flag: (0, flag[0])),
                whole((count, width)),
                pl.BlockSpec((count, rows), lambda i, flag: (0, flag[0])),
                pl.BlockSpec((count, width), lambda i, flag: (0, jnp.maximum(i - 1, 0))),
            ],
            out_specs=[whole((rows, width))] * PIECES,
            scratch_shapes=[pltpu.VMEM((rows, count), BRAIN)],
        ),
        out_shape=[jax.ShapeDtypeStruct((rows, width), BRAIN)] * PIECES,
        cost_estimate=cost(weight, 1),
        compiler_params=pltpu.CompilerParams(vmem_limit_bytes=10 * MEGA),
        name="merge_project_half",
    )(side, context, one, x, packed)


def fold_kernel(flag_ref, *refs, count, side):
    keep, other, outs = refs[:count], refs[count : 2 * count], refs[2 * count :]
    rows = outs[0].shape[0]
    columns = outs[0].shape[1] // count
    for out_ref, half in zip(outs, (1 - flag_ref[side], flag_ref[side])):

        @pl.loop(0, rows // PACKED)
        def _(block):
            to = pl.ds(pl.multiple_of(block * PACKED, PACKED), PACKED)
            at = pl.ds(pl.multiple_of(half * rows + block * PACKED, PACKED), PACKED)
            for piece in range(count):
                total = wide(keep[piece].at[at]) + wide(other[piece].at[at])
                out_ref[to, piece * columns : (piece + 1) * columns] = total.astype(BRAIN)


def folded(flags, place, keep, other, weight):
    rows, columns = keep[0].shape
    count = len(keep)
    if rows % (2 * PACKED):
        (mine,), (theirs,) = keep, other
        bit = flags[place]
        return part_sum(mine, theirs, 1 - bit), part_sum(mine, theirs, bit)
    shape = jax.ShapeDtypeStruct((rows // 2, count * columns), BRAIN)
    return pl.pallas_call(
        functools.partial(fold_kernel, count=count, side=place),
        grid_spec=pltpu.PrefetchScalarGridSpec(
            num_scalar_prefetch=1,
            grid=(1,),
            in_specs=[whole((rows, columns))] * 2 * count,
            out_specs=[whole(shape.shape)] * 2,
        ),
        out_shape=[shape, shape],
        cost_estimate=cost(weight, 1),
        compiler_params=pltpu.CompilerParams(vmem_limit_bytes=5 * MEGA),
        name="fold",
    )(flags, *keep, *other)


def add_kernel(mine_ref, other_ref, out_ref):
    out_ref[...] = (wide(mine_ref) + wide(other_ref)).astype(out_ref.dtype)


def added(mine, other, weight=1):
    return pl.pallas_call(
        add_kernel,
        out_shape=jax.ShapeDtypeStruct(mine.shape, mine.dtype),
        cost_estimate=cost(weight, 1),
        compiler_params=pltpu.CompilerParams(vmem_limit_bytes=2 * MEGA),
        name="add",
    )(mine, other)


def join_kernel(flag_ref, mine_ref, other_ref, out_ref, *, side):
    rows = mine_ref.shape[0]
    out_ref[pl.ds(pl.multiple_of(flag_ref[side] * rows, rows), rows), :] = mine_ref[...]
    out_ref[pl.ds(pl.multiple_of((1 - flag_ref[side]) * rows, rows), rows), :] = other_ref[...]


def joined(flags, place, mine, other, weight):
    rows, columns = mine.shape
    if rows % PACKED:
        return joined_by_bit(mine, other, flags[place])
    return pl.pallas_call(
        functools.partial(join_kernel, side=place),
        grid_spec=pltpu.PrefetchScalarGridSpec(
            num_scalar_prefetch=1,
            grid=(1,),
            in_specs=[whole(mine.shape)] * 2,
            out_specs=whole((2 * rows, columns)),
        ),
        out_shape=jax.ShapeDtypeStruct((2 * rows, columns), BRAIN),
        cost_estimate=cost(weight, 1),
        compiler_params=pltpu.CompilerParams(vmem_limit_bytes=4 * MEGA),
        name="join",
    )(flags, mine, other)


def tokens_kernel(one_ref, packed_ref, project_ref, out_ref):
    out_ref[...] = one_ref[...] + dot_rows(packed_ref[...], project_ref[...])


def tokens_back(one, packed, project, tm=256, weight=1):
    count, width = one.shape
    return pl.pallas_call(
        tokens_kernel,
        grid=(count // tm,),
        in_specs=[row_block(tm, width), row_block(tm, 3 * width), whole(project.shape)],
        out_specs=row_block(tm, width),
        out_shape=jax.ShapeDtypeStruct((count, width), FLOAT_KIND),
        cost_estimate=cost(weight, 1),
        compiler_params=pltpu.CompilerParams(vmem_limit_bytes=13 * MEGA),
        name="tokens_back",
    )(one, packed, project)


def pack_kernel(packed_ref, attend_ref, lift_ref, output_ref, out_ref):
    width = attend_ref.shape[1]
    out_ref[...] = jnp.zeros_like(out_ref)
    out_ref[0:1] = packed_ref[:, :width]
    out_ref[1:2] = packed_ref[:, 2 * width :]
    out_ref[2:5] = attend_ref[0:3]
    for part in range(4):
        out_ref[5 + part : 6 + part] = lift_ref[:, part * width : (part + 1) * width]
    out_ref[9:12] = output_ref[0:3]


def pack_vectors(packed_sums, attend_sums, lift_sums, output_sums):
    width = attend_sums.shape[1]
    return pl.pallas_call(
        pack_kernel,
        out_shape=jax.ShapeDtypeStruct((16, width), FLOAT_KIND),
        cost_estimate=cost(1, 1),
        compiler_params=pltpu.CompilerParams(vmem_limit_bytes=2 * MEGA),
        name="pack_vectors",
    )(packed_sums, attend_sums, lift_sums, output_sums)


def unpack_kernel(mine_ref, other_ref, offset_ref, adjust_ref, scale_ref, center_ref, lift_ref, settle_ref, rescale_ref, recenter_ref):
    width = mine_ref.shape[1]
    total = mine_ref[...] + other_ref[...]
    offset_ref[:, :width] = total[0:1]
    offset_ref[:, width:] = total[1:2]
    scale_ref[...] = total[2:3]
    center_ref[...] = total[3:4]
    adjust_ref[...] = total[4:5]
    for part in range(4):
        lift_ref[:, part * width : (part + 1) * width] = total[5 + part : 6 + part]
    rescale_ref[...] = total[9:10]
    recenter_ref[...] = total[10:11]
    settle_ref[...] = total[11:12]


def unpack_vectors(mine, other):
    width = mine.shape[1]
    shapes = [2, 1, 1, 1, 4, 1, 1, 1]
    return pl.pallas_call(
        unpack_kernel,
        out_shape=[jax.ShapeDtypeStruct((1, k * width), FLOAT_KIND) for k in shapes],
        cost_estimate=cost(1, 1),
        compiler_params=pltpu.CompilerParams(vmem_limit_bytes=2 * MEGA),
        name="unpack_vectors",
    )(mine, other)


def place_kernel(flag_ref, value_ref, *refs, kept):
    at = 0
    for out_ref in refs[kept:]:
        columns = out_ref.shape[1]
        out_ref[...] = value_ref[:, at : at + columns].astype(FLOAT_KIND)
        at += columns


def place_half(flags, side, value, columns, before, tm=192):
    rows = value.shape[0]
    steps = rows // tm
    kept = [] if before is None else list(before)
    return pl.pallas_call(
        functools.partial(place_kernel, kept=len(kept)),
        grid_spec=pltpu.PrefetchScalarGridSpec(
            num_scalar_prefetch=1,
            grid=(steps,),
            in_specs=[row_block(tm, value.shape[1])]
            + [pl.BlockSpec(memory_space=pl.ANY)] * len(kept),
            out_specs=[
                pl.BlockSpec((tm, size), lambda i, flag: (flag[side] * steps + i, 0))
                for size in columns
            ],
        ),
        out_shape=[jax.ShapeDtypeStruct((2 * rows, size), FLOAT_KIND) for size in columns],
        input_output_aliases={2 + k: k for k in range(len(kept))},
        cost_estimate=cost(1, 1),
        compiler_params=pltpu.CompilerParams(vmem_limit_bytes=10 * MEGA),
        name="place_half",
    )(flags, value, *kept)


def place_turned_kernel(flag_ref, value_ref, *refs):
    refs[-1][...] = value_ref[...].astype(FLOAT_KIND).T


def place_turned_half(flags, side, value, before, tm=1536):
    rows, columns = value.shape
    kept = [] if before is None else list(before)
    return pl.pallas_call(
        place_turned_kernel,
        grid_spec=pltpu.PrefetchScalarGridSpec(
            num_scalar_prefetch=1,
            grid=(columns // tm,),
            in_specs=[pl.BlockSpec((rows, tm), lambda i, flag: (0, i))]
            + [pl.BlockSpec(memory_space=pl.ANY)] * len(kept),
            out_specs=[pl.BlockSpec((tm, rows), lambda i, flag: (i, flag[side]))],
        ),
        out_shape=[jax.ShapeDtypeStruct((columns, 2 * rows), FLOAT_KIND)],
        input_output_aliases={2 + k: k for k in range(len(kept))},
        cost_estimate=cost(1, 1),
        compiler_params=pltpu.CompilerParams(vmem_limit_bytes=14 * MEGA),
        name="place_turned_half",
    )(flags, value, *kept)


def swapped(value, axis, apart):
    mask = 2**apart
    pairs = [(source, source ^ mask) for source in range(lax.axis_size(axis))]
    return lax.ppermute(value, axis, pairs)


def swapped_by_core(value, stage):
    count = lax.axis_size("batch")
    pairs = [(source, source ^ (1 << stage[source & 1])) for source in range(count)]
    return lax.ppermute(value, "batch", pairs)


def bit_count(axis):
    return lax.axis_size(axis).bit_length() - 1


def to_low(values):
    return values.astype(BRAIN)


def part_sum(mine, other, bit):
    half = mine.shape[0] // 2
    left = lax.dynamic_slice_in_dim(mine, bit * half, half, 0).astype(FLOAT_KIND)
    right = lax.dynamic_slice_in_dim(other, bit * half, half, 0).astype(FLOAT_KIND)
    return to_low(left + right)


def joined_by_bit(mine, other, bit):
    low_part = jnp.where(bit == 0, mine, other)
    high_part = jnp.where(bit == 0, other, mine)
    return jnp.concatenate([low_part, high_part], axis=0)


class Sequence:
    def __init__(self):
        self.last = None

    def run(self, step, *inputs):
        if self.last is not None:
            *inputs, _ = lax.optimization_barrier((*inputs, self.last))
        result = step(*inputs)
        self.last = jax.tree.leaves(result)[0]
        return result


class Reduction:
    def __init__(self, sequence, flags, stages, at, put):
        self.run = sequence.run
        self.flags = flags
        self.stages = stages
        self.at = at
        self.put = put
        count = len(stages)
        self.steps = [functools.partial(self.scatter, k) for k in range(count)]
        self.steps.append(self.finish)
        self.steps += [functools.partial(self.gather, k) for k in reversed(range(count))]
        self.steps.append(self.place)

    def advance(self, weight=1):
        self.steps.pop(0)(weight)

    def begin(self, send, keep):
        self.keep = list(keep)
        self.other = [swapped(piece, "batch", 0) for piece in send]

    def scatter(self, stage, weight):
        count = len(self.keep)
        send, keep = self.run(
            lambda *v: folded(self.flags, self.at + stage, v[:count], v[count:], weight),
            *self.keep,
            *self.other,
        )
        self.keep = [keep]
        self.other = [swapped_by_core(send, self.stages[stage])]

    def finish(self, weight):
        self.value = self.run(lambda a, b: added(a, b, weight), *self.keep, *self.other)
        self.other = swapped_by_core(self.value, self.stages[-1])

    def gather(self, stage, weight):
        self.value = self.run(
            lambda v, o: joined(self.flags, self.at + stage, v, o, weight), self.value, self.other
        )
        if stage > 0:
            self.other = swapped_by_core(self.value, self.stages[stage - 1])
            return
        self.other = swapped(self.value, "batch", 0)
        self.placed = self.run(lambda v: self.put(self.flags, KEEP, v, None), self.value)

    def place(self, weight):
        self.total = self.run(
            lambda o, *p: self.put(self.flags, SEND, o, p), self.other, *self.placed
        )


def shards(
    tokens,
    cotangent,
    projection,
    offsets,
    merger,
    adjust,
    scaling,
    centering,
    expansion,
    lifting,
    contraction,
    settling,
    rescale,
    recenter,
    segments,
    passage_starts,
    passage_counts,
    positives,
):
    index = lax.axis_index("batch").astype(jnp.int32)
    slots = passage_starts.shape[0]
    bits = bit_count("batch")
    plain = [(apart, apart) for apart in range(1, bits)]
    mixed = [(apart, other) for (apart, _), (other, _) in zip(plain, plain[1:] + plain[:1])]
    kinds = (plain, mixed, [(odd, even) for even, odd in mixed])
    flags = jnp.stack(
        [lax.axis_index("enc").astype(jnp.int32), index & 1, 1 - (index & 1)]
        + [
            (index >> jnp.where(index & 1 == 0, even, odd)) & 1
            for stages in kinds
            for even, odd in stages
        ]
    )
    order = list(reversed(range(bits)))
    place = jnp.arange(lax.axis_size("batch"), dtype=jnp.int32)
    away = sum(((place >> k) & 1) << apart for k, apart in enumerate(order))
    device = (index ^ away)[:, None]
    slot = jnp.arange(slots, dtype=jnp.int32)[None, :]
    held = jnp.sum(jnp.where(device == place[None, :], passage_counts[None, :], 0), axis=1)
    columns = jnp.where(slot < held[:, None], device * slots + slot, -1).reshape(1, -1)
    keep_side = (index & 1)[None]
    flags, keep_side, send_side, columns, tokens = lax.optimization_barrier(
        (flags, keep_side, 1 - keep_side, columns, tokens)
    )
    width = tokens.shape[2]
    x, project, merge, expand, shrink, outer = (
        in_hbm(tokens[0]),
        in_hbm(projection[0]),
        in_hbm(merger[0]),
        expansion[0],
        in_hbm(contraction[0]),
        in_hbm(cotangent[0]),
    )
    first = (in_hbm(scaling), in_hbm(centering))
    second = (in_hbm(rescale), in_hbm(recenter))
    adjust, lifting, settling, offsets = (
        in_hbm(v) for v in (adjust, lifting, settling, offsets)
    )

    sequence = Sequence()
    run = sequence.run
    packed, weights, context, normal_one, inverse_one, low = attend(
        flags, x, project, offsets, in_hbm(segments[None]), merge, adjust, *first
    )
    parcel = summarize(
        flags,
        passage_starts,
        positives,
        normal_one,
        first,
        expand,
        lifting,
        shrink,
        settling,
        second,
    )
    sequence.last = parcel
    parts = 4
    every = parcel[None]
    other = swapped(parcel, "enc", 0)[None]
    wide_pair = run(lambda v: widen(0, parts, v, expand, lifting, None), low)
    every = run(lambda a, b: jnp.stack([a, b], axis=1), every, other)
    for part, apart in enumerate(order, 1):
        other = swapped(every, "batch", apart)
        if part < parts:
            wide_pair = run(
                lambda v, *p: widen(part, parts, v, expand, lifting, p), low, *wide_pair
            )
        elif part == parts:
            active, slope = wide_pair
            normal_two, inverse_two, encoded = run(
                lambda a, n: shrink_back_to_width(a, contraction[0], n, first, settling, second),
                active,
                normal_one,
            )
        every = run(lambda a, b: jnp.concatenate([a, b], axis=0), every, other)
    two, two_low, output_sums = run(
        lambda *v: contrast(flags, passage_starts, *v, outer, second[0]),
        every,
        columns,
        normal_two,
        inverse_two,
    )

    puts = (
        place_turned_half,
        lambda f, s, v, p: place_half(f, s, v, (expansion.shape[2],), p),
        lambda f, s, v, p: place_half(f, s, v, (width, projection.shape[2]), p),
    )
    shrink_sum, expand_sum, project_sum = (
        Reduction(sequence, flags, kinds[kind], STAGES + kind * len(plain), put)
        for kind, put in zip(LINKS, puts)
    )
    product = lambda side: run(
        lambda c, o, p: merge_project_half(side, c, o, x, p, weight),
        context,
        one_low,
        packed_gradient,
    )
    vectors = []
    apart = 0
    for step in PLAN:
        weight = LEVELS[int(step[1:] or 0)]
        kind = step[0]
        if kind == "C":
            send = run(lambda a, t: contraction_half(send_side, a, t, weight), active, two_low)
            keep = run(lambda a, t: contraction_half(keep_side, a, t, weight), active, two_low)
            shrink_sum.begin(send, keep)
        elif kind == "F":
            lift_sums, gradient_first, *both = run(
                lambda t, s, g: feed_back(flags, t, shrink, s, low, expand, g, weight),
                two_low,
                slope,
                two,
            )
            expand_sum.begin(both[:PIECES], both[PIECES:])
        elif kind == "A":
            one, one_low, packed_gradient, attend_sums, packed_sums = run(
                lambda g, n, i, p, w: attend_back(g, n, i, first[0], merge, p, w, weight),
                gradient_first,
                normal_one,
                inverse_one,
                packed,
                weights,
            )
        elif kind == "S":
            send = product(send_side)
        elif kind == "K":
            keep = product(keep_side)
            project_sum.begin(send, keep)
        elif kind == "T":
            tokens_gradient = run(lambda o, p: tokens_back(o, p, project, weight=weight), one, packed_gradient)
        elif kind == "P":
            vectors = [run(pack_vectors, packed_sums, attend_sums, lift_sums, output_sums)]
            vectors.append(swapped(vectors[0], "batch", apart))
        elif kind == "v":
            apart += 1
            vectors = [run(lambda a, b, w=weight: added(a, b, w), *vectors)]
            vectors.append(swapped(vectors[0], "batch", apart))
        else:
            {"c": shrink_sum, "e": expand_sum, "m": project_sum}[kind].advance(weight)
    while apart < bits - 1:
        apart += 1
        vectors = [run(added, *vectors)]
        vectors.append(swapped(vectors[0], "batch", apart))
    vector_totals = run(unpack_vectors, *vectors)
    for reduction in (shrink_sum, expand_sum, project_sum):
        while reduction.steps:
            reduction.advance()
    (total_contraction,) = shrink_sum.total
    (total_expansion,) = expand_sum.total
    total_merger, total_projection = project_sum.total
    (
        total_offsets,
        total_adjust,
        total_scaling,
        total_centering,
        total_lifting,
        total_settling,
        total_rescale,
        total_recenter,
    ) = vector_totals
    return (
        encoded[None],
        tokens_gradient[None],
        total_projection[None],
        total_offsets,
        total_merger[None],
        total_adjust,
        total_scaling,
        total_centering,
        total_expansion[None],
        total_lifting,
        total_contraction[None],
        total_settling,
        total_rescale,
        total_recenter,
    )


def solution(mesh):
    matrix = P("enc", None, None)
    vector = P("enc", None)
    rows = P("enc", "batch", None)
    return jax.shard_map(
        shards,
        mesh=mesh,
        in_specs=(
            rows,
            rows,
            matrix,
            vector,
            matrix,
            vector,
            vector,
            vector,
            matrix,
            vector,
            matrix,
            vector,
            vector,
            vector,
            P("batch"),
            P("batch"),
            P(),
            P("batch"),
        ),
        out_specs=(
            rows,
            rows,
            matrix,
            vector,
            matrix,
            vector,
            vector,
            vector,
            matrix,
            vector,
            matrix,
            vector,
            vector,
            vector,
        ),
        check_vma=False,
    )
```

```python
import functools
import math

import jax
import jax.numpy as jnp
from jax import lax
from jax.experimental import pallas as pl
from jax.experimental.pallas import tpu as pltpu
from jax.sharding import PartitionSpec as P

QLEN = 64
ROWS = 256
HEAD = 64
TILE = 8
LANES = 128
PIECES = 4
PACKED = 16
PLAN = (
    "C4", "c", "F2", "c", "e4", "A2", "c", "S3", "e3", "c2", "P", "K3",
    "m1", "e3", "T", "v", "c3", "e2", "m3", "c3", "m1", "e", "m1", "c1",
    "m3", "e", "v1", "m1", "c", "e", "v", "m", "e2", "m4",
)
LINKS = (2, 2, 2)
LEVELS = (1, 2 * 10**9, 6 * 10**9, 2 * 10**10, 10**11)
ENC, KEEP, SEND, STAGES = 0, 1, 2, 3
MEGA = 2**20
EPSILON = 1e-12
SHARPNESS_DIVISOR = 2.0
LOSS_WEIGHT = 2.0
HIDDEN_SCORE = -1e30
FLOAT_KIND = jnp.float32
BRAIN = jnp.bfloat16

TAIL = tuple(
    0.5 * a for a in (0.254829592, -0.284496736, 1.421413741, -1.453152027, 1.061405429)
)
TAIL_SLOPE = 0.3275911 / math.sqrt(2.0)
DENSITY = 1.0 / math.sqrt(2.0 * math.pi)


def dot(left, right):
    return jnp.dot(left, right, preferred_element_type=FLOAT_KIND)


def dot_rows(left, right):
    return lax.dot_general(left, right, (((1,), (1,)), ((), ())), preferred_element_type=FLOAT_KIND)


def dot_columns(left, right):
    return lax.dot_general(left, right, (((0,), (0,)), ((), ())), preferred_element_type=FLOAT_KIND)


def whole(shape):
    return pl.BlockSpec(shape, lambda *_: (0,) * len(shape))


def row_block(rows, columns):
    return pl.BlockSpec((rows, columns), lambda i, *_: (i, 0))


def in_hbm(value):
    return pltpu.with_memory_space_constraint(value, pltpu.HBM)


def hbm_shape(shape, dtype):
    return pltpu.HBM(shape, dtype)


def cost(flops, moved, transcendentals=0):
    return pl.CostEstimate(flops=flops, bytes_accessed=1, transcendentals=0)


def wide(ref):
    return ref[...].astype(FLOAT_KIND)


def row_sum(values):
    return jnp.sum(values, axis=0, keepdims=True)


def normalized(values):
    centered = values - jnp.mean(values, axis=1, keepdims=True)
    spread = jnp.mean(centered * centered, axis=1, keepdims=True)
    scale = lax.rsqrt(spread + EPSILON)
    return centered * scale, scale


def norm_backward(gradient, normal, inverse, gain):
    scaled = gradient * gain
    return (
        scaled
        - jnp.mean(scaled, axis=1, keepdims=True)
        - normal * jnp.mean(scaled * normal, axis=1, keepdims=True)
    ) * inverse


def both_heads(values):
    low_lane = lax.broadcasted_iota(jnp.int32, (1, LANES), 1) < HEAD
    nothing = jnp.zeros_like(values)
    return jnp.concatenate(
        [jnp.where(low_lane, values, nothing), jnp.where(low_lane, nothing, values)], axis=0
    )


def gelu_and_slope(hidden):
    bell = jnp.exp(hidden * hidden * -0.5)
    t = 1.0 / (1.0 + TAIL_SLOPE * jnp.abs(hidden))
    series = TAIL[3] + t * TAIL[4]
    series = TAIL[2] + t * series
    series = TAIL[1] + t * series
    series = TAIL[0] + t * series
    tail = t * series * bell
    below = jnp.where(hidden < 0.0, tail, 1.0 - tail)
    return hidden * below, below + hidden * bell * DENSITY


def attend_kernel(
    flag_ref,
    x_ref,
    project_ref,
    offset_ref,
    segment_ref,
    merge_ref,
    adjust_ref,
    gain_ref,
    shift_ref,
    packed_ref,
    weight_ref,
    context_ref,
    normal_ref,
    inverse_ref,
    low_ref,
):
    width = x_ref.shape[1]
    x = x_ref[...]
    for part in range(3):
        columns = slice(part * width, (part + 1) * width)
        sums = dot(x, project_ref[:, columns])
        if part != 1:
            at = 0 if part == 0 else width
            sums = sums + offset_ref[:, at : at + width].astype(FLOAT_KIND)
        packed_ref[:, columns] = sums.astype(BRAIN)
    position = lax.broadcasted_iota(jnp.int32, (1, ROWS), 1)
    marks = jnp.where(flag_ref[ENC] == 1, segment_ref[...], position // QLEN).astype(FLOAT_KIND)
    spread_marks = jnp.broadcast_to(marks, (ROWS, ROWS))
    hide = jnp.where(spread_marks == spread_marks.T, 0.0, HIDDEN_SCORE)
    hide = jnp.concatenate([hide, hide], axis=0)
    low_lane = lax.broadcasted_iota(jnp.int32, (1, LANES), 1) < HEAD
    scale = 1.0 / math.sqrt(HEAD)
    for pair in range(width // LANES):
        at = LANES * pair
        queries = both_heads(packed_ref[:, at : at + LANES] * scale)
        keys = packed_ref[:, width + at : width + at + LANES]
        values = packed_ref[:, 2 * width + at : 2 * width + at + LANES]
        scores = dot_rows(queries, keys) + hide
        raised = jnp.exp(scores - jnp.max(scores, axis=1, keepdims=True))
        weights = (raised * (1.0 / jnp.sum(raised, axis=1, keepdims=True))).astype(BRAIN)
        weight_ref[pair] = weights.T
        context = dot(weights, values)
        context = jnp.where(low_lane, context[:ROWS], context[ROWS:])
        context_ref[:, at : at + LANES] = context.astype(BRAIN)
    attended = dot(context_ref[...], merge_ref[...]) + wide(adjust_ref)
    normal, inverse = normalized(x.astype(FLOAT_KIND) + attended)
    normal_ref[...] = normal
    inverse_ref[...] = inverse
    low_ref[...] = (normal * wide(gain_ref) + wide(shift_ref)).astype(BRAIN)


def attend(enc, x, project, offsets, segments, merge, adjust, gain, shift):
    count, width = x.shape
    blocks = count // ROWS
    heads = width // HEAD
    return pl.pallas_call(
        attend_kernel,
        grid_spec=pltpu.PrefetchScalarGridSpec(
            num_scalar_prefetch=1,
            grid=(blocks,),
            in_specs=[
                row_block(ROWS, width),
                whole(project.shape),
                whole(offsets.shape),
                pl.BlockSpec((1, ROWS), lambda i, *_: (0, i)),
                whole(merge.shape),
                whole(adjust.shape),
                whole(gain.shape),
                whole(shift.shape),
            ],
            out_specs=[
                row_block(ROWS, 3 * width),
                pl.BlockSpec((None, heads // 2, ROWS, 2 * ROWS), lambda i, *_: (i, 0, 0, 0)),
                row_block(ROWS, width),
                row_block(ROWS, width),
                row_block(ROWS, 1),
                row_block(ROWS, width),
            ],
        ),
        out_shape=[
            jax.ShapeDtypeStruct((count, 3 * width), BRAIN),
            jax.ShapeDtypeStruct((blocks, heads // 2, ROWS, 2 * ROWS), BRAIN),
            jax.ShapeDtypeStruct((count, width), BRAIN),
            jax.ShapeDtypeStruct((count, width), FLOAT_KIND),
            jax.ShapeDtypeStruct((count, 1), FLOAT_KIND),
            jax.ShapeDtypeStruct((count, width), BRAIN),
        ],
        cost_estimate=cost(1, 1),
        compiler_params=pltpu.CompilerParams(vmem_limit_bytes=17 * MEGA),
        name="attend",
    )(enc, x, project, offsets, segments, merge, adjust, gain, shift)


def summary_kernel(
    flag_ref,
    start_ref,
    target_ref,
    normal_ref,
    gain_one_ref,
    shift_one_ref,
    expand_ref,
    lift_ref,
    shrink_ref,
    settle_ref,
    gain_two_ref,
    shift_two_ref,
    out_ref,
    tile_ref,
    row_ref,
    low_ref,
    total_ref,
    copy_sem,
):
    slots, width = row_ref.shape
    step = pl.program_id(0)

    @pl.when(step == 0)
    def _():
        copies = [
            pltpu.make_async_copy(
                normal_ref.at[jnp.where(flag_ref[ENC] == 1, start_ref[slot], slot * QLEN) // TILE],
                tile_ref.at[slot],
                copy_sem.at[slot],
            )
            for slot in range(slots)
        ]
        for copy in copies:
            copy.start()
        for copy in copies:
            copy.wait()
        rows = tile_ref[:, 0, :] * wide(gain_one_ref) + wide(shift_one_ref)
        row_ref[...] = rows
        low_ref[...] = rows.astype(BRAIN)
        total_ref[...] = jnp.zeros_like(total_ref)

    activated, _ = gelu_and_slope(dot(low_ref[...], expand_ref[...]) + wide(lift_ref))
    total_ref[...] += dot(activated.astype(BRAIN), shrink_ref[...])

    @pl.when(step == pl.num_programs(0) - 1)
    def _():
        normal, _ = normalized(row_ref[...] + (total_ref[...] + wide(settle_ref)))
        out_ref[:, :width] = (normal * wide(gain_two_ref) + wide(shift_two_ref)).astype(BRAIN)
        lane = lax.broadcasted_iota(jnp.int32, (slots, LANES), 1)
        place = lax.broadcasted_iota(jnp.int32, (slots, LANES), 0)
        digits = jnp.zeros((slots, LANES), jnp.int32)
        for slot in range(slots):
            target = target_ref[slot]
            pair = jnp.where(lane == 0, target // LANES, jnp.where(lane == 1, target % LANES, 0))
            digits = jnp.where(place == slot, pair, digits)
        out_ref[:, width:] = digits.astype(FLOAT_KIND).astype(BRAIN)


def summarize(enc, starts, targets, normal, first, expand, lift, shrink, settle, second, tn=1536):
    count, width = normal.shape
    hidden = expand.shape[1]
    slots = starts.shape[0]
    row = whole((1, width))
    return pl.pallas_call(
        summary_kernel,
        grid_spec=pltpu.PrefetchScalarGridSpec(
            num_scalar_prefetch=3,
            grid=(hidden // tn,),
            in_specs=[
                pl.BlockSpec(memory_space=pl.ANY),
                row,
                row,
                pl.BlockSpec((width, tn), lambda i, *_: (0, i)),
                pl.BlockSpec((1, tn), lambda i, *_: (0, i)),
                pl.BlockSpec((tn, width), lambda i, *_: (i, 0)),
                row,
                row,
                row,
            ],
            out_specs=whole((slots, width + LANES)),
            scratch_shapes=[
                pltpu.VMEM((slots, TILE, width), FLOAT_KIND),
                pltpu.VMEM((slots, width), FLOAT_KIND),
                pltpu.VMEM((slots, width), BRAIN),
                pltpu.VMEM((slots, width), FLOAT_KIND),
                pltpu.SemaphoreType.DMA((slots,)),
            ],
        ),
        out_shape=jax.ShapeDtypeStruct((slots, width + LANES), BRAIN),
        cost_estimate=cost(1, 1),
        compiler_params=pltpu.CompilerParams(vmem_limit_bytes=15 * MEGA),
        name="summarize",
    )(
        enc,
        starts,
        targets,
        normal.reshape(count // TILE, TILE, width),
        *first,
        expand,
        lift,
        shrink,
        settle,
        *second,
    )


def widen_kernel(low_ref, expand_ref, lift_ref, *refs):
    active_ref, slope_ref = refs[-2:]

    @pl.loop(0, low_ref.shape[0] // ROWS)
    def _(block):
        rows = pl.ds(pl.multiple_of(block * ROWS, ROWS), ROWS)
        hidden = dot(low_ref[rows, :], expand_ref[...]) + wide(lift_ref)
        activated, slope = gelu_and_slope(hidden)
        active_ref[rows, :] = activated.astype(BRAIN)
        slope_ref[rows, :] = slope.astype(BRAIN)


def widen(part, parts, low, expand, lift, before, tn=768):
    count, width = low.shape
    hidden = expand.shape[1]
    steps = hidden // parts // tn
    column = lambda rows: pl.BlockSpec((rows, tn), lambda i: (0, part * steps + i))
    kept = [] if before is None else list(before)
    return pl.pallas_call(
        widen_kernel,
        grid=(steps,),
        in_specs=[whole(low.shape), column(width), column(1)]
        + [pl.BlockSpec(memory_space=pl.ANY)] * len(kept),
        out_specs=[column(count), column(count)],
        out_shape=[jax.ShapeDtypeStruct((count, hidden), BRAIN)] * 2,
        input_output_aliases={3 + k: k for k in range(len(kept))},
        cost_estimate=cost(1, 1),
        compiler_params=pltpu.CompilerParams(vmem_limit_bytes=10 * MEGA),
        name="widen",
    )(low, expand, lift, *kept)


def shrink_kernel(
    active_ref,
    shrink_ref,
    normal_ref,
    gain_one_ref,
    shift_one_ref,
    settle_ref,
    gain_two_ref,
    shift_two_ref,
    out_ref,
    inverse_ref,
    encoded_ref,
):
    normed = normal_ref[...] * wide(gain_one_ref) + wide(shift_one_ref)
    shrunk = dot(active_ref[...], shrink_ref[...]) + wide(settle_ref)
    normal, inverse = normalized(normed + shrunk)
    out_ref[...] = normal
    inverse_ref[...] = inverse
    encoded_ref[...] = (normal * wide(gain_two_ref) + wide(shift_two_ref)).astype(BRAIN)


def shrink_back_to_width(active, shrink, normal, first, settle, second, tm=256):
    count, hidden = active.shape
    width = shrink.shape[1]
    row = whole((1, width))
    return pl.pallas_call(
        shrink_kernel,
        grid=(count // tm,),
        in_specs=[row_block(tm, hidden), whole(shrink.shape), row_block(tm, width)] + [row] * 5,
        out_specs=[row_block(tm, width), row_block(tm, 1), row_block(tm, width)],
        out_shape=[
            jax.ShapeDtypeStruct((count, width), FLOAT_KIND),
            jax.ShapeDtypeStruct((count, 1), FLOAT_KIND),
            jax.ShapeDtypeStruct((count, width), BRAIN),
        ],
        cost_estimate=cost(1, 1),
        compiler_params=pltpu.CompilerParams(vmem_limit_bytes=8 * MEGA),
        name="shrink",
    )(active, shrink, normal, *first, settle, *second)


def contrast_kernel(
    flag_ref,
    start_ref,
    every_ref,
    column_ref,
    normal_ref,
    inverse_ref,
    cotangent_ref,
    gain_ref,
    two_ref,
    low_ref,
    sums_ref,
    summary_ref,
    rows_ref,
):
    width = normal_ref.shape[1]
    slots = start_ref.shape[0]
    devices = every_ref.shape[0]
    step = pl.program_id(0)
    sharpness = SHARPNESS_DIVISOR / math.sqrt(width)

    def flat(which, at, count):
        return every_ref[pl.ds(at, count), which].reshape(count * slots, width + LANES)

    def logits_of(questions, passages):
        return jnp.where(
            column_ref[...] >= 0, dot_rows(questions, passages) * sharpness, HIDDEN_SCORE
        )

    def targets_of(rows):
        digits = rows[:, width:].astype(FLOAT_KIND)
        return (digits[:, 0:1] * LANES + digits[:, 1:2]).astype(jnp.int32)

    @pl.when(step == 0)
    def _():
        sums_ref[...] = jnp.zeros_like(sums_ref)

        @pl.when(flag_ref[ENC] == 0)
        def _():
            own = every_ref[0, 0]
            passages = flat(1, 0, devices)[:, :width]
            logits = logits_of(own[:, :width], passages)
            top = jnp.max(logits, axis=1, keepdims=True)
            raised = jnp.exp(logits - top)
            probability = raised / jnp.sum(raised, axis=1, keepdims=True)
            hit = (column_ref[...] == targets_of(own)).astype(FLOAT_KIND)
            gradient = (LOSS_WEIGHT * (probability - hit)).astype(BRAIN)
            summary_ref[...] = dot(gradient, passages) * sharpness

        @pl.when(flag_ref[ENC] == 1)
        def _():
            passages = flat(0, 0, devices)[:, :width]
            block = 16

            def part(at):
                rows = flat(1, at, block)
                questions = rows[:, :width]
                logits = logits_of(questions, passages)
                top = jnp.max(logits, axis=1, keepdims=True)
                total = jnp.sum(jnp.exp(logits - top), axis=1, keepdims=True)
                probability = jnp.exp(logits[:, :LANES] - top) / total
                hit = (column_ref[:, :LANES] == targets_of(rows)).astype(FLOAT_KIND)
                gradient = (LOSS_WEIGHT * (probability - hit)).astype(BRAIN)
                return dot_columns(gradient, questions)[:slots] * sharpness

            if devices == block:
                summary_ref[...] = part(0)
            else:
                summary_ref[...] = jnp.zeros_like(summary_ref)

                @pl.loop(0, devices // block)
                def _(k):
                    summary_ref[...] += part(k * block)

    rows_ref[...] = wide(cotangent_ref)
    tiles = rows_ref.shape[0] // TILE
    first = lax.broadcasted_iota(jnp.int32, (TILE, 1), 0) == 0
    for slot in range(slots):
        start = jnp.where(flag_ref[ENC] == 1, start_ref[slot], slot * QLEN)
        local = start // TILE - step * tiles
        inside = (local >= 0) & (local < tiles)
        at = pl.multiple_of(jnp.clip(local, 0, tiles - 1) * TILE, TILE)
        rows_ref[pl.ds(at, TILE), :] += jnp.where(
            first & inside, summary_ref[slot : slot + 1, :], 0.0
        )
    gradient = rows_ref[...]
    normal = normal_ref[...]
    sums_ref[0:1] += row_sum(gradient * normal)
    sums_ref[1:2] += row_sum(gradient)
    two = norm_backward(gradient, normal, inverse_ref[...], wide(gain_ref))
    two_ref[...] = two
    low = two.astype(BRAIN)
    low_ref[...] = low
    sums_ref[2:3] += row_sum(low.astype(FLOAT_KIND))


def contrast(enc, starts, every, columns, normal, inverse, cotangent, gain, tm=256):
    count, width = normal.shape
    slots = starts.shape[0]
    return pl.pallas_call(
        contrast_kernel,
        grid_spec=pltpu.PrefetchScalarGridSpec(
            num_scalar_prefetch=2,
            grid=(count // tm,),
            in_specs=[
                whole(every.shape),
                whole(columns.shape),
                row_block(tm, width),
                row_block(tm, 1),
                row_block(tm, width),
                whole(gain.shape),
            ],
            out_specs=[row_block(tm, width), row_block(tm, width), whole((TILE, width))],
            scratch_shapes=[
                pltpu.VMEM((slots, width), FLOAT_KIND),
                pltpu.VMEM((tm, width), FLOAT_KIND),
            ],
        ),
        out_shape=[
            jax.ShapeDtypeStruct((count, width), FLOAT_KIND),
            jax.ShapeDtypeStruct((count, width), BRAIN),
            jax.ShapeDtypeStruct((TILE, width), FLOAT_KIND),
        ],
        cost_estimate=cost(1, 1),
        compiler_params=pltpu.CompilerParams(vmem_limit_bytes=8 * MEGA),
        name="contrast",
    )(enc, starts, every, columns, normal, inverse, cotangent, gain)


def contraction_kernel(flag_ref, low_ref, active_ref, *refs):
    turned_ref = refs[-1]
    step = pl.program_id(0)

    @pl.when(step == 0)
    def _():
        turned_ref[...] = low_ref[...].T

    value = dot(turned_ref[...], active_ref[...]).astype(BRAIN)
    for piece, out_ref in enumerate(refs[:-1]):

        @pl.when(step == piece)
        def _():
            out_ref[...] = value


def contraction_half(side, active, low, weight=1):
    count, hidden = active.shape
    width = low.shape[1]
    rows = width // 2
    tn = hidden // PIECES
    return pl.pallas_call(
        contraction_kernel,
        grid_spec=pltpu.PrefetchScalarGridSpec(
            num_scalar_prefetch=1,
            grid=(PIECES,),
            in_specs=[
                pl.BlockSpec((count, rows), lambda i, flag: (0, flag[0])),
                pl.BlockSpec((count, tn), lambda i, flag: (0, i)),
            ],
            out_specs=[whole((rows, tn))] * PIECES,
            scratch_shapes=[pltpu.VMEM((rows, count), BRAIN)],
        ),
        out_shape=[jax.ShapeDtypeStruct((rows, tn), BRAIN)] * PIECES,
        cost_estimate=cost(weight, 1),
        compiler_params=pltpu.CompilerParams(vmem_limit_bytes=8 * MEGA),
        name="contraction_half",
    )(side, low, active)


def feed_kernel(
    flag_ref,
    two_low_ref,
    shrink_ref,
    slope_ref,
    low_ref,
    expand_ref,
    two_ref,
    lift_ref,
    first_ref,
    *refs,
):
    pieces, turned_ref = refs[:-1], refs[-1]
    rows = turned_ref.shape[1]
    step = pl.program_id(0)

    @pl.when(step == 0)
    def _():
        first_ref[...] = two_ref[...]
        for side in range(2):

            @pl.when(flag_ref[SEND] == side)
            def _():
                turned_ref[0] = low_ref[:, side * rows : (side + 1) * rows].T
                turned_ref[1] = low_ref[:, (1 - side) * rows : (2 - side) * rows].T

    hidden = dot_rows(two_low_ref[...], shrink_ref[...]) * wide(slope_ref)
    low = hidden.astype(BRAIN)
    lift_ref[...] = row_sum(low.astype(FLOAT_KIND))
    first_ref[...] += dot_rows(low, expand_ref[...])
    for side in range(2):
        value = dot(turned_ref[side], low).astype(BRAIN)
        for piece in range(PIECES):

            @pl.when(step == piece)
            def _():
                pieces[side * PIECES + piece][...] = value


def feed_back(flags, two_low, shrink, slope, low, expand, two, weight=1):
    count, width = two.shape
    hidden = shrink.shape[0]
    rows = width // 2
    tn = hidden // PIECES
    column = lambda rows: pl.BlockSpec((rows, tn), lambda i, *_: (0, i))
    return pl.pallas_call(
        feed_kernel,
        grid_spec=pltpu.PrefetchScalarGridSpec(
            num_scalar_prefetch=1,
            grid=(PIECES,),
            in_specs=[
                whole((count, width)),
                row_block(tn, width),
                column(count),
                whole((count, width)),
                column(width),
                whole((count, width)),
            ],
            out_specs=[column(1), whole((count, width))] + [whole((rows, tn))] * 2 * PIECES,
            scratch_shapes=[pltpu.VMEM((2, rows, count), BRAIN)],
        ),
        out_shape=[
            jax.ShapeDtypeStruct((1, hidden), FLOAT_KIND),
            jax.ShapeDtypeStruct((count, width), FLOAT_KIND),
        ]
        + [jax.ShapeDtypeStruct((rows, tn), BRAIN)] * 2 * PIECES,
        cost_estimate=cost(weight, 1),
        compiler_params=pltpu.CompilerParams(vmem_limit_bytes=14 * MEGA),
        name="feed_back",
    )(flags, two_low, shrink, slope, low, expand, two)


def attend_back_kernel(
    first_ref,
    normal_ref,
    inverse_ref,
    gain_ref,
    merge_ref,
    packed_ref,
    weight_ref,
    one_ref,
    low_ref,
    packed_gradient_ref,
    sums_ref,
    packed_sums_ref,
    context_gradient_ref,
):
    width = normal_ref.shape[1]

    @pl.when(pl.program_id(0) == 0)
    def _():
        sums_ref[...] = jnp.zeros_like(sums_ref)
        packed_sums_ref[...] = jnp.zeros_like(packed_sums_ref)

    gradient = first_ref[...]
    normal = normal_ref[...]
    sums_ref[0:1] += row_sum(gradient * normal)
    sums_ref[1:2] += row_sum(gradient)
    one = norm_backward(gradient, normal, inverse_ref[...], wide(gain_ref))
    one_ref[...] = one
    low = one.astype(BRAIN)
    low_ref[...] = low
    sums_ref[2:3] += row_sum(low.astype(FLOAT_KIND))
    context_gradient_ref[...] = dot_rows(low, merge_ref[...]).astype(BRAIN)
    low_row = lax.broadcasted_iota(jnp.int32, (LANES, 1), 0) < HEAD
    scale = 1.0 / math.sqrt(HEAD)
    for pair in range(width // LANES):
        at = LANES * pair
        queries = both_heads(packed_ref[:, at : at + LANES] * scale)
        keys = packed_ref[:, width + at : width + at + LANES] * scale
        values = packed_ref[:, 2 * width + at : 2 * width + at + LANES]
        outer = both_heads(context_gradient_ref[:, at : at + LANES])
        weights = weight_ref[pair]
        probability = weights.astype(FLOAT_KIND)
        inner = dot_rows(values, outer)
        scores = (probability * (inner - row_sum(probability * inner))).astype(BRAIN)
        turned = dot(keys.T, scores)
        found = (
            jnp.where(low_row, turned[:, :ROWS], turned[:, ROWS:]).T,
            dot(scores, queries),
            dot(weights, outer),
        )
        for part in range(3):
            columns = slice(part * width + at, part * width + at + LANES)
            packed_gradient_ref[:, columns] = found[part].astype(BRAIN)
    packed_sums_ref[...] += row_sum(wide(packed_gradient_ref))


def attend_back(first, normal, inverse, gain, merge, packed, weights, weight=1):
    count, width = normal.shape
    heads = width // HEAD
    return pl.pallas_call(
        attend_back_kernel,
        grid=(count // ROWS,),
        in_specs=[
            row_block(ROWS, width),
            row_block(ROWS, width),
            row_block(ROWS, 1),
            whole(gain.shape),
            whole(merge.shape),
            row_block(ROWS, 3 * width),
            pl.BlockSpec((None, heads // 2, ROWS, 2 * ROWS), lambda i: (i, 0, 0, 0)),
        ],
        out_specs=[
            row_block(ROWS, width),
            row_block(ROWS, width),
            row_block(ROWS, 3 * width),
            whole((TILE, width)),
            whole((1, 3 * width)),
        ],
        out_shape=[
            jax.ShapeDtypeStruct((count, width), FLOAT_KIND),
            jax.ShapeDtypeStruct((count, width), BRAIN),
            jax.ShapeDtypeStruct((count, 3 * width), BRAIN),
            jax.ShapeDtypeStruct((TILE, width), FLOAT_KIND),
            jax.ShapeDtypeStruct((1, 3 * width), FLOAT_KIND),
        ],
        scratch_shapes=[pltpu.VMEM((ROWS, width), BRAIN)],
        cost_estimate=cost(weight, 1),
        compiler_params=pltpu.CompilerParams(vmem_limit_bytes=11 * MEGA),
        name="attend_back",
    )(first, normal, inverse, gain, merge, packed, weights)


def merge_project_kernel(flag_ref, context_ref, one_ref, x_ref, packed_ref, *refs):
    pieces, turned_ref = refs[:-1], refs[-1]
    step = pl.program_id(0)

    @pl.when(step == 0)
    def _():
        turned_ref[...] = context_ref[...].T
        pieces[0][...] = dot(turned_ref[...], one_ref[...]).astype(BRAIN)
        turned_ref[...] = x_ref[...].T

    @pl.when(step > 0)
    def _():
        value = dot(turned_ref[...], packed_ref[...]).astype(BRAIN)
        for piece in range(1, PIECES):

            @pl.when(step == piece)
            def _():
                pieces[piece][...] = value


def merge_project_half(side, context, one, x, packed, weight=1):
    count, width = x.shape
    rows = width // 2
    return pl.pallas_call(
        merge_project_kernel,
        grid_spec=pltpu.PrefetchScalarGridSpec(
            num_scalar_prefetch=1,
            grid=(PIECES,),
            in_specs=[
                pl.BlockSpec((count, rows), lambda i, flag: (0, flag[0])),
                whole((count, width)),
                pl.BlockSpec((count, rows), lambda i, flag: (0, flag[0])),
                pl.BlockSpec((count, width), lambda i, flag: (0, jnp.maximum(i - 1, 0))),
            ],
            out_specs=[whole((rows, width))] * PIECES,
            scratch_shapes=[pltpu.VMEM((rows, count), BRAIN)],
        ),
        out_shape=[jax.ShapeDtypeStruct((rows, width), BRAIN)] * PIECES,
        cost_estimate=cost(weight, 1),
        compiler_params=pltpu.CompilerParams(vmem_limit_bytes=10 * MEGA),
        name="merge_project_half",
    )(side, context, one, x, packed)


def fold_kernel(flag_ref, *refs, count, side):
    keep, other, outs = refs[:count], refs[count : 2 * count], refs[2 * count :]
    rows = outs[0].shape[0]
    columns = outs[0].shape[1] // count
    for out_ref, half in zip(outs, (1 - flag_ref[side], flag_ref[side])):

        @pl.loop(0, rows // PACKED)
        def _(block):
            to = pl.ds(pl.multiple_of(block * PACKED, PACKED), PACKED)
            at = pl.ds(pl.multiple_of(half * rows + block * PACKED, PACKED), PACKED)
            for piece in range(count):
                total = wide(keep[piece].at[at]) + wide(other[piece].at[at])
                out_ref[to, piece * columns : (piece + 1) * columns] = total.astype(BRAIN)


def folded(flags, place, keep, other, weight):
    rows, columns = keep[0].shape
    count = len(keep)
    if rows % (2 * PACKED):
        (mine,), (theirs,) = keep, other
        bit = flags[place]
        return part_sum(mine, theirs, 1 - bit), part_sum(mine, theirs, bit)
    shape = jax.ShapeDtypeStruct((rows // 2, count * columns), BRAIN)
    return pl.pallas_call(
        functools.partial(fold_kernel, count=count, side=place),
        grid_spec=pltpu.PrefetchScalarGridSpec(
            num_scalar_prefetch=1,
            grid=(1,),
            in_specs=[whole((rows, columns))] * 2 * count,
            out_specs=[whole(shape.shape)] * 2,
        ),
        out_shape=[shape, shape],
        cost_estimate=cost(weight, 1),
        compiler_params=pltpu.CompilerParams(vmem_limit_bytes=5 * MEGA),
        name="fold",
    )(flags, *keep, *other)


def add_kernel(mine_ref, other_ref, out_ref):
    out_ref[...] = (wide(mine_ref) + wide(other_ref)).astype(out_ref.dtype)


def added(mine, other, weight=1):
    return pl.pallas_call(
        add_kernel,
        out_shape=jax.ShapeDtypeStruct(mine.shape, mine.dtype),
        cost_estimate=cost(weight, 1),
        compiler_params=pltpu.CompilerParams(vmem_limit_bytes=2 * MEGA),
        name="add",
    )(mine, other)


def join_kernel(flag_ref, mine_ref, other_ref, out_ref, *, side):
    rows = mine_ref.shape[0]
    out_ref[pl.ds(pl.multiple_of(flag_ref[side] * rows, rows), rows), :] = mine_ref[...]
    out_ref[pl.ds(pl.multiple_of((1 - flag_ref[side]) * rows, rows), rows), :] = other_ref[...]


def joined(flags, place, mine, other, weight):
    rows, columns = mine.shape
    if rows % PACKED:
        return joined_by_bit(mine, other, flags[place])
    return pl.pallas_call(
        functools.partial(join_kernel, side=place),
        grid_spec=pltpu.PrefetchScalarGridSpec(
            num_scalar_prefetch=1,
            grid=(1,),
            in_specs=[whole(mine.shape)] * 2,
            out_specs=whole((2 * rows, columns)),
        ),
        out_shape=jax.ShapeDtypeStruct((2 * rows, columns), BRAIN),
        cost_estimate=cost(weight, 1),
        compiler_params=pltpu.CompilerParams(vmem_limit_bytes=4 * MEGA),
        name="join",
    )(flags, mine, other)


def tokens_kernel(one_ref, packed_ref, project_ref, out_ref):
    out_ref[...] = one_ref[...] + dot_rows(packed_ref[...], project_ref[...])


def tokens_back(one, packed, project, tm=256, weight=1):
    count, width = one.shape
    return pl.pallas_call(
        tokens_kernel,
        grid=(count // tm,),
        in_specs=[row_block(tm, width), row_block(tm, 3 * width), whole(project.shape)],
        out_specs=row_block(tm, width),
        out_shape=jax.ShapeDtypeStruct((count, width), FLOAT_KIND),
        cost_estimate=cost(weight, 1),
        compiler_params=pltpu.CompilerParams(vmem_limit_bytes=13 * MEGA),
        name="tokens_back",
    )(one, packed, project)


def pack_kernel(packed_ref, attend_ref, lift_ref, output_ref, out_ref):
    width = attend_ref.shape[1]
    out_ref[...] = jnp.zeros_like(out_ref)
    out_ref[0:1] = packed_ref[:, :width]
    out_ref[1:2] = packed_ref[:, 2 * width :]
    out_ref[2:5] = attend_ref[0:3]
    for part in range(4):
        out_ref[5 + part : 6 + part] = lift_ref[:, part * width : (part + 1) * width]
    out_ref[9:12] = output_ref[0:3]


def pack_vectors(packed_sums, attend_sums, lift_sums, output_sums):
    width = attend_sums.shape[1]
    return pl.pallas_call(
        pack_kernel,
        out_shape=jax.ShapeDtypeStruct((16, width), FLOAT_KIND),
        cost_estimate=cost(1, 1),
        compiler_params=pltpu.CompilerParams(vmem_limit_bytes=2 * MEGA),
        name="pack_vectors",
    )(packed_sums, attend_sums, lift_sums, output_sums)


def unpack_kernel(mine_ref, other_ref, offset_ref, adjust_ref, scale_ref, center_ref, lift_ref, settle_ref, rescale_ref, recenter_ref):
    width = mine_ref.shape[1]
    total = mine_ref[...] + other_ref[...]
    offset_ref[:, :width] = total[0:1]
    offset_ref[:, width:] = total[1:2]
    scale_ref[...] = total[2:3]
    center_ref[...] = total[3:4]
    adjust_ref[...] = total[4:5]
    for part in range(4):
        lift_ref[:, part * width : (part + 1) * width] = total[5 + part : 6 + part]
    rescale_ref[...] = total[9:10]
    recenter_ref[...] = total[10:11]
    settle_ref[...] = total[11:12]


def unpack_vectors(mine, other):
    width = mine.shape[1]
    shapes = [2, 1, 1, 1, 4, 1, 1, 1]
    return pl.pallas_call(
        unpack_kernel,
        out_shape=[jax.ShapeDtypeStruct((1, k * width), FLOAT_KIND) for k in shapes],
        cost_estimate=cost(1, 1),
        compiler_params=pltpu.CompilerParams(vmem_limit_bytes=2 * MEGA),
        name="unpack_vectors",
    )(mine, other)


def place_kernel(flag_ref, value_ref, *refs, kept):
    at = 0
    for out_ref in refs[kept:]:
        columns = out_ref.shape[1]
        out_ref[...] = value_ref[:, at : at + columns].astype(FLOAT_KIND)
        at += columns


def place_half(flags, side, value, columns, before, tm=192):
    rows = value.shape[0]
    steps = rows // tm
    kept = [] if before is None else list(before)
    return pl.pallas_call(
        functools.partial(place_kernel, kept=len(kept)),
        grid_spec=pltpu.PrefetchScalarGridSpec(
            num_scalar_prefetch=1,
            grid=(steps,),
            in_specs=[row_block(tm, value.shape[1])]
            + [pl.BlockSpec(memory_space=pl.ANY)] * len(kept),
            out_specs=[
                pl.BlockSpec((tm, size), lambda i, flag: (flag[side] * steps + i, 0))
                for size in columns
            ],
        ),
        out_shape=[jax.ShapeDtypeStruct((2 * rows, size), FLOAT_KIND) for size in columns],
        input_output_aliases={2 + k: k for k in range(len(kept))},
        cost_estimate=cost(1, 1),
        compiler_params=pltpu.CompilerParams(vmem_limit_bytes=10 * MEGA),
        name="place_half",
    )(flags, value, *kept)


def place_turned_kernel(flag_ref, value_ref, *refs):
    refs[-1][...] = value_ref[...].astype(FLOAT_KIND).T


def place_turned_half(flags, side, value, before, tm=1536):
    rows, columns = value.shape
    kept = [] if before is None else list(before)
    return pl.pallas_call(
        place_turned_kernel,
        grid_spec=pltpu.PrefetchScalarGridSpec(
            num_scalar_prefetch=1,
            grid=(columns // tm,),
            in_specs=[pl.BlockSpec((rows, tm), lambda i, flag: (0, i))]
            + [pl.BlockSpec(memory_space=pl.ANY)] * len(kept),
            out_specs=[pl.BlockSpec((tm, rows), lambda i, flag: (i, flag[side]))],
        ),
        out_shape=[jax.ShapeDtypeStruct((columns, 2 * rows), FLOAT_KIND)],
        input_output_aliases={2 + k: k for k in range(len(kept))},
        cost_estimate=cost(1, 1),
        compiler_params=pltpu.CompilerParams(vmem_limit_bytes=14 * MEGA),
        name="place_turned_half",
    )(flags, value, *kept)


def swapped(value, axis, apart):
    mask = 2**apart
    pairs = [(source, source ^ mask) for source in range(lax.axis_size(axis))]
    return lax.ppermute(value, axis, pairs)


def swapped_by_core(value, stage):
    count = lax.axis_size("batch")
    pairs = [(source, source ^ (1 << stage[source & 1])) for source in range(count)]
    return lax.ppermute(value, "batch", pairs)


def bit_count(axis):
    return lax.axis_size(axis).bit_length() - 1


def to_low(values):
    return values.astype(BRAIN)


def part_sum(mine, other, bit):
    half = mine.shape[0] // 2
    left = lax.dynamic_slice_in_dim(mine, bit * half, half, 0).astype(FLOAT_KIND)
    right = lax.dynamic_slice_in_dim(other, bit * half, half, 0).astype(FLOAT_KIND)
    return to_low(left + right)


def joined_by_bit(mine, other, bit):
    low_part = jnp.where(bit == 0, mine, other)
    high_part = jnp.where(bit == 0, other, mine)
    return jnp.concatenate([low_part, high_part], axis=0)


class Sequence:
    def __init__(self):
        self.last = None

    def run(self, step, *inputs):
        if self.last is not None:
            *inputs, _ = lax.optimization_barrier((*inputs, self.last))
        result = step(*inputs)
        self.last = jax.tree.leaves(result)[0]
        return result


class Reduction:
    def __init__(self, sequence, flags, stages, at, put):
        self.run = sequence.run
        self.flags = flags
        self.stages = stages
        self.at = at
        self.put = put
        count = len(stages)
        self.steps = [functools.partial(self.scatter, k) for k in range(count)]
        self.steps.append(self.finish)
        self.steps += [functools.partial(self.gather, k) for k in reversed(range(count))]
        self.steps.append(self.place)

    def advance(self, weight=1):
        self.steps.pop(0)(weight)

    def begin(self, send, keep):
        self.keep = list(keep)
        self.other = [swapped(piece, "batch", 0) for piece in send]

    def scatter(self, stage, weight):
        count = len(self.keep)
        send, keep = self.run(
            lambda *v: folded(self.flags, self.at + stage, v[:count], v[count:], weight),
            *self.keep,
            *self.other,
        )
        self.keep = [keep]
        self.other = [swapped_by_core(send, self.stages[stage])]

    def finish(self, weight):
        self.value = self.run(lambda a, b: added(a, b, weight), *self.keep, *self.other)
        self.other = swapped_by_core(self.value, self.stages[-1])

    def gather(self, stage, weight):
        self.value = self.run(
            lambda v, o: joined(self.flags, self.at + stage, v, o, weight), self.value, self.other
        )
        if stage > 0:
            self.other = swapped_by_core(self.value, self.stages[stage - 1])
            return
        self.other = swapped(self.value, "batch", 0)
        self.placed = self.run(lambda v: self.put(self.flags, KEEP, v, None), self.value)

    def place(self, weight):
        self.total = self.run(
            lambda o, *p: self.put(self.flags, SEND, o, p), self.other, *self.placed
        )


def shards(
    tokens,
    cotangent,
    projection,
    offsets,
    merger,
    adjust,
    scaling,
    centering,
    expansion,
    lifting,
    contraction,
    settling,
    rescale,
    recenter,
    segments,
    passage_starts,
    passage_counts,
    positives,
):
    index = lax.axis_index("batch").astype(jnp.int32)
    slots = passage_starts.shape[0]
    bits = bit_count("batch")
    plain = [(apart, apart) for apart in range(1, bits)]
    mixed = [(apart, other) for (apart, _), (other, _) in zip(plain, plain[1:] + plain[:1])]
    kinds = (plain, mixed, [(odd, even) for even, odd in mixed])
    flags = jnp.stack(
        [lax.axis_index("enc").astype(jnp.int32), index & 1, 1 - (index & 1)]
        + [
            (index >> jnp.where(index & 1 == 0, even, odd)) & 1
            for stages in kinds
            for even, odd in stages
        ]
    )
    order = list(reversed(range(bits)))
    place = jnp.arange(lax.axis_size("batch"), dtype=jnp.int32)
    away = sum(((place >> k) & 1) << apart for k, apart in enumerate(order))
    device = (index ^ away)[:, None]
    slot = jnp.arange(slots, dtype=jnp.int32)[None, :]
    held = jnp.sum(jnp.where(device == place[None, :], passage_counts[None, :], 0), axis=1)
    columns = jnp.where(slot < held[:, None], device * slots + slot, -1).reshape(1, -1)
    keep_side = (index & 1)[None]
    flags, keep_side, send_side, columns, tokens = lax.optimization_barrier(
        (flags, keep_side, 1 - keep_side, columns, tokens)
    )
    width = tokens.shape[2]
    x, project, merge, expand, shrink, outer = (
        in_hbm(tokens[0]),
        in_hbm(projection[0]),
        in_hbm(merger[0]),
        expansion[0],
        in_hbm(contraction[0]),
        in_hbm(cotangent[0]),
    )
    first = (in_hbm(scaling), in_hbm(centering))
    second = (in_hbm(rescale), in_hbm(recenter))
    adjust, lifting, settling, offsets = (
        in_hbm(v) for v in (adjust, lifting, settling, offsets)
    )

    sequence = Sequence()
    run = sequence.run
    packed, weights, context, normal_one, inverse_one, low = attend(
        flags, x, project, offsets, in_hbm(segments[None]), merge, adjust, *first
    )
    parcel = summarize(
        flags,
        passage_starts,
        positives,
        normal_one,
        first,
        expand,
        lifting,
        shrink,
        settling,
        second,
    )
    sequence.last = parcel
    parts = 4
    every = parcel[None]
    other = swapped(parcel, "enc", 0)[None]
    wide_pair = run(lambda v: widen(0, parts, v, expand, lifting, None), low)
    every = run(lambda a, b: jnp.stack([a, b], axis=1), every, other)
    for part, apart in enumerate(order, 1):
        other = swapped(every, "batch", apart)
        if part < parts:
            wide_pair = run(
                lambda v, *p: widen(part, parts, v, expand, lifting, p), low, *wide_pair
            )
        elif part == parts:
            active, slope = wide_pair
            normal_two, inverse_two, encoded = run(
                lambda a, n: shrink_back_to_width(a, contraction[0], n, first, settling, second),
                active,
                normal_one,
            )
        every = run(lambda a, b: jnp.concatenate([a, b], axis=0), every, other)
    two, two_low, output_sums = run(
        lambda *v: contrast(flags, passage_starts, *v, outer, second[0]),
        every,
        columns,
        normal_two,
        inverse_two,
    )

    puts = (
        place_turned_half,
        lambda f, s, v, p: place_half(f, s, v, (expansion.shape[2],), p),
        lambda f, s, v, p: place_half(f, s, v, (width, projection.shape[2]), p),
    )
    shrink_sum, expand_sum, project_sum = (
        Reduction(sequence, flags, kinds[kind], STAGES + kind * len(plain), put)
        for kind, put in zip(LINKS, puts)
    )
    product = lambda side: run(
        lambda c, o, p: merge_project_half(side, c, o, x, p, weight),
        context,
        one_low,
        packed_gradient,
    )
    vectors = []
    apart = 0
    for step in PLAN:
        weight = LEVELS[int(step[1:] or 0)]
        kind = step[0]
        if kind == "C":
            send = run(lambda a, t: contraction_half(send_side, a, t, weight), active, two_low)
            keep = run(lambda a, t: contraction_half(keep_side, a, t, weight), active, two_low)
            shrink_sum.begin(send, keep)
        elif kind == "F":
            lift_sums, gradient_first, *both = run(
                lambda t, s, g: feed_back(flags, t, shrink, s, low, expand, g, weight),
                two_low,
                slope,
                two,
            )
            expand_sum.begin(both[:PIECES], both[PIECES:])
        elif kind == "A":
            one, one_low, packed_gradient, attend_sums, packed_sums = run(
                lambda g, n, i, p, w: attend_back(g, n, i, first[0], merge, p, w, weight),
                gradient_first,
                normal_one,
                inverse_one,
                packed,
                weights,
            )
        elif kind == "S":
            send = product(send_side)
        elif kind == "K":
            keep = product(keep_side)
            project_sum.begin(send, keep)
        elif kind == "T":
            tokens_gradient = run(lambda o, p: tokens_back(o, p, project, weight=weight), one, packed_gradient)
        elif kind == "P":
            vectors = [run(pack_vectors, packed_sums, attend_sums, lift_sums, output_sums)]
            vectors.append(swapped(vectors[0], "batch", apart))
        elif kind == "v":
            apart += 1
            vectors = [run(lambda a, b, w=weight: added(a, b, w), *vectors)]
            vectors.append(swapped(vectors[0], "batch", apart))
        else:
            {"c": shrink_sum, "e": expand_sum, "m": project_sum}[kind].advance(weight)
    while apart < bits - 1:
        apart += 1
        vectors = [run(added, *vectors)]
        vectors.append(swapped(vectors[0], "batch", apart))
    vector_totals = run(unpack_vectors, *vectors)
    for reduction in (shrink_sum, expand_sum, project_sum):
        while reduction.steps:
            reduction.advance()
    (total_contraction,) = shrink_sum.total
    (total_expansion,) = expand_sum.total
    total_merger, total_projection = project_sum.total
    (
        total_offsets,
        total_adjust,
        total_scaling,
        total_centering,
        total_lifting,
        total_settling,
        total_rescale,
        total_recenter,
    ) = vector_totals
    return (
        encoded[None],
        tokens_gradient[None],
        total_projection[None],
        total_offsets,
        total_merger[None],
        total_adjust,
        total_scaling,
        total_centering,
        total_expansion[None],
        total_lifting,
        total_contraction[None],
        total_settling,
        total_rescale,
        total_recenter,
    )


def solution(mesh):
    matrix = P("enc", None, None)
    vector = P("enc", None)
    rows = P("enc", "batch", None)
    return jax.shard_map(
        shards,
        mesh=mesh,
        in_specs=(
            rows,
            rows,
            matrix,
            vector,
            matrix,
            vector,
            vector,
            vector,
            matrix,
            vector,
            matrix,
            vector,
            vector,
            vector,
            P("batch"),
            P("batch"),
            P(),
            P("batch"),
        ),
        out_specs=(
            rows,
            rows,
            matrix,
            vector,
            matrix,
            vector,
            vector,
            vector,
            matrix,
            vector,
            matrix,
            vector,
            vector,
            vector,
        ),
        check_vma=False,
    )
```
